32 devices in a mesh: rows: 8 (over y, x, core), cols: 4 (over z).
Axes of the slice: x: 2, y: 2, z: 4, core: 2. Of those that a mesh axis runs over, the one named last changes fastest.
Arguments:
- loading: float32 [8, 512, 512], P(None, 'rows', 'cols')
- viscosity: float32 [8, 512, 512], P(None, 'rows', 'cols'), may hold values from 0.01 to 100
- aggregate: int32 [32, 32], P('rows', 'cols'), may hold values from 0 to 511
- coarse_inverse: float32 [512, 512], P(None, 'rows'), as said below
Outputs:
- solution: float32 [8, 512, 512], P(None, 'rows', 'cols')
- residual: float32 [8, 512, 512], P(None, 'rows', 'cols')
The draws below stay inside these ranges and needn't reach their ends.
Inputs may be any that keep to these rules, and one draw needn't show every extreme that they name: `coarse_inverse`: symmetric; each diagonal entry exceeds the sum of the magnitudes of the other entries of its row.
All inputs are finite; a program needn't handle non-finite values.
Results may differ from the reference program's by a relative error of at most 0.0012.
Values sent between devices are 32-bit elements; how exact they have to be, the bound alone decides.
No kernel may reach another device: no remote copies, remote signals or barrier semaphores. Data moves between devices by JAX's collectives and lax.ppermute only.
A program may use at most 64 MiB of HBM per device.

```python
import math
import jax
import jax.numpy as jnp
from jax import lax

LAYERS = 8
BLOCK = 16
COARSE = 512
ITERS = 4
NX = 512
NY = 512
BX = 32
BY = 32


def draw_loading(key, part):
    first, second, third, fourth = jax.random.split(jax.random.fold_in(key, 37), 4)
    freq_x = jax.random.randint(second, (3,), 1, 5).astype(jnp.float32)
    freq_y = jax.random.randint(third, (3,), 1, 5).astype(jnp.float32)
    phases = jax.random.uniform(fourth, (3,), jnp.float32, 0.0, 6.2831853)
    place_x = jnp.arange(NX, dtype=jnp.float32)[:, None] / NX
    place_y = jnp.arange(NY, dtype=jnp.float32)[None, :] / NY
    smooth = jnp.zeros((NX, NY), jnp.float32)
    for index in range(3):
        smooth = smooth + 0.6 * jnp.sin(6.2831853 * (freq_x[index] * place_x + freq_y[index] * place_y) + phases[index])
    rough = jnp.clip(jax.random.normal(first, (LAYERS, NX, NY), jnp.float32), -6.0, 6.0)
    return rough + smooth[None, :, :]


def draw_coarse_inverse(key, part):
    first, second = jax.random.split(jax.random.fold_in(key, 11))
    bound = 1.5 / COARSE
    rough = jax.random.uniform(first, (COARSE, COARSE), jnp.float32, -bound, bound)
    symmetric = 0.5 * (rough + rough.T)
    leading = jax.random.uniform(second, (COARSE,), jnp.float32, 2.0, 3.0)
    scale = 1.0 / (2.0 * (LAYERS * NX * NY / COARSE))
    return (symmetric + jnp.diag(leading)) * scale


def draw_aggregate(key, part):
    first, second = jax.random.split(jax.random.fold_in(key, 23))
    patches_y = 8
    patches_x = COARSE // patches_y
    jitter_x = jax.random.randint(first, (BX, BY), -1, 2)
    jitter_y = jax.random.randint(second, (BX, BY), -1, 2)
    index_x = jnp.arange(BX, dtype=jnp.int32)[:, None] + jitter_x
    index_y = jnp.arange(BY, dtype=jnp.int32)[None, :] + jitter_y
    index_x = jnp.clip(index_x, 0, BX - 1)
    index_y = jnp.clip(index_y, 0, BY - 1)
    patch_x = index_x * patches_x // BX
    patch_y = index_y * patches_y // BY
    result = (patch_x * patches_y + patch_y).astype(jnp.int32)
    result = result.at[0, 0].set(0)
    result = result.at[BX - 1, BY - 1].set(COARSE - 1)
    return result


def steps_of(stream_key, dims, pieces, smallest, largest):
    factor_of, own = 1.0, jax.random.fold_in(stream_key, 6)
    for axis_at, parts in pieces:
        steps = jnp.exp(jax.random.uniform(jax.random.fold_in(own, axis_at), (parts,), jnp.float32, smallest / len(pieces), largest / len(pieces)))
        factor_of = factor_of * jnp.repeat(steps, dims[axis_at] // parts).reshape([-1 if axis == axis_at else 1 for axis in range(len(dims))])
    return factor_of


def setup_inputs(seed: int = 0) -> dict:
    streams_of = jax.random.split(jax.random.key(seed), 5)
    loading = draw_loading(jax.random.fold_in(streams_of[4], 71), 0)
    viscosity = jnp.clip(jnp.exp(math.log(100.0) - 9.2103404 * jax.random.uniform(streams_of[1], (LAYERS, NX, NY), jnp.float32) ** steps_of(streams_of[1], (LAYERS, NX, NY), ((1, 8), (2, 4)), -0.2, 0.2)), 0.01, 100.0)
    aggregate = draw_aggregate(jax.random.fold_in(streams_of[4], 71), 0)
    coarse_inverse = draw_coarse_inverse(jax.random.fold_in(streams_of[4], 71), 0)
    return dict(loading=loading, viscosity=viscosity, aggregate=aggregate, coarse_inverse=coarse_inverse)


MASS_TERM = 1.0
PRECISE = lax.Precision.HIGHEST


def neighbour_views(wider):
    return [wider[:-2, 1:-1, 1:-1], wider[2:, 1:-1, 1:-1], wider[1:-1, :-2, 1:-1],
            wider[1:-1, 2:, 1:-1], wider[1:-1, 1:-1, :-2], wider[1:-1, 1:-1, 2:]]


def operate(field, weights):
    sides = neighbour_views(jnp.pad(field, 1))
    total = MASS_TERM * field
    for weight, side in zip(weights, sides):
        total = total + weight * (field - side)
    return total


def restrict(field, aggregate):
    blocks_x, blocks_y = aggregate.shape
    blocks = field.reshape(LAYERS, blocks_x, BLOCK, blocks_y, BLOCK).sum(axis=(0, 2, 4))
    return jax.ops.segment_sum(blocks.reshape(-1), aggregate.reshape(-1), num_segments=COARSE)


def prolong(values, aggregate):
    blocks_x, blocks_y = aggregate.shape
    per_block = jnp.take(values, aggregate.reshape(-1)).reshape(blocks_x, blocks_y)
    spread = jnp.broadcast_to(per_block[None, :, None, :, None], (LAYERS, blocks_x, BLOCK, blocks_y, BLOCK))
    return spread.reshape(LAYERS, blocks_x * BLOCK, blocks_y * BLOCK)


def reference(loading, viscosity, aggregate, coarse_inverse):
    sides = neighbour_views(jnp.pad(viscosity, 1))
    weights = [0.5 * (viscosity + side) for side in sides]
    diagonal = MASS_TERM + weights[0]
    for weight in weights[1:]:
        diagonal = diagonal + weight
    inverse = 1.0 / diagonal

    def precondition(resid):
        coarse = restrict(resid, aggregate)
        lifted = jnp.dot(coarse_inverse, coarse, precision=PRECISE)
        result = inverse * resid + prolong(lifted, aggregate)
        inner = jnp.sum(resid * inverse * resid) + jnp.dot(coarse, lifted, precision=PRECISE)
        return result, inner

    solution = jnp.zeros_like(loading)
    residual = loading
    direction, inner_now = precondition(residual)
    for iteration in range(ITERS):
        image = operate(direction, weights)
        alpha = inner_now / jnp.sum(direction * image)
        solution = solution + alpha * direction
        residual = residual - alpha * image
        if iteration + 1 < ITERS:
            precond, inner_next = precondition(residual)
            direction = precond + (inner_next / inner_now) * direction
            inner_now = inner_next
    return solution, residual
```

```python
import jax
import jax.numpy as jnp
from jax import lax
from jax.sharding import PartitionSpec as P

BLOCK = 16
COARSE = 512
ITERS = 4
HALO = 8

MASS_TERM = 1.0
PRECISE = lax.Precision.HIGHEST
BOTH = ("rows", "cols")


def from_sides(block, axis, dim, width):
    count = lax.axis_size(axis)
    forward = [(i, i + 1) for i in range(count - 1)]
    backward = [(target, source) for source, target in forward]
    size = block.shape[dim]
    low = lax.ppermute(lax.slice_in_dim(block, size - width, size, axis=dim), axis, forward)
    high = lax.ppermute(lax.slice_in_dim(block, 0, width, axis=dim), axis, backward)
    return low, high


def widened(block, width_x, width_y):
    low, high = from_sides(block, "rows", block.ndim - 2, width_x)
    block = jnp.concatenate([low, block, high], axis=-2)
    turned = jnp.swapaxes(block, -1, -2)
    low, high = from_sides(turned, "cols", turned.ndim - 2, width_y)
    low, high = jnp.swapaxes(low, -1, -2), jnp.swapaxes(high, -1, -2)
    return jnp.concatenate([low, block, high], axis=-1)


def all_sum(values):
    count = lax.axis_size("rows") * lax.axis_size("cols")
    if count > 64:
        return lax.psum(lax.psum(values, "cols"), "rows")
    spread = jnp.broadcast_to(values[None], (count,) + values.shape)
    return lax.all_to_all(spread, BOTH, 0, 0).sum(axis=0)


def shifted(field, axis, step):
    return jnp.roll(field, step, axis=axis)


def local(loading, viscosity, aggregate, coarse_inverse):
    layers, cells_x, cells_y = loading.shape
    blocks_x, blocks_y = aggregate.shape
    ids = jnp.arange(COARSE, dtype=jnp.int32)
    whole_matrix = lax.all_gather(coarse_inverse, "rows", axis=1, tiled=True)
    fields = widened(jnp.stack([loading, viscosity]), HALO, HALO)
    wide_aggregate = widened(aggregate + 1, 1, 1) - 1
    table = (aggregate.reshape(-1)[:, None] == ids[None, :]).astype(jnp.float32)
    wide_table = (wide_aggregate.reshape(-1)[:, None] == ids[None, :]).astype(jnp.float32)

    residual, visc = fields[0], fields[1]
    inside = visc > 0.0
    pads = ((1, 1), (0, 0), (0, 0))
    padded = jnp.pad(visc, pads)
    weights = [
        0.5 * (visc + padded[:-2]),
        0.5 * (visc + padded[2:]),
        0.5 * (visc + shifted(visc, 1, 1)),
        0.5 * (visc + shifted(visc, 1, -1)),
        0.5 * (visc + shifted(visc, 2, 1)),
        0.5 * (visc + shifted(visc, 2, -1)),
    ]
    diagonal = MASS_TERM + sum(weights)
    inverse = jnp.where(inside, 1.0 / diagonal, 0.0)

    def operate(field):
        layered = jnp.pad(field, pads)
        sides = [
            layered[:-2],
            layered[2:],
            shifted(field, 1, 1),
            shifted(field, 1, -1),
            shifted(field, 2, 1),
            shifted(field, 2, -1),
        ]
        total = MASS_TERM * field
        for weight, side in zip(weights, sides):
            total = total + weight * (field - side)
        return total

    def inner_part(field):
        return field[:, HALO:-HALO, HALO:-HALO]

    def restrict(field):
        blocks = field.reshape(layers, blocks_x, BLOCK, blocks_y, BLOCK).sum(axis=(0, 2, 4))
        return jnp.dot(blocks.reshape(-1), table, precision=PRECISE).reshape(4, COARSE // 4)

    def prolong(values):
        per_block = jnp.dot(wide_table, values.reshape(-1), precision=PRECISE)
        per_block = per_block.reshape(blocks_x + 2, blocks_y + 2)
        spread = jnp.repeat(jnp.repeat(per_block, BLOCK, axis=0), BLOCK, axis=1)
        cut = BLOCK - HALO
        return spread[cut:-cut, cut:-cut][None]

    def coarse_apply(coarse):
        return jnp.dot(whole_matrix, coarse.reshape(-1), precision=PRECISE).reshape(coarse.shape)

    def scalars(*values):
        return jnp.stack([jnp.broadcast_to(v, (COARSE // 4,)) for v in values])

    coarse = all_sum(restrict(loading))
    lifted = coarse_apply(coarse)
    direction = inverse * residual + prolong(lifted)
    answer = jnp.zeros_like(loading)
    scaled_sum = inner_now = None
    for iteration in range(ITERS):
        image = operate(direction)
        near_image, near_scaled = inner_part(image), inner_part(inverse * image)
        near_direction, near_residual = inner_part(direction), inner_part(residual)
        packed = jnp.concatenate(
            [
                restrict(near_image),
                scalars(
                    jnp.sum(near_direction * near_image),
                    jnp.sum(near_residual * near_scaled),
                    jnp.sum(near_image * near_scaled),
                    jnp.sum(near_residual * inner_part(inverse) * near_residual),
                ),
            ]
        )
        packed = all_sum(packed)
        curvature, cross, square = packed[4, 0], packed[5, 0], packed[6, 0]
        if scaled_sum is None:
            scaled_sum = packed[7, 0]
            inner_now = scaled_sum + jnp.sum(coarse * lifted)
        alpha = inner_now / curvature
        answer = answer + alpha * near_direction
        residual = residual - alpha * image
        if iteration + 1 < ITERS:
            coarse = coarse - alpha * packed[:4]
            scaled_sum = scaled_sum - 2.0 * alpha * cross + alpha * alpha * square
            lifted = coarse_apply(coarse)
            inner_next = scaled_sum + jnp.sum(coarse * lifted)
            direction = inverse * residual + prolong(lifted) + inner_next / inner_now * direction
            inner_now = inner_next
    return answer, inner_part(residual)


def solution(mesh):
    in_specs = (
        P(None, "rows", "cols"),
        P(None, "rows", "cols"),
        P("rows", "cols"),
        P(None, "rows"),
    )
    out_specs = (P(None, "rows", "cols"), P(None, "rows", "cols"))
    return jax.shard_map(local, mesh=mesh, in_specs=in_specs, out_specs=out_specs, check_vma=False)
```

```python
import jax
import jax.numpy as jnp
from jax import lax
from jax.experimental import pallas as pl
from jax.experimental.pallas import tpu as pltpu
from jax.sharding import PartitionSpec as P

BLOCK = 16
COARSE = 512
ITERS = 4
HALO = 8
SIDE = 7
LANES = 128

MASS_TERM = 1.0
PRECISE = lax.Precision.HIGHEST
BOTH = ("rows", "cols")


def iota(shape, dim):
    return lax.broadcasted_iota(jnp.int32, shape, dim)


def roll(x, shift, axis):
    size = x.shape[axis]
    shift = shift % size
    return x if shift == 0 else pltpu.roll(x, shift, axis)


def lane_row():
    return iota((1, LANES), 1)


def block_sums(folded):
    spread = (iota((LANES, LANES), 0) // BLOCK == iota((LANES, LANES), 1) % (LANES // BLOCK))
    return jnp.dot(folded, spread.astype(jnp.float32), precision=PRECISE)


def fold_rows(plane):
    rows = plane.shape[0]
    return plane.reshape(rows // BLOCK, 2, 8, LANES).sum(axis=1)


def pack_blocks(folds, first):
    count = folds[0].shape[0]
    pad = (-count * len(folds)) % 8
    stacked = jnp.concatenate(folds + ([jnp.zeros((pad, LANES), jnp.float32)] if pad else []), axis=0)
    summed = block_sums(stacked)
    group = lane_row() // (LANES // BLOCK)
    row = jnp.zeros((1, LANES), jnp.float32)
    for index in range(len(folds) * count):
        row = row + jnp.where(group == first * count + index, summed[index : index + 1], 0.0)
    return row


def pack_scalars(partials, offset):
    lane = lane_row()
    row = jnp.zeros((1, LANES), jnp.float32)
    for index, partial in enumerate(partials):
        total = jnp.sum(jnp.sum(partial, axis=0, keepdims=True), axis=1, keepdims=True)
        row = row + jnp.where(lane == offset + index, total, 0.0)
    return row


def unfold(values, offset, width):
    devices = values.shape[0]
    lane = iota((devices, LANES), 1)
    part = jnp.where(lane < width, roll(values, -offset, 1), 0.0)
    step = width
    while step < LANES:
        part = part + roll(part, step, 1)
        step *= 2
    per_tile = LANES // width
    tiles = []
    for tile in range(devices // per_tile):
        owner = iota((devices, LANES), 0) == tile * per_tile + lane // width
        tiles.append(jnp.sum(jnp.where(owner, part, 0.0), axis=0, keepdims=True))
    return tiles


def restrict_column(values, ids):
    pieces = []
    for chunk in range(COARSE // 64):
        names = (iota((64, LANES), 0) + (chunk * 64 + 1)).astype(jnp.float32)
        total = jnp.zeros((64, LANES), jnp.float32)
        for value, name in zip(values, ids):
            total = total + jnp.where(names == name, value, 0.0)
        pieces.append(jnp.sum(total, axis=1, keepdims=True))
    return pieces


def column_to_row(pieces):
    eye = iota((64, LANES), 0) == iota((64, LANES), 1)
    eye_high = iota((64, LANES), 0) + 64 == iota((64, LANES), 1)
    tiles = []
    for pair in range(len(pieces) // 2):
        both = jnp.where(eye, pieces[2 * pair], 0.0) + jnp.where(eye_high, pieces[2 * pair + 1], 0.0)
        tiles.append(jnp.sum(both, axis=0, keepdims=True))
    return jnp.concatenate(tiles, axis=1)


def coarse_solve(values, ids, matrix_refs):
    row = column_to_row(restrict_column(values, ids))
    return [
        jnp.sum(ref[...] * row, axis=1, keepdims=True) for ref in matrix_refs
    ]


def lookup(pieces, position, id_tiles):
    totals = [jnp.zeros((8, LANES), jnp.float32) for _ in id_tiles]
    for part, piece in enumerate(pieces):
        names = (iota((64, LANES), 0) + ((position ^ part) * 64 + 1)).astype(jnp.float32)
        wide = jnp.broadcast_to(piece, (64, LANES))
        for index, name in enumerate(id_tiles):
            hit = jnp.where(names == name, wide, 0.0)
            totals[index] = totals[index] + hit.reshape(8, 8, LANES).sum(axis=0)
    return [jnp.sum(total, axis=0, keepdims=True) for total in totals]


def joined(tiles):
    return jnp.concatenate(tiles, axis=1)


def split_tiles(row):
    return [row[:, t * LANES : (t + 1) * LANES] for t in range(row.shape[1] // LANES)]


def apply_blocks(own, east, south, values, grid):
    count_x, count_y, blocks_x, blocks_y = grid
    width = blocks_x * blocks_y
    index = iota(values.shape, 1)
    device = index // width
    row, col = device // count_y, device % count_y
    at_x, at_y = (index % width) // blocks_y, index % blocks_y
    values_8 = values
    step_e = width - (blocks_y - 1)
    step_s = count_y * width - (blocks_x - 1) * blocks_y

    def take(x, inner, outer, is_inner, exists):
        moved = jnp.where(is_inner, roll(x, inner, 1), roll(x, outer, 1))
        return jnp.where(exists, moved, 0.0)

    from_e = take(values_8, -1, -step_e, at_y < blocks_y - 1, (at_y < blocks_y - 1) | (col < count_y - 1))
    from_s = take(
        values_8, -blocks_y, -step_s, at_x < blocks_x - 1, (at_x < blocks_x - 1) | (row < count_x - 1)
    )
    from_w = take(east * values_8, 1, step_e, at_y > 0, (at_y > 0) | (col > 0))
    from_n = take(south * values_8, blocks_y, step_s, at_x > 0, (at_x > 0) | (row > 0))
    return own * values - east * from_e - south * from_s - from_w - from_n


def prolong_plane(tiles, rows):
    pieces = []
    bounds = [0, HALO]
    while bounds[-1] + BLOCK < rows:
        bounds.append(bounds[-1] + BLOCK)
    bounds.append(rows)
    for index in range(len(bounds) - 1):
        line = joined(tiles[2 * index : 2 * index + 2])
        pieces.append(jnp.broadcast_to(line, (bounds[index + 1] - bounds[index], 2 * LANES)))
    return jnp.concatenate(pieces, axis=0)


def plane_ids(ids_ref):
    rows = ids_ref.shape[0]
    starts = [0] + list(range(HALO, rows, BLOCK))
    tiles = []
    for start in starts:
        tiles += split_tiles(ids_ref[start : start + 1, :])
    return tiles


class Operator:
    def __init__(self, w_layer, w_row, w_col):
        self.w_layer, self.w_row, self.w_col = w_layer, w_row, w_col

    def planes(self, source):
        layers = self.w_row.shape[0]
        current = source(0)
        below = self.w_layer[0] * current
        for layer in range(layers):
            after = source(layer + 1) if layer + 1 < layers else None
            above = self.w_layer[layer + 1] * (current - after if after is not None else current)
            total = MASS_TERM * current + above
            total = total + below if layer == 0 else total - below
            flux = self.w_row[layer] * (current - roll(current, -1, 0))
            total = total + flux - roll(flux, 1, 0)
            flux = self.w_col[layer] * (current - roll(current, -1, 1))
            total = total + flux - roll(flux, 1, 1)
            yield layer, total
            current, below = after, above


def near(plane):
    return plane[HALO:-HALO, :LANES]


def tally(plane):
    return plane.reshape(plane.shape[0] // 8, 8, LANES).sum(axis=0)


def first_kernel(aggregate, loading, viscosity, shard, down, up, sums, turned):
    layers, rows, _ = loading.shape
    blocks_x, blocks_y = aggregate.shape
    lane = lane_row()
    fold = jnp.zeros((blocks_x, 8, LANES), jnp.float32)
    for layer in range(layers):
        fold = fold + fold_rows(loading[layer])
        up[layer] = loading[layer, :HALO, :]
        up[layers + layer] = viscosity[layer, :HALO, :]
        down[layer] = loading[layer, rows - HALO :, :]
        down[layers + layer] = viscosity[layer, rows - HALO :, :]
    row = pack_blocks([fold.sum(axis=1)], 0)
    width = blocks_x * blocks_y
    for bx in range(blocks_x):
        names = jnp.zeros((1, LANES), jnp.float32)
        for by in range(blocks_y):
            name = (aggregate[bx, by] + 1).astype(jnp.float32)
            row = row + jnp.where(lane == width + bx * blocks_y + by, name, 0.0)
            names = jnp.where(lane // BLOCK == by, name, names)
        if bx == 0:
            up[2 * layers] = jnp.broadcast_to(names, (HALO, LANES))
        if bx == blocks_x - 1:
            down[2 * layers] = jnp.broadcast_to(names, (HALO, LANES))
    sums[...] = jnp.broadcast_to(row, sums.shape)
    turned[...] = shard[...].T


def own_ids(aggregate):
    lane = lane_row()
    blocks_x, blocks_y = aggregate.shape
    pieces = []
    for bx in range(blocks_x):
        names = jnp.zeros((1, LANES), jnp.float32)
        for by in range(blocks_y):
            names = jnp.where(lane // BLOCK == by, (aggregate[bx, by] + 1).astype(jnp.float32), names)
        pieces.append(jnp.broadcast_to(names, (BLOCK, LANES)))
    return jnp.concatenate(pieces, axis=0)


def tall_plane(slot, own, low, high):
    return jnp.concatenate([low[slot], own, high[slot]], axis=0)


def edge_kernel(aggregate, loading, viscosity, low, high, rightward, leftward):
    layers = loading.shape[0]
    lane = lane_row()
    right = left = None
    for slot in range(2 * layers + 1):
        if slot < layers:
            own = loading[slot]
        elif slot < 2 * layers:
            own = viscosity[slot - layers]
        else:
            own = own_ids(aggregate)
        plane = tall_plane(slot, own, low, high)
        at = slot * SIDE
        here = (lane >= at) & (lane < at + SIDE)
        moved_right = roll(plane, at + SIDE, 1)
        moved_left = roll(plane, at, 1)
        if right is None:
            right = jnp.where(here, moved_right, 0.0)
            left = jnp.where(here, moved_left, 0.0)
        else:
            right = jnp.where(here, moved_right, right)
            left = jnp.where(here, moved_left, left)
    rightward[...] = right
    leftward[...] = left


def start_kernel(
    position, aggregate, loading, viscosity, low, high, west, east, sums, *rest
):
    matrix, (resid, direction, image, inverse, w_layer, w_row, w_col, ids, message), scratch = (
        rest[:8],
        rest[8:17],
        rest[17:],
    )
    wide, plane_scratch, scaled, scaled_image = scratch
    layers = loading.shape[0]
    blocks_x, blocks_y = aggregate.shape
    width = blocks_x * blocks_y
    lane = lane_row()

    from_west, from_east = west[...], east[...]

    def widen(slot, own):
        at = slot * SIDE
        beyond = jnp.where(lane < SIDE, roll(from_east, -at, 1), 0.0)
        beyond = jnp.where(lane >= LANES - SIDE, roll(from_west, LANES - SIDE - at, 1), beyond)
        return jnp.concatenate([tall_plane(slot, own, low, high), beyond], axis=1)

    for layer in range(layers):
        resid[layer] = widen(layer, loading[layer])
        wide[layer] = widen(layers + layer, viscosity[layer])
    ids[...] = widen(2 * layers, own_ids(aggregate))

    face_rows = jnp.zeros((blocks_x + 1, LANES), jnp.float32)
    face_cols = jnp.zeros((layers * 8, 2 * LANES), jnp.float32)
    for layer in range(layers):
        visc = wide[layer]
        before = 0.5 * visc if layer == 0 else 0.5 * (visc + wide[layer - 1])
        after = 0.5 * visc if layer == layers - 1 else 0.5 * (visc + wide[layer + 1])
        by_row = 0.5 * (visc + roll(visc, -1, 0))
        by_col = 0.5 * (visc + roll(visc, -1, 1))
        if layer == 0:
            w_layer[0] = before
        w_layer[layer + 1] = after
        w_row[layer] = by_row
        w_col[layer] = by_col
        diagonal = MASS_TERM + before + after + by_row + roll(by_row, 1, 0) + by_col + roll(by_col, 1, 1)
        inverse[layer] = jnp.where(visc > 0.0, 1.0 / diagonal, 0.0)
    folds_own, folds_east, folds_south = block_matrix(w_layer, w_row, w_col)

    totals, names = unfold(sums[...], 0, width), unfold(sums[...], width, width)
    pieces = coarse_solve(totals, names, matrix)
    plane_scratch[...] = prolong_plane(lookup(pieces, position[0], plane_ids(ids)), ids.shape[0])
    for layer in range(layers):
        part = inverse[layer] * resid[layer]
        scaled[layer] = part
        direction[layer] = part + plane_scratch[...]

    operator = Operator(w_layer, w_row, w_col)
    zero = jnp.zeros((8, LANES), jnp.float32)
    folds = [jnp.zeros((blocks_x, 8, LANES), jnp.float32) for _ in range(3)]
    s_rp = s_rd = s_dq = s_eq = s_pq = s_dd = s_de = s_ee = zero
    for layer, plane in operator.planes(lambda k: direction[k]):
        image[layer] = plane
        part = inverse[layer] * plane
        scaled_image[layer] = part
        q, e, d, r, p = near(plane), near(part), near(scaled[layer]), near(resid[layer]), near(direction[layer])
        s_rp += tally(r * p)
        s_rd += tally(r * d)
        s_dq += tally(d * q)
        s_eq += tally(e * q)
        s_pq += tally(p * q)
        folds[0] += fold_rows(q)
    for layer, plane in operator.planes(lambda k: scaled[k]):
        s_dd += tally(near(plane) * near(scaled[layer]))
        s_de += tally(near(plane) * near(scaled_image[layer]))
        folds[1] += fold_rows(near(plane))
    for layer, plane in operator.planes(lambda k: scaled_image[k]):
        s_ee += tally(near(plane) * near(scaled_image[layer]))
        folds[2] += fold_rows(near(plane))
    upper = pack_blocks([fold.sum(axis=1) for fold in folds], 0)
    upper = upper + pack_scalars([s_rp, s_rd, s_dq, s_eq, s_pq, s_dd, s_de, s_ee], 3 * width)
    lower = pack_blocks([folds_own, folds_east, folds_south], 0)
    write_message(message, upper, lower)


def write_message(message, upper, lower):
    rows = iota(message.shape, 0)
    message[...] = jnp.where(rows % 2 == 0, upper, lower)


def block_matrix(w_layer, w_row, w_col):
    layers = w_row.shape[0]
    rows = w_row.shape[1]
    lane = lane_row()
    cols = jnp.zeros((rows, 2 * LANES), jnp.float32)
    line = jnp.zeros((rows, LANES), jnp.float32)
    for layer in range(layers):
        cols = cols + w_col[layer]
        line = line + w_row[layer, :, :LANES]
    ends = near(w_layer[0]) + near(w_layer[layers])
    own_cells = fold_rows(ends).sum(axis=1)
    east_face = fold_rows(jnp.where(lane % BLOCK == BLOCK - 1, near(cols), 0.0)).sum(axis=1)
    west_face = fold_rows(jnp.where(lane % BLOCK == 0, near(roll(cols, 1, 1)), 0.0)).sum(axis=1)
    count = own_cells.shape[0]
    south_face = jnp.concatenate(
        [line[HALO + BLOCK * (k + 1) - 1 : HALO + BLOCK * (k + 1)] for k in range(count)], axis=0
    )
    north_face = jnp.concatenate(
        [line[HALO + BLOCK * k - 1 : HALO + BLOCK * k] for k in range(count)], axis=0
    )
    mass = jnp.full((count, LANES), MASS_TERM * layers * BLOCK, jnp.float32)
    own = mass + own_cells + east_face + west_face + south_face + north_face
    return own, east_face, south_face


def lane_total(values, lane_at):
    return jnp.sum(values[:, lane_at : lane_at + 1], axis=0, keepdims=True)


def dot_rows(left, right):
    return jnp.sum(left * right, axis=1, keepdims=True)


def received(ref, parity):
    return ref[pl.ds(parity, ref.shape[0] // 2, stride=2), :]


def middle_kernel(grid, position, sums, arrived, ids, *rest):
    matrix = rest[:8]
    resid, direction, image, inverse, w_layer, w_row, w_col = rest[8:15]
    out_resid, out_lifted, prev_direction, prev_image, lifted_image, scalars, coarse_out, message = rest[15:23]
    scaled, scaled_prev, scaled_lifted, plane_scratch, plane_scratch_2 = rest[23:]
    width = grid[2] * grid[3]
    layers = resid.shape[0]
    blocks_x = grid[2]
    upper, lower = received(arrived, 0), received(arrived, 1)
    totals, names = unfold(sums[...], 0, width), unfold(sums[...], width, width)
    s_rp, s_rd, s_dq, s_eq, s_pq, s_dd, s_de, s_ee = [lane_total(upper, 3 * width + k) for k in range(8)]
    r_q, r_d, r_e = [joined(unfold(upper, k * width, width)) for k in range(3)]
    own, east, south = [joined(unfold(lower, k * width, width)) for k in range(3)]
    alpha0 = s_rp / s_pq
    scaled_sum = s_rd - 2.0 * alpha0 * s_dq + alpha0 * alpha0 * s_eq
    coarse1 = joined(totals) - alpha0 * r_q
    pieces = coarse_solve(split_tiles(coarse1), names, matrix)
    tiles = lookup(pieces, position[0], names + plane_ids(ids))
    lifted1 = joined(tiles[: len(names)])
    plane_scratch[...] = prolong_plane(tiles[len(names) :], ids.shape[0])
    inner1 = scaled_sum + dot_rows(coarse1, lifted1)
    beta0 = inner1 / s_rp
    r_x = r_d - alpha0 * r_e + beta0 * r_q
    energy = (
        s_dd
        - 2.0 * alpha0 * s_de
        + alpha0 * alpha0 * s_ee
        + 2.0 * beta0 * (s_dq - alpha0 * s_eq)
        + beta0 * beta0 * s_pq
    )
    block_image = apply_blocks(own, east, south, lifted1, grid)
    curvature = energy + dot_rows(lifted1, 2.0 * r_x + block_image)
    alpha1 = inner1 / curvature
    coarse2 = coarse1 - alpha1 * (r_x + block_image)
    pieces2 = coarse_solve(split_tiles(coarse2), names, matrix)
    tiles2 = lookup(pieces2, position[0], names + plane_ids(ids))
    coarse_out[...] = jnp.broadcast_to(joined(tiles2[: len(names)]), coarse_out.shape)
    plane_scratch_2[...] = prolong_plane(tiles2[len(names) :], ids.shape[0])
    lane = lane_row()
    numbers = jnp.where(lane == 0, alpha0, jnp.where(lane == 1, alpha1, jnp.where(lane == 2, inner1, 0.0)))
    scalars[...] = jnp.broadcast_to(numbers, scalars.shape)

    operator = Operator(w_layer, w_row, w_col)
    for layer in range(layers):
        after = resid[layer] - alpha0 * image[layer]
        out_resid[layer] = after
        prev_direction[layer] = inverse[layer] * after + plane_scratch[...] + beta0 * direction[layer]
    zero = jnp.zeros((8, LANES), jnp.float32)
    folds = [jnp.zeros((blocks_x, 8, LANES), jnp.float32) for _ in range(6)]
    s_rz = s_rd = s_zu = s_zq = s_pq = s_du = s_dq = s_us = s_uw = s_qw = zero
    s_dd = s_ds = s_dw = s_ss = s_sw = s_ww = zero
    for layer, plane in operator.planes(lambda k: prev_direction[k]):
        prev_image[layer] = plane
        after = out_resid[layer] - alpha1 * plane
        out_resid[layer] = after
        part = inverse[layer] * after
        scaled[layer] = part
        lifted = part + plane_scratch_2[...]
        out_lifted[layer] = lifted
        weighted = inverse[layer] * plane
        scaled_prev[layer] = weighted
        q, r, d, z, w, p = near(plane), near(after), near(part), near(lifted), near(weighted), near(prev_direction[layer])
        s_rz += tally(r * z)
        s_rd += tally(r * d)
        s_zq += tally(z * q)
        s_pq += tally(p * q)
        s_dq += tally(d * q)
        s_qw += tally(q * w)
        folds[1] += fold_rows(q)
        folds[5] += fold_rows(r)
    for layer, plane in operator.planes(lambda k: out_lifted[k]):
        lifted_image[layer] = plane
        part = inverse[layer] * plane
        scaled_lifted[layer] = part
        u, s = near(plane), near(part)
        s_zu += tally(u * near(out_lifted[layer]))
        s_du += tally(u * near(scaled[layer]))
        s_us += tally(u * s)
        s_uw += tally(u * near(scaled_prev[layer]))
        folds[0] += fold_rows(u)
    for layer, plane in operator.planes(lambda k: scaled[k]):
        image_d = near(plane)
        s_dd += tally(image_d * near(scaled[layer]))
        s_ds += tally(image_d * near(scaled_lifted[layer]))
        s_dw += tally(image_d * near(scaled_prev[layer]))
        folds[2] += fold_rows(image_d)
    for layer, plane in operator.planes(lambda k: scaled_lifted[k]):
        image_s = near(plane)
        s_ss += tally(image_s * near(scaled_lifted[layer]))
        s_sw += tally(image_s * near(scaled_prev[layer]))
        folds[3] += fold_rows(image_s)
    for layer, plane in operator.planes(lambda k: scaled_prev[k]):
        image_w = near(plane)
        s_ww += tally(image_w * near(scaled_prev[layer]))
        folds[4] += fold_rows(image_w)
    rows = [fold.sum(axis=1) for fold in folds]
    upper = pack_blocks(rows[:4], 0)
    lower = pack_blocks(rows[4:], 0) + pack_scalars(
        [s_rz, s_rd, s_zu, s_zq, s_pq, s_du, s_dq, s_us, s_uw, s_qw, s_dd, s_ds, s_dw, s_ss, s_sw, s_ww],
        2 * width,
    )
    write_message(message, upper, lower)


def last_kernel(grid, position, sums, before, arrived, ids, scalars, lifted2_ref, *rest):
    matrix = rest[:8]
    resid, lifted, direction1, image1, lifted_image, direction0, inverse, w_layer, w_row, w_col = rest[8:18]
    answer, out_resid = rest[18:20]
    direction3, plane_scratch = rest[20:]
    width = grid[2] * grid[3]
    layers = resid.shape[0]
    upper, lower = received(arrived, 0), received(arrived, 1)
    names = unfold(sums[...], width, width)
    blocks = received(before, 1)
    own, east, south = [joined(unfold(blocks, k * width, width)) for k in range(3)]
    r_u, r_q, r_d, r_s = [joined(unfold(upper, k * width, width)) for k in range(4)]
    r_w, r_r = [joined(unfold(lower, k * width, width)) for k in range(2)]
    (s_rz, s_rd, s_zu, s_zq, s_pq, s_du, s_dq, s_us, s_uw, s_qw, s_dd, s_ds, s_dw, s_ss, s_sw, s_ww) = [
        lane_total(lower, 2 * width + k) for k in range(16)
    ]
    alpha0, alpha1, inner1 = [scalars[0:1, k : k + 1] for k in range(3)]
    inner2 = s_rz
    beta1 = inner2 / inner1
    alpha2 = inner2 / (s_zu + 2.0 * beta1 * s_zq + beta1 * beta1 * s_pq)
    coarse3 = r_r - alpha2 * (r_u + beta1 * r_q)
    pieces = coarse_solve(split_tiles(coarse3), names, matrix)
    tiles = lookup(pieces, position[0], names + plane_ids(ids))
    lifted3 = joined(tiles[: len(names)])
    plane_scratch[...] = prolong_plane(tiles[len(names) :], ids.shape[0])
    scaled_sum = (
        s_rd
        - 2.0 * alpha2 * (s_du + beta1 * s_dq)
        + alpha2 * alpha2 * (s_us + 2.0 * beta1 * s_uw + beta1 * beta1 * s_qw)
    )
    inner3 = scaled_sum + dot_rows(coarse3, lifted3)
    beta2 = inner3 / inner2
    rise = lifted3 + beta2 * lifted2_ref[0:1, :]
    k_d, k_s, k_w, k_p = 1.0 + beta2, -alpha2, -alpha2 * beta1, beta2 * beta1
    energy = (
        k_d * k_d * s_dd
        + k_s * k_s * s_ss
        + k_w * k_w * s_ww
        + k_p * k_p * s_pq
        + 2.0 * (k_d * (k_s * s_ds + k_w * s_dw + k_p * s_dq) + k_s * (k_w * s_sw + k_p * s_uw) + k_w * k_p * s_qw)
    )
    r_x = k_d * r_d + k_s * r_s + k_w * r_w + k_p * r_q
    block_image = apply_blocks(own, east, south, rise, grid)
    curvature = energy + dot_rows(rise, 2.0 * r_x + block_image)
    alpha3 = inner3 / curvature

    operator = Operator(w_layer, w_row, w_col)
    for layer in range(layers):
        direction2 = lifted[layer] + beta1 * direction1[layer]
        image2 = lifted_image[layer] + beta1 * image1[layer]
        after = resid[layer] - alpha2 * image2
        step = inverse[layer] * after + plane_scratch[...] + beta2 * direction2
        direction3[layer] = step
        out_resid[layer] = near(after)
        answer[layer] = (
            alpha0 * near(direction0[layer])
            + alpha1 * near(direction1[layer])
            + alpha2 * near(direction2)
            + alpha3 * near(step)
        )
    for layer, plane in operator.planes(lambda k: direction3[k]):
        out_resid[layer] = out_resid[layer] - alpha3 * near(plane)


def call(kernel, outs, scratch, name, smem, *operands):
    whole = pl.BlockSpec(memory_space=pltpu.VMEM)
    scalar = pl.BlockSpec(memory_space=pltpu.SMEM)
    return pl.pallas_call(
        kernel,
        out_shape=[jax.ShapeDtypeStruct(shape, jnp.float32) for shape in outs],
        in_specs=[scalar] * smem + [whole] * (len(operands) - smem),
        out_specs=[whole] * len(outs),
        scratch_shapes=[pltpu.VMEM(shape, jnp.float32) for shape in scratch],
        compiler_params=pltpu.CompilerParams(vmem_limit_bytes=48 * 1024 * 1024),
        name=name,
    )(*operands)


def exchange(message):
    return lax.all_to_all(message, BOTH, 0, 0, tiled=True)


def shift(values, axis, step):
    count = lax.axis_size(axis)
    pairs = [(i, i + step) for i in range(count) if 0 <= i + step < count]
    return lax.ppermute(values, axis, pairs)


def cross(values, mask):
    return lax.ppermute(values, "rows", [(i, i ^ mask) for i in range(lax.axis_size("rows"))])


def local_steps(loading, viscosity, aggregate, coarse_inverse):
    layers, cells_x, cells_y = loading.shape
    blocks_x, blocks_y = aggregate.shape
    count_x, count_y = lax.axis_size("rows"), lax.axis_size("cols")
    devices = count_x * count_y
    grid = (count_x, count_y, blocks_x, blocks_y)
    position = lax.axis_index("rows").astype(jnp.int32).reshape(1)
    tall = cells_x + 2 * HALO
    edge = (2 * layers + 1, HALO, LANES)

    down, up, sums, turned = call(
        first_kernel,
        [edge, edge, (devices, LANES), (coarse_inverse.shape[1], COARSE)],
        [],
        "first",
        1,
        aggregate,
        loading,
        viscosity,
        coarse_inverse,
    )
    low, high = shift(down, "rows", 1), shift(up, "rows", -1)
    matrix = [turned] + [cross(turned, mask) for mask in (2, 4, 6)]
    rightward, leftward = call(
        edge_kernel, [(tall, LANES)] * 2, [], "edges", 1, aggregate, loading, viscosity, low, high
    )
    west, east = shift(rightward, "cols", 1), shift(leftward, "cols", -1)
    partner = [cross(part, 1) for part in matrix]
    matrix = [part for pair in zip(matrix, partner) for part in pair]
    sums = exchange(sums)

    field = (layers, tall, 2 * LANES)
    taller = (layers + 1, tall, 2 * LANES)
    plane = (tall, 2 * LANES)
    message = (2 * devices, LANES)
    resid, direction0, image0, inverse, w_layer, w_row, w_col, ids, message1 = call(
        start_kernel,
        [field] * 4 + [taller, field, field, plane, message],
        [field, plane, field, field],
        "start",
        2,
        position,
        aggregate,
        loading,
        viscosity,
        low,
        high,
        west,
        east,
        sums,
        *matrix,
    )
    arrived1 = exchange(message1)
    blocks = (8, devices * blocks_x * blocks_y)
    resid, lifted, direction1, image1, lifted_image, scalars, lifted2, message2 = call(
        lambda *refs: middle_kernel(grid, *refs),
        [field] * 5 + [(8, LANES), blocks, message],
        [field] * 3 + [plane] * 2,
        "middle",
        1,
        position,
        sums,
        arrived1,
        ids,
        *matrix,
        resid,
        direction0,
        image0,
        inverse,
        w_layer,
        w_row,
        w_col,
    )
    arrived2 = exchange(message2)
    return call(
        lambda *refs: last_kernel(grid, *refs),
        [loading.shape] * 2,
        [field, plane],
        "last",
        1,
        position,
        sums,
        arrived1,
        arrived2,
        ids,
        scalars,
        lifted2,
        *matrix,
        resid,
        lifted,
        direction1,
        image1,
        lifted_image,
        direction0,
        inverse,
        w_layer,
        w_row,
        w_col,
    )


def from_sides(block, axis, dim, width):
    count = lax.axis_size(axis)
    forward = [(i, i + 1) for i in range(count - 1)]
    backward = [(target, source) for source, target in forward]
    size = block.shape[dim]
    low = lax.ppermute(lax.slice_in_dim(block, size - width, size, axis=dim), axis, forward)
    high = lax.ppermute(lax.slice_in_dim(block, 0, width, axis=dim), axis, backward)
    return low, high


def widened(block, width_x, width_y):
    low, high = from_sides(block, "rows", block.ndim - 2, width_x)
    block = jnp.concatenate([low, block, high], axis=-2)
    turned = jnp.swapaxes(block, -1, -2)
    low, high = from_sides(turned, "cols", turned.ndim - 2, width_y)
    low, high = jnp.swapaxes(low, -1, -2), jnp.swapaxes(high, -1, -2)
    return jnp.concatenate([low, block, high], axis=-1)


def all_sum(values):
    count = lax.axis_size("rows") * lax.axis_size("cols")
    if count > 64:
        return lax.psum(lax.psum(values, "cols"), "rows")
    spread = jnp.broadcast_to(values[None], (count,) + values.shape)
    return lax.all_to_all(spread, BOTH, 0, 0).sum(axis=0)


def shifted(field, axis, step):
    return jnp.roll(field, step, axis=axis)


def local_general(loading, viscosity, aggregate, coarse_inverse):
    layers, cells_x, cells_y = loading.shape
    blocks_x, blocks_y = aggregate.shape
    ids = jnp.arange(COARSE, dtype=jnp.int32)
    whole_matrix = lax.all_gather(coarse_inverse, "rows", axis=1, tiled=True)
    fields = widened(jnp.stack([loading, viscosity]), HALO, HALO)
    wide_aggregate = widened(aggregate + 1, 1, 1) - 1
    table = (aggregate.reshape(-1)[:, None] == ids[None, :]).astype(jnp.float32)
    wide_table = (wide_aggregate.reshape(-1)[:, None] == ids[None, :]).astype(jnp.float32)

    residual, visc = fields[0], fields[1]
    inside = visc > 0.0
    pads = ((1, 1), (0, 0), (0, 0))
    padded = jnp.pad(visc, pads)
    weights = [
        0.5 * (visc + padded[:-2]),
        0.5 * (visc + padded[2:]),
        0.5 * (visc + shifted(visc, 1, 1)),
        0.5 * (visc + shifted(visc, 1, -1)),
        0.5 * (visc + shifted(visc, 2, 1)),
        0.5 * (visc + shifted(visc, 2, -1)),
    ]
    diagonal = MASS_TERM + sum(weights)
    inverse = jnp.where(inside, 1.0 / diagonal, 0.0)

    def operate(field):
        layered = jnp.pad(field, pads)
        sides = [
            layered[:-2],
            layered[2:],
            shifted(field, 1, 1),
            shifted(field, 1, -1),
            shifted(field, 2, 1),
            shifted(field, 2, -1),
        ]
        total = MASS_TERM * field
        for weight, side in zip(weights, sides):
            total = total + weight * (field - side)
        return total

    def inner_part(field):
        return field[:, HALO:-HALO, HALO:-HALO]

    def restrict(field):
        blocks = field.reshape(layers, blocks_x, BLOCK, blocks_y, BLOCK).sum(axis=(0, 2, 4))
        return jnp.dot(blocks.reshape(-1), table, precision=PRECISE).reshape(4, COARSE // 4)

    def prolong(values):
        per_block = jnp.dot(wide_table, values.reshape(-1), precision=PRECISE)
        per_block = per_block.reshape(blocks_x + 2, blocks_y + 2)
        spread = jnp.repeat(jnp.repeat(per_block, BLOCK, axis=0), BLOCK, axis=1)
        cut = BLOCK - HALO
        return spread[cut:-cut, cut:-cut][None]

    def coarse_apply(coarse):
        return jnp.dot(whole_matrix, coarse.reshape(-1), precision=PRECISE).reshape(coarse.shape)

    def scalars(*values):
        return jnp.stack([jnp.broadcast_to(v, (COARSE // 4,)) for v in values])

    coarse = all_sum(restrict(loading))
    lifted = coarse_apply(coarse)
    direction = inverse * residual + prolong(lifted)
    answer = jnp.zeros_like(loading)
    scaled_sum = inner_now = None
    for iteration in range(ITERS):
        image = operate(direction)
        near_image, near_scaled = inner_part(image), inner_part(inverse * image)
        near_direction, near_residual = inner_part(direction), inner_part(residual)
        packed = jnp.concatenate(
            [
                restrict(near_image),
                scalars(
                    jnp.sum(near_direction * near_image),
                    jnp.sum(near_residual * near_scaled),
                    jnp.sum(near_image * near_scaled),
                    jnp.sum(near_residual * inner_part(inverse) * near_residual),
                ),
            ]
        )
        packed = all_sum(packed)
        curvature, cross, square = packed[4, 0], packed[5, 0], packed[6, 0]
        if scaled_sum is None:
            scaled_sum = packed[7, 0]
            inner_now = scaled_sum + jnp.sum(coarse * lifted)
        alpha = inner_now / curvature
        answer = answer + alpha * near_direction
        residual = residual - alpha * image
        if iteration + 1 < ITERS:
            coarse = coarse - alpha * packed[:4]
            scaled_sum = scaled_sum - 2.0 * alpha * cross + alpha * alpha * square
            lifted = coarse_apply(coarse)
            inner_next = scaled_sum + jnp.sum(coarse * lifted)
            direction = inverse * residual + prolong(lifted) + inner_next / inner_now * direction
            inner_now = inner_next
    return answer, inner_part(residual)


def solution(mesh):
    in_specs = (
        P(None, "rows", "cols"),
        P(None, "rows", "cols"),
        P("rows", "cols"),
        P(None, "rows"),
    )
    out_specs = (P(None, "rows", "cols"), P(None, "rows", "cols"))
    small = mesh.shape["rows"] == 8 and mesh.shape["rows"] * mesh.shape["cols"] <= 64
    body = local_steps if small else local_general
    return jax.shard_map(body, mesh=mesh, in_specs=in_specs, out_specs=out_specs, check_vma=False)
```

```python
import jax
import jax.numpy as jnp
from jax import lax
from jax.experimental import pallas as pl
from jax.experimental.pallas import tpu as pltpu
from jax.sharding import PartitionSpec as P

BLOCK = 16
COARSE = 512
ITERS = 4
HALO = 8
SIDE = 7
LANES = 128
PART = 64

MASS_TERM = 1.0
PRECISE = lax.Precision.HIGHEST
BOTH = ("rows", "cols")


def iota(shape, dim):
    return lax.broadcasted_iota(jnp.int32, shape, dim)


def roll(x, shift, axis):
    size = x.shape[axis]
    shift = shift % size
    return x if shift == 0 else pltpu.roll(x, shift, axis)


def lane_row():
    return iota((1, LANES), 1)


def pick_lanes(values, index):
    return jnp.take_along_axis(values, index, axis=1, mode="promise_in_bounds")


def fold_rows(plane):
    rows = plane.shape[0]
    return plane.reshape(rows // BLOCK, 2, 8, LANES).sum(axis=1)


def pack_blocks(folds):
    count = folds[0].shape[0]
    pad = (-count * len(folds)) % 8
    stacked = jnp.concatenate(folds + ([jnp.zeros((pad, LANES), jnp.float32)] if pad else []), axis=0)
    spread = iota((LANES, LANES), 0) // BLOCK == iota((LANES, LANES), 1) % (LANES // BLOCK)
    summed = jnp.dot(stacked, spread.astype(jnp.float32), precision=PRECISE)
    group = lane_row() // (LANES // BLOCK)
    row = jnp.zeros((1, LANES), jnp.float32)
    for index in range(len(folds) * count):
        row = row + jnp.where(group == index, summed[index : index + 1], 0.0)
    return row


def pack_scalars(partials, offset):
    lane = lane_row()
    row = jnp.zeros((1, LANES), jnp.float32)
    for index, partial in enumerate(partials):
        total = jnp.sum(jnp.sum(partial, axis=0, keepdims=True), axis=1, keepdims=True)
        row = row + jnp.where(lane == offset + index, total, 0.0)
    return row


def unfold(values, slot, width):
    devices = values.shape[0]
    lane = iota((devices, LANES), 1)
    part = jnp.where(lane < width, roll(values, -slot * width, 1), 0.0)
    step = width
    while step < LANES:
        part = part + roll(part, step, 1)
        step *= 2
    per_row = LANES // width
    own = jnp.where(iota((devices, LANES), 0) % per_row == lane // width, part, 0.0)
    rows = [
        jnp.sum(own[k * per_row : (k + 1) * per_row], axis=0, keepdims=True) for k in range(devices // per_row)
    ]
    return jnp.concatenate(rows, axis=0)


def coarse_solve(values, names, position, parts):
    line = jnp.zeros((8, COARSE), jnp.float32)
    for part, ref in enumerate(parts):
        aggregate = iota((PART, LANES), 0) + ((position ^ part) * PART + 1)
        total = jnp.zeros((PART, LANES), jnp.float32)
        for row in range(8):
            total = total + jnp.where(aggregate == names[row : row + 1], values[row : row + 1], 0.0)
        column = jnp.sum(total, axis=1, keepdims=True)
        line = line + (ref[...] * column).reshape(PART // 8, 8, COARSE).sum(axis=0)
    line = jnp.broadcast_to(jnp.sum(line, axis=0, keepdims=True), (8, COARSE))
    return [line[:, t * LANES : (t + 1) * LANES] for t in range(COARSE // LANES)]


def lookup(coarse, names):
    index = jnp.maximum(names - 1, 0)
    inner = index % LANES
    result = jnp.zeros(names.shape, jnp.float32)
    for tile, values in enumerate(coarse):
        result = jnp.where(index // LANES == tile, pick_lanes(values, inner), result)
    return jnp.where(names > 0, result, 0.0)


def apply_blocks(own, east, south, values, grid):
    count_x, count_y, blocks_x, blocks_y = grid
    width = blocks_x * blocks_y
    lane = iota(values.shape, 1)
    row, col = iota(values.shape, 0), lane // width
    at_x, at_y = (lane % width) // blocks_y, lane % blocks_y
    last_x, last_y = at_x == blocks_x - 1, at_y == blocks_y - 1
    step_e = width - (blocks_y - 1)
    step_s = (blocks_x - 1) * blocks_y

    def take(x, inner, outer, is_outer, missing):
        return jnp.where(missing, 0.0, jnp.where(is_outer, outer(x), inner(x)))

    from_e = take(
        values, lambda x: roll(x, -1, 1), lambda x: roll(x, -step_e, 1), last_y, last_y & (col == count_y - 1)
    )
    from_w = take(
        east * values, lambda x: roll(x, 1, 1), lambda x: roll(x, step_e, 1), at_y == 0, (at_y == 0) & (col == 0)
    )
    from_s = take(
        values,
        lambda x: roll(x, -blocks_y, 1),
        lambda x: roll(roll(x, -1, 0), step_s, 1),
        last_x,
        last_x & (row == count_x - 1),
    )
    from_n = take(
        south * values,
        lambda x: roll(x, blocks_y, 1),
        lambda x: roll(roll(x, 1, 0), -step_s, 1),
        at_x == 0,
        (at_x == 0) & (row == 0),
    )
    return own * values - east * from_e - south * from_s - from_w - from_n


def local_names(ids):
    rows = ids.shape[0]
    lane = iota((8, LANES), 1)
    at = lane % BLOCK
    starts = [0] + list(range(HALO, rows, BLOCK))
    result = jnp.zeros((8, LANES), jnp.float32)
    for index, start in enumerate(starts):
        main = ids[start : start + 8, :LANES]
        side = ids[start : start + 8, LANES:]
        inner = pick_lanes(main, (at * BLOCK) % LANES)
        outer = pick_lanes(side, jnp.where(at == 8, 0, LANES - 1))
        both = jnp.where(at < 8, inner, jnp.where(at < 10, outer, 0.0))
        result = jnp.where(lane // BLOCK == index, both, result)
    return result


def prolong_plane(values, rows):
    lane = iota((8, LANES), 1)
    bounds = [0] + list(range(HALO, rows, BLOCK)) + [rows]
    pieces = []
    for index in range(len(bounds) - 1):
        main = pick_lanes(values, lane // BLOCK + index * BLOCK)
        side = pick_lanes(values, jnp.where(lane < BLOCK, 8, 9) + index * BLOCK)
        line = jnp.concatenate([main, side], axis=1)
        pieces += [line] * ((bounds[index + 1] - bounds[index]) // 8)
    return jnp.concatenate(pieces, axis=0)


class Operator:
    def __init__(self, w_layer, w_row, w_col):
        self.w_layer, self.w_row, self.w_col = w_layer, w_row, w_col

    def wide(self, source):
        layers = self.w_row.shape[0]
        current = source(0)
        below = self.w_layer[0] * current
        for layer in range(layers):
            after = source(layer + 1) if layer + 1 < layers else None
            above = self.w_layer[layer + 1] * (current - after if after is not None else current)
            total = MASS_TERM * current + above
            total = total + below if layer == 0 else total - below
            flux = self.w_row[layer] * (current - roll(current, -1, 0))
            total = total + flux - roll(flux, 1, 0)
            flux = self.w_col[layer] * (current - roll(current, -1, 1))
            total = total + flux - roll(flux, 1, 1)
            yield layer, total
            current, below = after, above

    def near(self, source):
        layers, rows = self.w_row.shape[:2]
        inner = slice(HALO, rows - HALO)
        plane = source(0)
        current = near(plane)
        below = self.w_layer[0, inner, :LANES] * current
        for layer in range(layers):
            following = source(layer + 1) if layer + 1 < layers else None
            after = near(following) if following is not None else None
            above = self.w_layer[layer + 1, inner, :LANES] * (current - after if after is not None else current)
            total = MASS_TERM * current + above
            total = total + below if layer == 0 else total - below
            column = plane[:, :LANES]
            flux = self.w_row[layer, :, :LANES] * (column - roll(column, -1, 0))
            total = total + (flux - roll(flux, 1, 0))[HALO:-HALO]
            band = plane[HALO:-HALO]
            flux = self.w_col[layer, inner, :] * (band - roll(band, -1, 1))
            total = total + (flux - roll(flux, 1, 1))[:, :LANES]
            yield layer, total
            plane, current, below = following, after, above


def near(plane):
    return plane[HALO:-HALO, :LANES]


def tally(plane):
    return plane.reshape(plane.shape[0] // 8, 8, LANES).sum(axis=0)


def own_ids(ids):
    blocks_x = ids.shape[0] // 2
    lines = [jnp.broadcast_to(ids[bx : bx + 1], (BLOCK, LANES)) for bx in range(blocks_x)]
    return jnp.concatenate(lines, axis=0)


def rows_kernel(
    position, aggregate_hbm, loading_hbm, viscosity_hbm,
    loading, viscosity, ids, near_rows, far_rows,
    aggregate, sems,
):
    layers, rows, _ = loading.shape
    odd = position[0] % 2
    copies = [
        pltpu.make_async_copy(aggregate_hbm, aggregate, sems.at[0]),
        pltpu.make_async_copy(loading_hbm, loading, sems.at[1]),
        pltpu.make_async_copy(viscosity_hbm, viscosity, sems.at[2]),
    ]
    for copy in copies:
        copy.start()
    copies[0].wait()
    blocks_x, blocks_y = aggregate.shape
    lane = lane_row()
    flat = jnp.zeros((1, LANES), jnp.float32)
    for bx in range(blocks_x):
        names = jnp.zeros((1, LANES), jnp.float32)
        for by in range(blocks_y):
            name = (aggregate[bx, by] + 1).astype(jnp.float32)
            names = jnp.where(lane // BLOCK == by, name, names)
            flat = jnp.where(lane % (blocks_x * blocks_y) == bx * blocks_y + by, name, flat)
        ids[bx : bx + 1] = names
    ids[blocks_x:] = jnp.broadcast_to(flat, (ids.shape[0] - blocks_x, LANES))
    first, last = ids[0:1], ids[blocks_x - 1 : blocks_x]
    near_rows[2 * layers] = jnp.broadcast_to(jnp.where(odd == 1, first, last), (HALO, LANES))
    far_rows[2 * layers] = jnp.broadcast_to(jnp.where(odd == 1, last, first), (HALO, LANES))
    near_at = pl.multiple_of((1 - odd) * (rows - HALO), HALO)
    far_at = pl.multiple_of(odd * (rows - HALO), HALO)
    for k, (copy, source) in enumerate(zip(copies[1:], (loading, viscosity))):
        copy.wait()
        near_rows[k * layers : (k + 1) * layers] = source[:, pl.ds(near_at, HALO), :]
        far_rows[k * layers : (k + 1) * layers] = source[:, pl.ds(far_at, HALO), :]


def shard_kernel(source, _, target, sem):
    copy = pltpu.make_async_copy(source, target, sem)
    copy.start()
    copy.wait()


def tall_plane(slot, own, odd, near_rows, far_rows):
    low = jnp.where(odd == 1, near_rows[slot], far_rows[slot])
    high = jnp.where(odd == 1, far_rows[slot], near_rows[slot])
    return jnp.concatenate([low, own, high], axis=0)


def edge_kernel(position, loading, viscosity, own_names, near_rows, far_rows, near_cols, far_cols):
    layers = loading.shape[0]
    odd = position[0] % 2
    lane = lane_row()
    right = left = jnp.zeros(near_cols.shape, jnp.float32)
    for slot in range(2 * layers + 1):
        if slot < layers:
            own = loading[slot]
        elif slot < 2 * layers:
            own = viscosity[slot - layers]
        else:
            own = own_ids(own_names)
        plane = tall_plane(slot, own, odd, near_rows, far_rows)
        at = slot * SIDE
        here = (lane >= at) & (lane < at + SIDE)
        right = jnp.where(here, roll(plane, at + SIDE, 1), right)
        left = jnp.where(here, roll(plane, at, 1), left)
    odd_col = position[1] % 2
    near_cols[...] = jnp.where(odd_col == 1, left, right)
    far_cols[...] = jnp.where(odd_col == 1, right, left)


def start_kernel(
    position, loading, viscosity, own_names, near_rows, far_rows, near_cols, far_cols,
    resid, inverse, w_layer, w_row, w_col, names_out, message,
    wide, ids, scaled,
):
    layers = loading.shape[0]
    blocks_x, blocks_y = loading.shape[1] // BLOCK, LANES // BLOCK
    width = blocks_x * blocks_y
    odd, odd_col = position[0] % 2, position[1] % 2
    lane = lane_row()
    from_west = jnp.where(odd_col == 1, near_cols[...], far_cols[...])
    from_east = jnp.where(odd_col == 1, far_cols[...], near_cols[...])

    def widen(slot, own):
        at = slot * SIDE
        beyond = jnp.where(lane < SIDE, roll(from_east, -at, 1), 0.0)
        beyond = jnp.where(lane >= LANES - SIDE, roll(from_west, LANES - SIDE - at, 1), beyond)
        return jnp.concatenate([tall_plane(slot, own, odd, near_rows, far_rows), beyond], axis=1)

    for layer in range(layers):
        resid[layer] = widen(layer, loading[layer])
        wide[layer] = widen(layers + layer, viscosity[layer])
    ids[...] = widen(2 * layers, own_ids(own_names))
    names_out[...] = local_names(ids)

    for layer in range(layers):
        visc = wide[layer]
        before = 0.5 * visc if layer == 0 else 0.5 * (visc + wide[layer - 1])
        after = 0.5 * visc if layer == layers - 1 else 0.5 * (visc + wide[layer + 1])
        by_row = 0.5 * (visc + roll(visc, -1, 0))
        by_col = 0.5 * (visc + roll(visc, -1, 1))
        if layer == 0:
            w_layer[0] = before
        w_layer[layer + 1] = after
        w_row[layer] = by_row
        w_col[layer] = by_col
        diagonal = MASS_TERM + before + after + by_row + roll(by_row, 1, 0) + by_col + roll(by_col, 1, 1)
        part = jnp.where(visc > 0.0, 1.0 / diagonal, 0.0)
        inverse[layer] = part
        scaled[layer] = part * resid[layer]
    folds_own, folds_east, folds_south = block_matrix(w_layer, w_row, w_col)

    zero = jnp.zeros((8, LANES), jnp.float32)
    fold_r = fold_t = jnp.zeros((blocks_x, 8, LANES), jnp.float32)
    s_rd = s_dt = zero
    for layer, image in Operator(w_layer, w_row, w_col).near(lambda k: scaled[k]):
        r, d = near(resid[layer]), near(scaled[layer])
        s_rd += tally(r * d)
        s_dt += tally(d * image)
        fold_r += fold_rows(r)
        fold_t += fold_rows(image)
    upper = pack_blocks([fold_r.sum(axis=1), fold_t.sum(axis=1)]) + pack_scalars([s_rd, s_dt], 2 * width)
    lower = pack_blocks([folds_own, folds_east, folds_south])
    lower = lower + jnp.where(lane >= 3 * width, own_names[blocks_x : blocks_x + 1], 0.0)
    write_message(message, upper, lower)


def write_message(message, upper, lower):
    rows = iota(message.shape, 0)
    message[...] = jnp.where(rows % 2 == 0, upper, lower)


def block_matrix(w_layer, w_row, w_col):
    layers = w_row.shape[0]
    rows = w_row.shape[1]
    lane = lane_row()
    cols = jnp.zeros((rows, 2 * LANES), jnp.float32)
    line = jnp.zeros((rows, LANES), jnp.float32)
    for layer in range(layers):
        cols = cols + w_col[layer]
        line = line + w_row[layer, :, :LANES]
    ends = near(w_layer[0]) + near(w_layer[layers])
    own_cells = fold_rows(ends).sum(axis=1)
    east_face = fold_rows(jnp.where(lane % BLOCK == BLOCK - 1, near(cols), 0.0)).sum(axis=1)
    west_face = fold_rows(jnp.where(lane % BLOCK == 0, near(roll(cols, 1, 1)), 0.0)).sum(axis=1)
    count = own_cells.shape[0]
    south_face = jnp.concatenate(
        [line[HALO + BLOCK * (k + 1) - 1 : HALO + BLOCK * (k + 1)] for k in range(count)], axis=0
    )
    north_face = jnp.concatenate(
        [line[HALO + BLOCK * k - 1 : HALO + BLOCK * k] for k in range(count)], axis=0
    )
    mass = jnp.full((count, LANES), MASS_TERM * layers * BLOCK, jnp.float32)
    own = mass + own_cells + east_face + west_face + south_face + north_face
    return own, east_face, south_face


def lane_total(values, lane_at):
    return jnp.sum(values[:, lane_at : lane_at + 1], axis=0, keepdims=True)


def dot_blocks(left, right):
    return jnp.sum(jnp.sum(left * right, axis=0, keepdims=True), axis=1, keepdims=True)


def received(ref, parity):
    return ref[pl.ds(parity, ref.shape[0] // 2, stride=2), :]


def block_operator(lower, width):
    own, east, south, names = [unfold(lower, k, width) for k in range(4)]
    return own, east, south, names.astype(jnp.int32)


def write_scalars(ref, values):
    lane = lane_row()
    line = jnp.zeros((1, LANES), jnp.float32)
    for index, value in enumerate(values):
        line = jnp.where(lane == index, value, line)
    ref[...] = jnp.broadcast_to(line, ref.shape)


def middle_kernel(grid, position, arrived, names_ref, *rest):
    parts = rest[:8]
    resid0, inverse, w_layer, w_row, w_col = rest[8:13]
    resid, lifted, direction, image, lifted_image, scalars, lifted_blocks, message = rest[13:21]
    scaled, scaled_image, scaled_lifted, rise_0, rise_1 = rest[21:]
    width = grid[2] * grid[3]
    layers, rows, _ = resid.shape
    upper, lower = received(arrived, 0), received(arrived, 1)
    own, east, south, names = block_operator(lower, width)
    here = names_ref[...].astype(jnp.int32)
    coarse0, r_d = unfold(upper, 0, width), unfold(upper, 1, width)
    s_rd, s_dt = lane_total(upper, 2 * width), lane_total(upper, 2 * width + 1)
    solved = coarse_solve(coarse0, names, position[0], parts)
    lifted0 = lookup(solved, names)
    rise_0[...] = prolong_plane(lookup(solved, here), rows)
    block_image = apply_blocks(own, east, south, lifted0, grid)
    inner0 = s_rd + dot_blocks(coarse0, lifted0)
    alpha0 = inner0 / (s_dt + dot_blocks(lifted0, 2.0 * r_d + block_image))
    coarse1 = coarse0 - alpha0 * (r_d + block_image)
    solved = coarse_solve(coarse1, names, position[0], parts)
    lifted_blocks[...] = lookup(solved, names)
    rise_1[...] = prolong_plane(lookup(solved, here), rows)
    write_scalars(scalars, [alpha0, inner0])

    operator = Operator(w_layer, w_row, w_col)
    for layer in range(layers):
        direction[layer] = inverse[layer] * resid0[layer] + rise_0[...]
    zero = jnp.zeros((8, LANES), jnp.float32)
    folds = [jnp.zeros((grid[2], 8, LANES), jnp.float32) for _ in range(6)]
    s_rz = s_rd = s_zu = s_zq = s_pq = s_du = s_dq = s_us = s_uw = s_qw = zero
    s_dd = s_ds = s_dw = s_ss = s_sw = s_ww = zero
    for layer, plane in operator.wide(lambda k: direction[k]):
        image[layer] = plane
        after = resid0[layer] - alpha0 * plane
        resid[layer] = after
        part = inverse[layer] * after
        scaled[layer] = part
        up = part + rise_1[...]
        lifted[layer] = up
        weighted = inverse[layer] * plane
        scaled_image[layer] = weighted
        q, r, d, z, w, p = near(plane), near(after), near(part), near(up), near(weighted), near(direction[layer])
        s_rz += tally(r * z)
        s_rd += tally(r * d)
        s_zq += tally(z * q)
        s_pq += tally(p * q)
        s_dq += tally(d * q)
        s_qw += tally(q * w)
        folds[1] += fold_rows(q)
        folds[5] += fold_rows(r)
    for layer, plane in operator.wide(lambda k: lifted[k]):
        lifted_image[layer] = plane
        part = inverse[layer] * plane
        scaled_lifted[layer] = part
        u, s = near(plane), near(part)
        s_zu += tally(u * near(lifted[layer]))
        s_du += tally(u * near(scaled[layer]))
        s_us += tally(u * s)
        s_uw += tally(u * near(scaled_image[layer]))
        folds[0] += fold_rows(u)
    for layer, image_d in operator.near(lambda k: scaled[k]):
        s_dd += tally(image_d * near(scaled[layer]))
        s_ds += tally(image_d * near(scaled_lifted[layer]))
        s_dw += tally(image_d * near(scaled_image[layer]))
        folds[2] += fold_rows(image_d)
    for layer, image_s in operator.near(lambda k: scaled_lifted[k]):
        s_ss += tally(image_s * near(scaled_lifted[layer]))
        s_sw += tally(image_s * near(scaled_image[layer]))
        folds[3] += fold_rows(image_s)
    for layer, image_w in operator.near(lambda k: scaled_image[k]):
        s_ww += tally(image_w * near(scaled_image[layer]))
        folds[4] += fold_rows(image_w)
    lines = [fold.sum(axis=1) for fold in folds]
    upper = pack_blocks(lines[:4])
    lower = pack_blocks(lines[4:]) + pack_scalars(
        [s_rz, s_rd, s_zu, s_zq, s_pq, s_du, s_dq, s_us, s_uw, s_qw, s_dd, s_ds, s_dw, s_ss, s_sw, s_ww],
        2 * width,
    )
    write_message(message, upper, lower)


def late_kernel(grid, position, before, arrived, names_ref, scalars, lifted1_ref, *rest):
    parts = rest[:8]
    resid1, lifted1, direction0, image0, lifted_image, inverse, w_layer, w_row, w_col = rest[8:17]
    answer, out_resid, out_direction, out_image, out_lifted, out_lifted_image, out_scalars, message = rest[17:25]
    direction, resid, lifted, rise_2, rise_3 = rest[25:]
    width = grid[2] * grid[3]
    layers, rows, _ = resid1.shape
    own, east, south, names = block_operator(received(before, 1), width)
    here = names_ref[...].astype(jnp.int32)
    upper, lower = received(arrived, 0), received(arrived, 1)
    r_u, r_q, r_d, r_s = [unfold(upper, k, width) for k in range(4)]
    r_w, r_r = [unfold(lower, k, width) for k in range(2)]
    (s_rz, s_rd, s_zu, s_zq, s_pq, s_du, s_dq, s_us, s_uw, s_qw, s_dd, s_ds, s_dw, s_ss, s_sw, s_ww) = [
        lane_total(lower, 2 * width + k) for k in range(16)
    ]
    alpha0, inner0 = [scalars[0:1, k : k + 1] for k in range(2)]
    inner1 = s_rz
    beta0 = inner1 / inner0
    alpha1 = inner1 / (s_zu + 2.0 * beta0 * s_zq + beta0 * beta0 * s_pq)
    coarse2 = r_r - alpha1 * (r_u + beta0 * r_q)
    solved = coarse_solve(coarse2, names, position[0], parts)
    lifted2 = lookup(solved, names)
    rise_2[...] = prolong_plane(lookup(solved, here), rows)
    scaled_sum = (
        s_rd
        - 2.0 * alpha1 * (s_du + beta0 * s_dq)
        + alpha1 * alpha1 * (s_us + 2.0 * beta0 * s_uw + beta0 * beta0 * s_qw)
    )
    inner2 = scaled_sum + dot_blocks(coarse2, lifted2)
    beta1 = inner2 / inner1
    rise = lifted2 + beta1 * lifted1_ref[...]
    k_d, k_s, k_w, k_p = 1.0 + beta1, -alpha1, -alpha1 * beta0, beta1 * beta0
    energy = (
        k_d * k_d * s_dd
        + k_s * k_s * s_ss
        + k_w * k_w * s_ww
        + k_p * k_p * s_pq
        + 2.0 * (k_d * (k_s * s_ds + k_w * s_dw + k_p * s_dq) + k_s * (k_w * s_sw + k_p * s_uw) + k_w * k_p * s_qw)
    )
    r_x = k_d * r_d + k_s * r_s + k_w * r_w + k_p * r_q
    block_image = apply_blocks(own, east, south, rise, grid)
    alpha2 = inner2 / (energy + dot_blocks(rise, 2.0 * r_x + block_image))
    coarse3 = coarse2 - alpha2 * (r_x + block_image)
    solved = coarse_solve(coarse3, names, position[0], parts)
    rise_3[...] = prolong_plane(lookup(solved, here), rows)
    write_scalars(out_scalars, [inner2])

    operator = Operator(w_layer, w_row, w_col)
    for layer in range(layers):
        step1 = lifted1[layer] + beta0 * direction0[layer]
        after = resid1[layer] - alpha1 * (lifted_image[layer] + beta0 * image0[layer])
        step2 = inverse[layer] * after + rise_2[...] + beta1 * step1
        direction[layer] = step2
        resid[layer] = after
        answer[layer] = alpha0 * near(direction0[layer]) + alpha1 * near(step1) + alpha2 * near(step2)
        out_direction[layer] = near(step2)
    s_rz = s_zu = s_zq = s_pq = jnp.zeros((8, LANES), jnp.float32)
    for layer, plane in operator.wide(lambda k: direction[k]):
        after = resid[layer] - alpha2 * plane
        up = inverse[layer] * after + rise_3[...]
        lifted[layer] = up
        q, r, z = near(plane), near(after), near(up)
        out_resid[layer] = r
        out_image[layer] = q
        out_lifted[layer] = z
        s_rz += tally(r * z)
        s_zq += tally(z * q)
        s_pq += tally(near(direction[layer]) * q)
    for layer, plane in operator.near(lambda k: lifted[k]):
        out_lifted_image[layer] = plane
        s_zu += tally(near(lifted[layer]) * plane)
    message[...] = jnp.broadcast_to(pack_scalars([s_rz, s_zu, s_zq, s_pq], 0), message.shape)


def last_kernel(arrived, scalars, answer, resid, direction, image, lifted, lifted_image, out, out_resid):
    s_rz, s_zu, s_zq, s_pq = [lane_total(arrived[...], k) for k in range(4)]
    beta = s_rz / scalars[0:1, 0:1]
    alpha = s_rz / (s_zu + 2.0 * beta * s_zq + beta * beta * s_pq)
    for layer in range(out.shape[0]):
        out[layer] = answer[layer] + alpha * (lifted[layer] + beta * direction[layer])
        out_resid[layer] = resid[layer] - alpha * (lifted_image[layer] + beta * image[layer])


def call(kernel, outs, scratch, name, smem, *operands, spaces=None):
    whole = pl.BlockSpec(memory_space=pltpu.VMEM)
    scalar = pl.BlockSpec(memory_space=pltpu.SMEM)
    specs = [scalar] * smem + [whole] * (len(operands) - smem)
    operands = list(operands)
    for index in spaces or ():
        specs[index] = pl.BlockSpec(memory_space=pltpu.HBM)
        operands[index] = pltpu.with_memory_space_constraint(operands[index], pltpu.HBM)
    return pl.pallas_call(
        kernel,
        out_shape=[jax.ShapeDtypeStruct(shape, jnp.float32) for shape in outs],
        in_specs=specs,
        out_specs=[whole] * len(outs),
        scratch_shapes=[pltpu.VMEM(s, jnp.float32) if isinstance(s, tuple) else s for s in scratch],
        compiler_params=pltpu.CompilerParams(vmem_limit_bytes=20 * 1024 * 1024),
        name=name,
    )(*operands)


def exchange(message):
    return lax.all_to_all(message, BOTH, 0, 0, tiled=True)


def pair(values, axis, mask):
    return lax.ppermute(values, axis, [(i, i ^ mask) for i in range(lax.axis_size(axis))])


def pair_far(values, axis):
    count = lax.axis_size(axis)
    return lax.ppermute(values, axis, [(i, i + 1 if i % 2 else i - 1) for i in range(1, count - 1)])


def local_steps(loading, viscosity, aggregate, coarse_inverse):
    layers, cells_x, cells_y = loading.shape
    blocks_x, blocks_y = aggregate.shape
    count_x, count_y = lax.axis_size("rows"), lax.axis_size("cols")
    devices = count_x * count_y
    grid = (count_x, count_y, blocks_x, blocks_y)
    position = jnp.stack([lax.axis_index(axis).astype(jnp.int32) for axis in BOTH])
    tall = cells_x + 2 * HALO
    edge = (2 * layers + 1, HALO, LANES)
    shard = coarse_inverse.T
    loading, viscosity, ids, near_rows, far_rows = call(
        rows_kernel,
        [loading.shape, viscosity.shape, (8, LANES), edge, edge],
        [pltpu.SMEM(aggregate.shape, jnp.int32), pltpu.SemaphoreType.DMA((3,))],
        "rows",
        1,
        position,
        aggregate,
        loading,
        viscosity,
        spaces=(1, 2, 3),
    )
    own = (position, loading, viscosity, ids)
    near_rows, far_rows = pair(near_rows, "rows", 1), pair_far(far_rows, "rows")
    near_cols, far_cols = call(edge_kernel, [(tall, LANES)] * 2, [], "edges", 1, *own, near_rows, far_rows)
    (shard,) = call(
        shard_kernel, [shard.shape], [pltpu.SemaphoreType.DMA(())], "shard", 0, shard, near_cols[:8], spaces=(0,)
    )
    near_cols, far_cols = pair(near_cols, "cols", 1), pair_far(far_cols, "cols")
    parts = [pair(shard, "rows", mask) for mask in (2, 4, 6)]

    field = (layers, tall, 2 * LANES)
    taller = (layers + 1, tall, 2 * LANES)
    plane = (tall, 2 * LANES)
    message = (2 * devices, LANES)
    line = (8, LANES)
    small = loading.shape
    resid, inverse, w_layer, w_row, w_col, names, message1 = call(
        start_kernel,
        [field, field, taller, field, field, line, message],
        [field, plane, field],
        "start",
        1,
        *own,
        near_rows,
        far_rows,
        near_cols,
        far_cols,
    )
    weights = (inverse, w_layer, w_row, w_col)
    arrived1 = exchange(message1)
    parts, arrived1 = lax.optimization_barrier(([shard] + parts, arrived1))
    parts = [part for both in ((part, pair(part, "rows", 1)) for part in parts) for part in both]
    resid, lifted, direction, image, lifted_image, scalars, lifted_blocks, message2 = call(
        lambda *refs: middle_kernel(grid, *refs),
        [field] * 5 + [line, line, message],
        [field] * 3 + [plane] * 2,
        "middle",
        1,
        position,
        arrived1,
        names,
        *parts,
        resid,
        *weights,
    )
    arrived2 = exchange(message2)
    answer, resid, direction, image, lifted, lifted_image, scalars, message3 = call(
        lambda *refs: late_kernel(grid, *refs),
        [small] * 6 + [line, (devices, LANES)],
        [field] * 3 + [plane] * 2,
        "late",
        1,
        position,
        arrived1,
        arrived2,
        names,
        scalars,
        lifted_blocks,
        *parts,
        resid,
        lifted,
        direction,
        image,
        lifted_image,
        *weights,
    )
    arrived3 = exchange(message3)
    return call(
        last_kernel,
        [small] * 2,
        [],
        "last",
        0,
        arrived3,
        scalars,
        answer,
        resid,
        direction,
        image,
        lifted,
        lifted_image,
    )


def from_sides(block, axis, dim, width):
    count = lax.axis_size(axis)
    forward = [(i, i + 1) for i in range(count - 1)]
    backward = [(target, source) for source, target in forward]
    size = block.shape[dim]
    low = lax.ppermute(lax.slice_in_dim(block, size - width, size, axis=dim), axis, forward)
    high = lax.ppermute(lax.slice_in_dim(block, 0, width, axis=dim), axis, backward)
    return low, high


def widened(block, width_x, width_y):
    low, high = from_sides(block, "rows", block.ndim - 2, width_x)
    block = jnp.concatenate([low, block, high], axis=-2)
    turned = jnp.swapaxes(block, -1, -2)
    low, high = from_sides(turned, "cols", turned.ndim - 2, width_y)
    low, high = jnp.swapaxes(low, -1, -2), jnp.swapaxes(high, -1, -2)
    return jnp.concatenate([low, block, high], axis=-1)


def all_sum(values):
    count = lax.axis_size("rows") * lax.axis_size("cols")
    if count > 64:
        return lax.psum(lax.psum(values, "cols"), "rows")
    spread = jnp.broadcast_to(values[None], (count,) + values.shape)
    return lax.all_to_all(spread, BOTH, 0, 0).sum(axis=0)


def shifted(field, axis, step):
    return jnp.roll(field, step, axis=axis)


def local_general(loading, viscosity, aggregate, coarse_inverse):
    layers, cells_x, cells_y = loading.shape
    blocks_x, blocks_y = aggregate.shape
    ids = jnp.arange(COARSE, dtype=jnp.int32)
    whole_matrix = lax.all_gather(coarse_inverse, "rows", axis=1, tiled=True)
    fields = widened(jnp.stack([loading, viscosity]), HALO, HALO)
    wide_aggregate = widened(aggregate + 1, 1, 1) - 1
    table = (aggregate.reshape(-1)[:, None] == ids[None, :]).astype(jnp.float32)
    wide_table = (wide_aggregate.reshape(-1)[:, None] == ids[None, :]).astype(jnp.float32)

    residual, visc = fields[0], fields[1]
    inside = visc > 0.0
    pads = ((1, 1), (0, 0), (0, 0))
    padded = jnp.pad(visc, pads)
    weights = [
        0.5 * (visc + padded[:-2]),
        0.5 * (visc + padded[2:]),
        0.5 * (visc + shifted(visc, 1, 1)),
        0.5 * (visc + shifted(visc, 1, -1)),
        0.5 * (visc + shifted(visc, 2, 1)),
        0.5 * (visc + shifted(visc, 2, -1)),
    ]
    diagonal = MASS_TERM + sum(weights)
    inverse = jnp.where(inside, 1.0 / diagonal, 0.0)

    def operate(field):
        layered = jnp.pad(field, pads)
        sides = [
            layered[:-2],
            layered[2:],
            shifted(field, 1, 1),
            shifted(field, 1, -1),
            shifted(field, 2, 1),
            shifted(field, 2, -1),
        ]
        total = MASS_TERM * field
        for weight, side in zip(weights, sides):
            total = total + weight * (field - side)
        return total

    def inner_part(field):
        return field[:, HALO:-HALO, HALO:-HALO]

    def restrict(field):
        blocks = field.reshape(layers, blocks_x, BLOCK, blocks_y, BLOCK).sum(axis=(0, 2, 4))
        return jnp.dot(blocks.reshape(-1), table, precision=PRECISE).reshape(4, COARSE // 4)

    def prolong(values):
        per_block = jnp.dot(wide_table, values.reshape(-1), precision=PRECISE)
        per_block = per_block.reshape(blocks_x + 2, blocks_y + 2)
        spread = jnp.repeat(jnp.repeat(per_block, BLOCK, axis=0), BLOCK, axis=1)
        cut = BLOCK - HALO
        return spread[cut:-cut, cut:-cut][None]

    def coarse_apply(coarse):
        return jnp.dot(whole_matrix, coarse.reshape(-1), precision=PRECISE).reshape(coarse.shape)

    def scalars(*values):
        return jnp.stack([jnp.broadcast_to(v, (COARSE // 4,)) for v in values])

    coarse = all_sum(restrict(loading))
    lifted = coarse_apply(coarse)
    direction = inverse * residual + prolong(lifted)
    answer = jnp.zeros_like(loading)
    scaled_sum = inner_now = None
    for iteration in range(ITERS):
        image = operate(direction)
        near_image, near_scaled = inner_part(image), inner_part(inverse * image)
        near_direction, near_residual = inner_part(direction), inner_part(residual)
        packed = jnp.concatenate(
            [
                restrict(near_image),
                scalars(
                    jnp.sum(near_direction * near_image),
                    jnp.sum(near_residual * near_scaled),
                    jnp.sum(near_image * near_scaled),
                    jnp.sum(near_residual * inner_part(inverse) * near_residual),
                ),
            ]
        )
        packed = all_sum(packed)
        curvature, cross, square = packed[4, 0], packed[5, 0], packed[6, 0]
        if scaled_sum is None:
            scaled_sum = packed[7, 0]
            inner_now = scaled_sum + jnp.sum(coarse * lifted)
        alpha = inner_now / curvature
        answer = answer + alpha * near_direction
        residual = residual - alpha * image
        if iteration + 1 < ITERS:
            coarse = coarse - alpha * packed[:4]
            scaled_sum = scaled_sum - 2.0 * alpha * cross + alpha * alpha * square
            lifted = coarse_apply(coarse)
            inner_next = scaled_sum + jnp.sum(coarse * lifted)
            direction = inverse * residual + prolong(lifted) + inner_next / inner_now * direction
            inner_now = inner_next
    return answer, inner_part(residual)


def solution(mesh):
    in_specs = (
        P(None, "rows", "cols"),
        P(None, "rows", "cols"),
        P("rows", "cols"),
        P(None, "rows"),
    )
    out_specs = (P(None, "rows", "cols"), P(None, "rows", "cols"))
    body = local_steps if (mesh.shape["rows"], mesh.shape["cols"]) == (8, 4) else local_general
    return jax.shard_map(body, mesh=mesh, in_specs=in_specs, out_specs=out_specs, check_vma=False)
```

```python
import jax
import jax.numpy as jnp
from jax import lax
from jax.experimental import pallas as pl
from jax.experimental.pallas import tpu as pltpu
from jax.sharding import PartitionSpec as P

BLOCK = 16
COARSE = 512
ITERS = 4
HALO = 8
SIDE = 7
LANES = 128
PART = 64

MASS_TERM = 1.0
PRECISE = lax.Precision.HIGHEST
BOTH = ("rows", "cols")


def iota(shape, dim):
    return lax.broadcasted_iota(jnp.int32, shape, dim)


def roll(x, shift, axis):
    size = x.shape[axis]
    shift = shift % size
    return x if shift == 0 else pltpu.roll(x, shift, axis)


def lane_row():
    return iota((1, LANES), 1)


def pick_lanes(values, index):
    return jnp.take_along_axis(values, index, axis=1, mode="promise_in_bounds")


def fold_rows(plane):
    rows = plane.shape[0]
    return plane.reshape(rows // BLOCK, 2, 8, LANES).sum(axis=1)


def pack_blocks(folds):
    count = folds[0].shape[0]
    pad = (-count * len(folds)) % 8
    stacked = jnp.concatenate(folds + ([jnp.zeros((pad, LANES), jnp.float32)] if pad else []), axis=0)
    spread = iota((LANES, LANES), 0) // BLOCK == iota((LANES, LANES), 1) % (LANES // BLOCK)
    summed = jnp.dot(stacked, spread.astype(jnp.float32), precision=PRECISE)
    group = lane_row() // (LANES // BLOCK)
    row = jnp.zeros((1, LANES), jnp.float32)
    for index in range(len(folds) * count):
        row = row + jnp.where(group == index, summed[index : index + 1], 0.0)
    return row


def pack_scalars(partials, offset):
    lane = lane_row()
    row = jnp.zeros((1, LANES), jnp.float32)
    for index, partial in enumerate(partials):
        total = jnp.sum(jnp.sum(partial, axis=0, keepdims=True), axis=1, keepdims=True)
        row = row + jnp.where(lane == offset + index, total, 0.0)
    return row


def unfold(values, slot, width):
    devices = values.shape[0]
    lane = iota((devices, LANES), 1)
    part = jnp.where(lane < width, roll(values, -slot * width, 1), 0.0)
    step = width
    while step < LANES:
        part = part + roll(part, step, 1)
        step *= 2
    per_row = LANES // width
    own = jnp.where(iota((devices, LANES), 0) % per_row == lane // width, part, 0.0)
    rows = [
        jnp.sum(own[k * per_row : (k + 1) * per_row], axis=0, keepdims=True) for k in range(devices // per_row)
    ]
    return jnp.concatenate(rows, axis=0)


def coarse_solve(values, names, position, parts):
    line = jnp.zeros((8, COARSE), jnp.float32)
    for part, ref in enumerate(parts):
        aggregate = iota((PART, LANES), 0) + ((position ^ part) * PART + 1)
        total = jnp.zeros((PART, LANES), jnp.float32)
        for row in range(8):
            total = total + jnp.where(aggregate == names[row : row + 1], values[row : row + 1], 0.0)
        column = jnp.sum(total, axis=1, keepdims=True)
        line = line + (ref[...] * column).reshape(PART // 8, 8, COARSE).sum(axis=0)
    line = jnp.broadcast_to(jnp.sum(line, axis=0, keepdims=True), (8, COARSE))
    return [line[:, t * LANES : (t + 1) * LANES] for t in range(COARSE // LANES)]


def lookup(coarse, names):
    index = jnp.maximum(names - 1, 0)
    inner = index % LANES
    result = jnp.zeros(names.shape, jnp.float32)
    for tile, values in enumerate(coarse):
        result = jnp.where(index // LANES == tile, pick_lanes(values, inner), result)
    return jnp.where(names > 0, result, 0.0)


def apply_blocks(own, east, south, values, grid):
    count_x, count_y, blocks_x, blocks_y = grid
    width = blocks_x * blocks_y
    lane = iota(values.shape, 1)
    row, col = iota(values.shape, 0), lane // width
    at_x, at_y = (lane % width) // blocks_y, lane % blocks_y
    last_x, last_y = at_x == blocks_x - 1, at_y == blocks_y - 1
    step_e = width - (blocks_y - 1)
    step_s = (blocks_x - 1) * blocks_y

    def take(x, inner, outer, is_outer, missing):
        return jnp.where(missing, 0.0, jnp.where(is_outer, outer(x), inner(x)))

    from_e = take(
        values, lambda x: roll(x, -1, 1), lambda x: roll(x, -step_e, 1), last_y, last_y & (col == count_y - 1)
    )
    from_w = take(
        east * values, lambda x: roll(x, 1, 1), lambda x: roll(x, step_e, 1), at_y == 0, (at_y == 0) & (col == 0)
    )
    from_s = take(
        values,
        lambda x: roll(x, -blocks_y, 1),
        lambda x: roll(roll(x, -1, 0), step_s, 1),
        last_x,
        last_x & (row == count_x - 1),
    )
    from_n = take(
        south * values,
        lambda x: roll(x, blocks_y, 1),
        lambda x: roll(roll(x, 1, 0), -step_s, 1),
        at_x == 0,
        (at_x == 0) & (row == 0),
    )
    return own * values - east * from_e - south * from_s - from_w - from_n


def local_names(ids):
    rows = ids.shape[0]
    lane = iota((8, LANES), 1)
    at = lane % BLOCK
    starts = [0] + list(range(HALO, rows, BLOCK))
    result = jnp.zeros((8, LANES), jnp.float32)
    for index, start in enumerate(starts):
        main = ids[start : start + 8, :LANES]
        side = ids[start : start + 8, LANES:]
        inner = pick_lanes(main, (at * BLOCK) % LANES)
        outer = pick_lanes(side, jnp.where(at == 8, 0, LANES - 1))
        both = jnp.where(at < 8, inner, jnp.where(at < 10, outer, 0.0))
        result = jnp.where(lane // BLOCK == index, both, result)
    return result


def prolong_plane(values, rows):
    lane = iota((8, LANES), 1)
    bounds = [0] + list(range(HALO, rows, BLOCK)) + [rows]
    pieces = []
    for index in range(len(bounds) - 1):
        main = pick_lanes(values, lane // BLOCK + index * BLOCK)
        side = pick_lanes(values, jnp.where(lane < BLOCK, 8, 9) + index * BLOCK)
        line = jnp.concatenate([main, side], axis=1)
        pieces += [line] * ((bounds[index + 1] - bounds[index]) // 8)
    return jnp.concatenate(pieces, axis=0)


class Operator:
    def __init__(self, w_layer, w_row, w_col):
        self.w_layer, self.w_row, self.w_col = w_layer, w_row, w_col

    def wide(self, source):
        layers = self.w_row.shape[0]
        current = source(0)
        below = self.w_layer[0] * current
        for layer in range(layers):
            after = source(layer + 1) if layer + 1 < layers else None
            above = self.w_layer[layer + 1] * (current - after if after is not None else current)
            total = MASS_TERM * current + above
            total = total + below if layer == 0 else total - below
            flux = self.w_row[layer] * (current - roll(current, -1, 0))
            total = total + flux - roll(flux, 1, 0)
            flux = self.w_col[layer] * (current - roll(current, -1, 1))
            total = total + flux - roll(flux, 1, 1)
            yield layer, total
            current, below = after, above

    def near(self, source):
        layers, rows = self.w_row.shape[:2]
        inner = slice(HALO, rows - HALO)
        plane = source(0)
        current = near(plane)
        below = self.w_layer[0, inner, :LANES] * current
        for layer in range(layers):
            following = source(layer + 1) if layer + 1 < layers else None
            after = near(following) if following is not None else None
            above = self.w_layer[layer + 1, inner, :LANES] * (current - after if after is not None else current)
            total = MASS_TERM * current + above
            total = total + below if layer == 0 else total - below
            column = plane[:, :LANES]
            flux = self.w_row[layer, :, :LANES] * (column - roll(column, -1, 0))
            total = total + (flux - roll(flux, 1, 0))[HALO:-HALO]
            band = plane[HALO:-HALO]
            flux = self.w_col[layer, inner, :] * (band - roll(band, -1, 1))
            total = total + (flux - roll(flux, 1, 1))[:, :LANES]
            yield layer, total
            plane, current, below = following, after, above


def near(plane):
    return plane[HALO:-HALO, :LANES]


def tally(plane):
    return plane.reshape(plane.shape[0] // 8, 8, LANES).sum(axis=0)


def own_ids(ids):
    blocks_x = ids.shape[0] // 2
    lines = [jnp.broadcast_to(ids[bx : bx + 1], (BLOCK, LANES)) for bx in range(blocks_x)]
    return jnp.concatenate(lines, axis=0)


def rows_kernel(
    position, aggregate_hbm, loading_hbm, viscosity_hbm, shard_hbm,
    loading, viscosity, ids, near_rows, far_rows, shard, message,
    aggregate, sems,
):
    layers, rows, _ = loading.shape
    odd = position[0] % 2
    copies = [
        pltpu.make_async_copy(aggregate_hbm, aggregate, sems.at[0]),
        pltpu.make_async_copy(loading_hbm, loading, sems.at[1]),
        pltpu.make_async_copy(viscosity_hbm, viscosity, sems.at[2]),
        pltpu.make_async_copy(shard_hbm, shard, sems.at[3]),
    ]
    for copy in copies:
        copy.start()
    copies[0].wait()
    blocks_x, blocks_y = aggregate.shape
    lane = lane_row()
    flat = jnp.zeros((1, LANES), jnp.float32)
    for bx in range(blocks_x):
        names = jnp.zeros((1, LANES), jnp.float32)
        for by in range(blocks_y):
            name = (aggregate[bx, by] + 1).astype(jnp.float32)
            names = jnp.where(lane // BLOCK == by, name, names)
            flat = jnp.where(lane % (blocks_x * blocks_y) == bx * blocks_y + by, name, flat)
        ids[bx : bx + 1] = names
    ids[blocks_x:] = jnp.broadcast_to(flat, (ids.shape[0] - blocks_x, LANES))
    first, last = ids[0:1], ids[blocks_x - 1 : blocks_x]
    near_rows[2 * layers] = jnp.broadcast_to(jnp.where(odd == 1, first, last), (HALO, LANES))
    far_rows[2 * layers] = jnp.broadcast_to(jnp.where(odd == 1, last, first), (HALO, LANES))
    near_at = pl.multiple_of((1 - odd) * (rows - HALO), HALO)
    far_at = pl.multiple_of(odd * (rows - HALO), HALO)
    for k, (copy, source) in enumerate(zip(copies[1:3], (loading, viscosity))):
        copy.wait()
        near_rows[k * layers : (k + 1) * layers] = source[:, pl.ds(near_at, HALO), :]
        far_rows[k * layers : (k + 1) * layers] = source[:, pl.ds(far_at, HALO), :]
    fold = jnp.zeros((blocks_x, 8, LANES), jnp.float32)
    for layer in range(layers):
        fold = fold + fold_rows(loading[layer])
    width = blocks_x * blocks_y
    line = pack_blocks([fold.sum(axis=1)]) + jnp.where((lane >= width) & (lane < 2 * width), flat, 0.0)
    message[...] = jnp.broadcast_to(line, message.shape)
    copies[3].wait()


def tall_plane(slot, own, odd, near_rows, far_rows):
    low = jnp.where(odd == 1, near_rows[slot], far_rows[slot])
    high = jnp.where(odd == 1, far_rows[slot], near_rows[slot])
    return jnp.concatenate([low, own, high], axis=0)


def edge_kernel(position, loading, viscosity, own_names, near_rows, far_rows, near_cols, far_cols):
    layers = loading.shape[0]
    odd = position[0] % 2
    lane = lane_row()
    right = left = jnp.zeros(near_cols.shape, jnp.float32)
    for slot in range(2 * layers + 1):
        if slot < layers:
            own = loading[slot]
        elif slot < 2 * layers:
            own = viscosity[slot - layers]
        else:
            own = own_ids(own_names)
        plane = tall_plane(slot, own, odd, near_rows, far_rows)
        at = slot * SIDE
        here = (lane >= at) & (lane < at + SIDE)
        right = jnp.where(here, roll(plane, at + SIDE, 1), right)
        left = jnp.where(here, roll(plane, at, 1), left)
    odd_col = position[1] % 2
    near_cols[...] = jnp.where(odd_col == 1, left, right)
    far_cols[...] = jnp.where(odd_col == 1, right, left)


def start_kernel(
    position, loading, viscosity, own_names, near_rows, far_rows, near_cols, far_cols, arrived, *rest
):
    parts = rest[:8]
    resid, direction, image, inverse, w_layer, w_row, w_col, names_out, message = rest[8:17]
    wide, ids, scaled, scaled_image, rise = rest[17:]
    layers = loading.shape[0]
    blocks_x, blocks_y = loading.shape[1] // BLOCK, LANES // BLOCK
    width = blocks_x * blocks_y
    odd, odd_col = position[0] % 2, position[1] % 2
    lane = lane_row()
    from_west = jnp.where(odd_col == 1, near_cols[...], far_cols[...])
    from_east = jnp.where(odd_col == 1, far_cols[...], near_cols[...])

    def widen(slot, own):
        at = slot * SIDE
        beyond = jnp.where(lane < SIDE, roll(from_east, -at, 1), 0.0)
        beyond = jnp.where(lane >= LANES - SIDE, roll(from_west, LANES - SIDE - at, 1), beyond)
        return jnp.concatenate([tall_plane(slot, own, odd, near_rows, far_rows), beyond], axis=1)

    for layer in range(layers):
        resid[layer] = widen(layer, loading[layer])
        wide[layer] = widen(layers + layer, viscosity[layer])
    ids[...] = widen(2 * layers, own_ids(own_names))
    names_out[...] = local_names(ids)

    for layer in range(layers):
        visc = wide[layer]
        before = 0.5 * visc if layer == 0 else 0.5 * (visc + wide[layer - 1])
        after = 0.5 * visc if layer == layers - 1 else 0.5 * (visc + wide[layer + 1])
        by_row = 0.5 * (visc + roll(visc, -1, 0))
        by_col = 0.5 * (visc + roll(visc, -1, 1))
        if layer == 0:
            w_layer[0] = before
        w_layer[layer + 1] = after
        w_row[layer] = by_row
        w_col[layer] = by_col
        diagonal = MASS_TERM + before + after + by_row + roll(by_row, 1, 0) + by_col + roll(by_col, 1, 1)
        part = jnp.where(visc > 0.0, 1.0 / diagonal, 0.0)
        inverse[layer] = part
        scaled[layer] = part * resid[layer]
    folds_own, folds_east, folds_south = block_matrix(w_layer, w_row, w_col)

    sums = arrived[...]
    names = unfold(sums, 1, width).astype(jnp.int32)
    solved = coarse_solve(unfold(sums, 0, width), names, position[0], parts)
    rise[...] = prolong_plane(lookup(solved, names_out[...].astype(jnp.int32)), ids.shape[0])
    for layer in range(layers):
        direction[layer] = scaled[layer] + rise[...]

    operator = Operator(w_layer, w_row, w_col)
    zero = jnp.zeros((8, LANES), jnp.float32)
    folds = [jnp.zeros((blocks_x, 8, LANES), jnp.float32) for _ in range(3)]
    s_rp = s_rd = s_dq = s_eq = s_pq = s_dd = s_de = s_ee = zero
    for layer, plane in operator.wide(lambda k: direction[k]):
        image[layer] = plane
        part = inverse[layer] * plane
        scaled_image[layer] = part
        q, e, d, r, p = near(plane), near(part), near(scaled[layer]), near(resid[layer]), near(direction[layer])
        s_rp += tally(r * p)
        s_rd += tally(r * d)
        s_dq += tally(d * q)
        s_eq += tally(e * q)
        s_pq += tally(p * q)
        folds[0] += fold_rows(q)
    for layer, image_d in operator.near(lambda k: scaled[k]):
        s_dd += tally(image_d * near(scaled[layer]))
        s_de += tally(image_d * near(scaled_image[layer]))
        folds[1] += fold_rows(image_d)
    for layer, image_e in operator.near(lambda k: scaled_image[k]):
        s_ee += tally(image_e * near(scaled_image[layer]))
        folds[2] += fold_rows(image_e)
    upper = pack_blocks([fold.sum(axis=1) for fold in folds])
    upper = upper + pack_scalars([s_rp, s_rd, s_dq, s_eq, s_pq, s_dd, s_de, s_ee], 3 * width)
    lower = pack_blocks([folds_own, folds_east, folds_south])
    write_message(message, upper, lower)


def write_message(message, upper, lower):
    rows = iota(message.shape, 0)
    message[...] = jnp.where(rows % 2 == 0, upper, lower)


def block_matrix(w_layer, w_row, w_col):
    layers = w_row.shape[0]
    rows = w_row.shape[1]
    lane = lane_row()
    cols = jnp.zeros((rows, 2 * LANES), jnp.float32)
    line = jnp.zeros((rows, LANES), jnp.float32)
    for layer in range(layers):
        cols = cols + w_col[layer]
        line = line + w_row[layer, :, :LANES]
    ends = near(w_layer[0]) + near(w_layer[layers])
    own_cells = fold_rows(ends).sum(axis=1)
    east_face = fold_rows(jnp.where(lane % BLOCK == BLOCK - 1, near(cols), 0.0)).sum(axis=1)
    west_face = fold_rows(jnp.where(lane % BLOCK == 0, near(roll(cols, 1, 1)), 0.0)).sum(axis=1)
    count = own_cells.shape[0]
    south_face = jnp.concatenate(
        [line[HALO + BLOCK * (k + 1) - 1 : HALO + BLOCK * (k + 1)] for k in range(count)], axis=0
    )
    north_face = jnp.concatenate(
        [line[HALO + BLOCK * k - 1 : HALO + BLOCK * k] for k in range(count)], axis=0
    )
    mass = jnp.full((count, LANES), MASS_TERM * layers * BLOCK, jnp.float32)
    own = mass + own_cells + east_face + west_face + south_face + north_face
    return own, east_face, south_face


def lane_total(values, lane_at):
    return jnp.sum(values[:, lane_at : lane_at + 1], axis=0, keepdims=True)


def dot_blocks(left, right):
    return jnp.sum(jnp.sum(left * right, axis=0, keepdims=True), axis=1, keepdims=True)


def received(ref, parity):
    return ref[pl.ds(parity, ref.shape[0] // 2, stride=2), :]


def write_scalars(ref, values):
    lane = lane_row()
    line = jnp.zeros((1, LANES), jnp.float32)
    for index, value in enumerate(values):
        line = jnp.where(lane == index, value, line)
    ref[...] = jnp.broadcast_to(line, ref.shape)


def middle_kernel(grid, position, arrived0, arrived, names_ref, *rest):
    parts = rest[:8]
    resid0, direction0, image0, inverse, w_layer, w_row, w_col = rest[8:15]
    resid, lifted, direction, image, lifted_image, scalars, lifted_blocks, message = rest[15:23]
    scaled, scaled_image, scaled_lifted, rise_0, rise_1 = rest[23:]
    width = grid[2] * grid[3]
    layers, rows, _ = resid.shape
    sums = arrived0[...]
    names = unfold(sums, 1, width).astype(jnp.int32)
    here = names_ref[...].astype(jnp.int32)
    upper, lower = received(arrived, 0), received(arrived, 1)
    s_rp, s_rd, s_dq, s_eq, s_pq, s_dd, s_de, s_ee = [lane_total(upper, 3 * width + k) for k in range(8)]
    r_q, r_d, r_e = [unfold(upper, k, width) for k in range(3)]
    own, east, south = [unfold(lower, k, width) for k in range(3)]
    alpha0 = s_rp / s_pq
    scaled_sum = s_rd - 2.0 * alpha0 * s_dq + alpha0 * alpha0 * s_eq
    coarse1 = unfold(sums, 0, width) - alpha0 * r_q
    solved = coarse_solve(coarse1, names, position[0], parts)
    lifted1 = lookup(solved, names)
    rise_0[...] = prolong_plane(lookup(solved, here), rows)
    inner1 = scaled_sum + dot_blocks(coarse1, lifted1)
    beta0 = inner1 / s_rp
    r_x = r_d - alpha0 * r_e + beta0 * r_q
    energy = (
        s_dd
        - 2.0 * alpha0 * s_de
        + alpha0 * alpha0 * s_ee
        + 2.0 * beta0 * (s_dq - alpha0 * s_eq)
        + beta0 * beta0 * s_pq
    )
    block_image = apply_blocks(own, east, south, lifted1, grid)
    alpha1 = inner1 / (energy + dot_blocks(lifted1, 2.0 * r_x + block_image))
    coarse2 = coarse1 - alpha1 * (r_x + block_image)
    solved = coarse_solve(coarse2, names, position[0], parts)
    lifted_blocks[...] = lookup(solved, names)
    rise_1[...] = prolong_plane(lookup(solved, here), rows)
    write_scalars(scalars, [alpha0, alpha1, inner1])

    operator = Operator(w_layer, w_row, w_col)
    for layer in range(layers):
        after = resid0[layer] - alpha0 * image0[layer]
        resid[layer] = after
        direction[layer] = inverse[layer] * after + rise_0[...] + beta0 * direction0[layer]
    zero = jnp.zeros((8, LANES), jnp.float32)
    folds = [jnp.zeros((grid[2], 8, LANES), jnp.float32) for _ in range(6)]
    s_rz = s_rd = s_zu = s_zq = s_pq = s_du = s_dq = s_us = s_uw = s_qw = zero
    s_dd = s_ds = s_dw = s_ss = s_sw = s_ww = zero
    for layer, plane in operator.wide(lambda k: direction[k]):
        image[layer] = plane
        after = resid[layer] - alpha1 * plane
        resid[layer] = after
        part = inverse[layer] * after
        scaled[layer] = part
        up = part + rise_1[...]
        lifted[layer] = up
        weighted = inverse[layer] * plane
        scaled_image[layer] = weighted
        q, r, d, z, w, p = near(plane), near(after), near(part), near(up), near(weighted), near(direction[layer])
        s_rz += tally(r * z)
        s_rd += tally(r * d)
        s_zq += tally(z * q)
        s_pq += tally(p * q)
        s_dq += tally(d * q)
        s_qw += tally(q * w)
        folds[1] += fold_rows(q)
        folds[5] += fold_rows(r)
    for layer, plane in operator.wide(lambda k: lifted[k]):
        lifted_image[layer] = plane
        part = inverse[layer] * plane
        scaled_lifted[layer] = part
        u, s = near(plane), near(part)
        s_zu += tally(u * near(lifted[layer]))
        s_du += tally(u * near(scaled[layer]))
        s_us += tally(u * s)
        s_uw += tally(u * near(scaled_image[layer]))
        folds[0] += fold_rows(u)
    for layer, image_d in operator.near(lambda k: scaled[k]):
        s_dd += tally(image_d * near(scaled[layer]))
        s_ds += tally(image_d * near(scaled_lifted[layer]))
        s_dw += tally(image_d * near(scaled_image[layer]))
        folds[2] += fold_rows(image_d)
    for layer, image_s in operator.near(lambda k: scaled_lifted[k]):
        s_ss += tally(image_s * near(scaled_lifted[layer]))
        s_sw += tally(image_s * near(scaled_image[layer]))
        folds[3] += fold_rows(image_s)
    for layer, image_w in operator.near(lambda k: scaled_image[k]):
        s_ww += tally(image_w * near(scaled_image[layer]))
        folds[4] += fold_rows(image_w)
    lines = [fold.sum(axis=1) for fold in folds]
    upper = pack_blocks(lines[:4])
    lower = pack_blocks(lines[4:]) + pack_scalars(
        [s_rz, s_rd, s_zu, s_zq, s_pq, s_du, s_dq, s_us, s_uw, s_qw, s_dd, s_ds, s_dw, s_ss, s_sw, s_ww],
        2 * width,
    )
    write_message(message, upper, lower)


def last_kernel(grid, position, arrived0, before, arrived, names_ref, scalars, lifted2_ref, *rest):
    parts = rest[:8]
    resid, lifted, direction1, image1, lifted_image, direction0, inverse, w_layer, w_row, w_col = rest[8:18]
    answer, out_resid = rest[18:20]
    direction, rise_3 = rest[20:]
    width = grid[2] * grid[3]
    layers, rows, _ = resid.shape
    names = unfold(arrived0[...], 1, width).astype(jnp.int32)
    here = names_ref[...].astype(jnp.int32)
    blocks = received(before, 1)
    own, east, south = [unfold(blocks, k, width) for k in range(3)]
    upper, lower = received(arrived, 0), received(arrived, 1)
    r_u, r_q, r_d, r_s = [unfold(upper, k, width) for k in range(4)]
    r_w, r_r = [unfold(lower, k, width) for k in range(2)]
    (s_rz, s_rd, s_zu, s_zq, s_pq, s_du, s_dq, s_us, s_uw, s_qw, s_dd, s_ds, s_dw, s_ss, s_sw, s_ww) = [
        lane_total(lower, 2 * width + k) for k in range(16)
    ]
    alpha0, alpha1, inner1 = [scalars[0:1, k : k + 1] for k in range(3)]
    inner2 = s_rz
    beta1 = inner2 / inner1
    alpha2 = inner2 / (s_zu + 2.0 * beta1 * s_zq + beta1 * beta1 * s_pq)
    coarse3 = r_r - alpha2 * (r_u + beta1 * r_q)
    solved = coarse_solve(coarse3, names, position[0], parts)
    lifted3 = lookup(solved, names)
    rise_3[...] = prolong_plane(lookup(solved, here), rows)
    scaled_sum = (
        s_rd
        - 2.0 * alpha2 * (s_du + beta1 * s_dq)
        + alpha2 * alpha2 * (s_us + 2.0 * beta1 * s_uw + beta1 * beta1 * s_qw)
    )
    inner3 = scaled_sum + dot_blocks(coarse3, lifted3)
    beta2 = inner3 / inner2
    rise = lifted3 + beta2 * lifted2_ref[...]
    k_d, k_s, k_w, k_p = 1.0 + beta2, -alpha2, -alpha2 * beta1, beta2 * beta1
    energy = (
        k_d * k_d * s_dd
        + k_s * k_s * s_ss
        + k_w * k_w * s_ww
        + k_p * k_p * s_pq
        + 2.0 * (k_d * (k_s * s_ds + k_w * s_dw + k_p * s_dq) + k_s * (k_w * s_sw + k_p * s_uw) + k_w * k_p * s_qw)
    )
    r_x = k_d * r_d + k_s * r_s + k_w * r_w + k_p * r_q
    block_image = apply_blocks(own, east, south, rise, grid)
    alpha3 = inner3 / (energy + dot_blocks(rise, 2.0 * r_x + block_image))

    for layer in range(layers):
        direction2 = lifted[layer] + beta1 * direction1[layer]
        after = resid[layer] - alpha2 * (lifted_image[layer] + beta1 * image1[layer])
        step = inverse[layer] * after + rise_3[...] + beta2 * direction2
        direction[layer] = step
        out_resid[layer] = near(after)
        answer[layer] = (
            alpha0 * near(direction0[layer])
            + alpha1 * near(direction1[layer])
            + alpha2 * near(direction2)
            + alpha3 * near(step)
        )
    for layer, plane in Operator(w_layer, w_row, w_col).near(lambda k: direction[k]):
        out_resid[layer] = out_resid[layer] - alpha3 * plane


def call(kernel, outs, scratch, name, smem, *operands, spaces=None):
    whole = pl.BlockSpec(memory_space=pltpu.VMEM)
    scalar = pl.BlockSpec(memory_space=pltpu.SMEM)
    specs = [scalar] * smem + [whole] * (len(operands) - smem)
    operands = list(operands)
    for index in spaces or ():
        specs[index] = pl.BlockSpec(memory_space=pltpu.HBM)
        operands[index] = pltpu.with_memory_space_constraint(operands[index], pltpu.HBM)
    return pl.pallas_call(
        kernel,
        out_shape=[jax.ShapeDtypeStruct(shape, jnp.float32) for shape in outs],
        in_specs=specs,
        out_specs=[whole] * len(outs),
        scratch_shapes=[pltpu.VMEM(s, jnp.float32) if isinstance(s, tuple) else s for s in scratch],
        compiler_params=pltpu.CompilerParams(vmem_limit_bytes=20 * 1024 * 1024),
        name=name,
    )(*operands)


def exchange(message):
    return lax.all_to_all(message, BOTH, 0, 0, tiled=True)


def pair(values, axis, mask):
    return lax.ppermute(values, axis, [(i, i ^ mask) for i in range(lax.axis_size(axis))])


def pair_far(values, axis):
    count = lax.axis_size(axis)
    return lax.ppermute(values, axis, [(i, i + 1 if i % 2 else i - 1) for i in range(1, count - 1)])


def local_steps(loading, viscosity, aggregate, coarse_inverse):
    layers, cells_x, cells_y = loading.shape
    blocks_x, blocks_y = aggregate.shape
    count_x, count_y = lax.axis_size("rows"), lax.axis_size("cols")
    devices = count_x * count_y
    grid = (count_x, count_y, blocks_x, blocks_y)
    position = jnp.stack([lax.axis_index(axis).astype(jnp.int32) for axis in BOTH])
    tall = cells_x + 2 * HALO
    edge = (2 * layers + 1, HALO, LANES)
    shard = coarse_inverse.T
    parts = [pair(shard, "rows", mask) for mask in (2, 4, 6)]
    loading, viscosity, ids, near_rows, far_rows, shard, message0 = call(
        rows_kernel,
        [loading.shape, viscosity.shape, (8, LANES), edge, edge, shard.shape, (devices, LANES)],
        [pltpu.SMEM(aggregate.shape, jnp.int32), pltpu.SemaphoreType.DMA((4,))],
        "rows",
        1,
        position,
        aggregate,
        loading,
        viscosity,
        shard,
        spaces=(1, 2, 3, 4),
    )
    own = (position, loading, viscosity, ids)
    near_rows, far_rows = pair(near_rows, "rows", 1), pair_far(far_rows, "rows")
    parts = [shard] + parts
    parts = [part for both in ((part, pair(part, "rows", 1)) for part in parts) for part in both]
    parts, far_rows = lax.optimization_barrier((parts, far_rows))
    near_cols, far_cols = call(edge_kernel, [(tall, LANES)] * 2, [], "edges", 1, *own, near_rows, far_rows)
    near_cols, far_cols = pair(near_cols, "cols", 1), pair_far(far_cols, "cols")
    arrived0 = exchange(message0)
    field = (layers, tall, 2 * LANES)
    taller = (layers + 1, tall, 2 * LANES)
    plane = (tall, 2 * LANES)
    message = (2 * devices, LANES)
    line = (8, LANES)
    resid, direction0, image0, inverse, w_layer, w_row, w_col, names, message1 = call(
        start_kernel,
        [field] * 4 + [taller, field, field, line, message],
        [field, plane, field, field, plane],
        "start",
        1,
        *own,
        near_rows,
        far_rows,
        near_cols,
        far_cols,
        arrived0,
        *parts,
    )
    weights = (inverse, w_layer, w_row, w_col)
    arrived1 = exchange(message1)
    resid, lifted, direction1, image1, lifted_image, scalars, lifted_blocks, message2 = call(
        lambda *refs: middle_kernel(grid, *refs),
        [field] * 5 + [line, line, message],
        [field] * 3 + [plane] * 2,
        "middle",
        1,
        position,
        arrived0,
        arrived1,
        names,
        *parts,
        resid,
        direction0,
        image0,
        *weights,
    )
    arrived2 = exchange(message2)
    return call(
        lambda *refs: last_kernel(grid, *refs),
        [loading.shape] * 2,
        [field, plane],
        "last",
        1,
        position,
        arrived0,
        arrived1,
        arrived2,
        names,
        scalars,
        lifted_blocks,
        *parts,
        resid,
        lifted,
        direction1,
        image1,
        lifted_image,
        direction0,
        *weights,
    )


def from_sides(block, axis, dim, width):
    count = lax.axis_size(axis)
    forward = [(i, i + 1) for i in range(count - 1)]
    backward = [(target, source) for source, target in forward]
    size = block.shape[dim]
    low = lax.ppermute(lax.slice_in_dim(block, size - width, size, axis=dim), axis, forward)
    high = lax.ppermute(lax.slice_in_dim(block, 0, width, axis=dim), axis, backward)
    return low, high


def widened(block, width_x, width_y):
    low, high = from_sides(block, "rows", block.ndim - 2, width_x)
    block = jnp.concatenate([low, block, high], axis=-2)
    turned = jnp.swapaxes(block, -1, -2)
    low, high = from_sides(turned, "cols", turned.ndim - 2, width_y)
    low, high = jnp.swapaxes(low, -1, -2), jnp.swapaxes(high, -1, -2)
    return jnp.concatenate([low, block, high], axis=-1)


def all_sum(values):
    count = lax.axis_size("rows") * lax.axis_size("cols")
    if count > 64:
        return lax.psum(lax.psum(values, "cols"), "rows")
    spread = jnp.broadcast_to(values[None], (count,) + values.shape)
    return lax.all_to_all(spread, BOTH, 0, 0).sum(axis=0)


def shifted(field, axis, step):
    return jnp.roll(field, step, axis=axis)


def local_general(loading, viscosity, aggregate, coarse_inverse):
    layers, cells_x, cells_y = loading.shape
    blocks_x, blocks_y = aggregate.shape
    ids = jnp.arange(COARSE, dtype=jnp.int32)
    whole_matrix = lax.all_gather(coarse_inverse, "rows", axis=1, tiled=True)
    fields = widened(jnp.stack([loading, viscosity]), HALO, HALO)
    wide_aggregate = widened(aggregate + 1, 1, 1) - 1
    table = (aggregate.reshape(-1)[:, None] == ids[None, :]).astype(jnp.float32)
    wide_table = (wide_aggregate.reshape(-1)[:, None] == ids[None, :]).astype(jnp.float32)

    residual, visc = fields[0], fields[1]
    inside = visc > 0.0
    pads = ((1, 1), (0, 0), (0, 0))
    padded = jnp.pad(visc, pads)
    weights = [
        0.5 * (visc + padded[:-2]),
        0.5 * (visc + padded[2:]),
        0.5 * (visc + shifted(visc, 1, 1)),
        0.5 * (visc + shifted(visc, 1, -1)),
        0.5 * (visc + shifted(visc, 2, 1)),
        0.5 * (visc + shifted(visc, 2, -1)),
    ]
    diagonal = MASS_TERM + sum(weights)
    inverse = jnp.where(inside, 1.0 / diagonal, 0.0)

    def operate(field):
        layered = jnp.pad(field, pads)
        sides = [
            layered[:-2],
            layered[2:],
            shifted(field, 1, 1),
            shifted(field, 1, -1),
            shifted(field, 2, 1),
            shifted(field, 2, -1),
        ]
        total = MASS_TERM * field
        for weight, side in zip(weights, sides):
            total = total + weight * (field - side)
        return total

    def inner_part(field):
        return field[:, HALO:-HALO, HALO:-HALO]

    def restrict(field):
        blocks = field.reshape(layers, blocks_x, BLOCK, blocks_y, BLOCK).sum(axis=(0, 2, 4))
        return jnp.dot(blocks.reshape(-1), table, precision=PRECISE).reshape(4, COARSE // 4)

    def prolong(values):
        per_block = jnp.dot(wide_table, values.reshape(-1), precision=PRECISE)
        per_block = per_block.reshape(blocks_x + 2, blocks_y + 2)
        spread = jnp.repeat(jnp.repeat(per_block, BLOCK, axis=0), BLOCK, axis=1)
        cut = BLOCK - HALO
        return spread[cut:-cut, cut:-cut][None]

    def coarse_apply(coarse):
        return jnp.dot(whole_matrix, coarse.reshape(-1), precision=PRECISE).reshape(coarse.shape)

    def scalars(*values):
        return jnp.stack([jnp.broadcast_to(v, (COARSE // 4,)) for v in values])

    coarse = all_sum(restrict(loading))
    lifted = coarse_apply(coarse)
    direction = inverse * residual + prolong(lifted)
    answer = jnp.zeros_like(loading)
    scaled_sum = inner_now = None
    for iteration in range(ITERS):
        image = operate(direction)
        near_image, near_scaled = inner_part(image), inner_part(inverse * image)
        near_direction, near_residual = inner_part(direction), inner_part(residual)
        packed = jnp.concatenate(
            [
                restrict(near_image),
                scalars(
                    jnp.sum(near_direction * near_image),
                    jnp.sum(near_residual * near_scaled),
                    jnp.sum(near_image * near_scaled),
                    jnp.sum(near_residual * inner_part(inverse) * near_residual),
                ),
            ]
        )
        packed = all_sum(packed)
        curvature, cross, square = packed[4, 0], packed[5, 0], packed[6, 0]
        if scaled_sum is None:
            scaled_sum = packed[7, 0]
            inner_now = scaled_sum + jnp.sum(coarse * lifted)
        alpha = inner_now / curvature
        answer = answer + alpha * near_direction
        residual = residual - alpha * image
        if iteration + 1 < ITERS:
            coarse = coarse - alpha * packed[:4]
            scaled_sum = scaled_sum - 2.0 * alpha * cross + alpha * alpha * square
            lifted = coarse_apply(coarse)
            inner_next = scaled_sum + jnp.sum(coarse * lifted)
            direction = inverse * residual + prolong(lifted) + inner_next / inner_now * direction
            inner_now = inner_next
    return answer, inner_part(residual)


def solution(mesh):
    in_specs = (
        P(None, "rows", "cols"),
        P(None, "rows", "cols"),
        P("rows", "cols"),
        P(None, "rows"),
    )
    out_specs = (P(None, "rows", "cols"), P(None, "rows", "cols"))
    body = local_steps if (mesh.shape["rows"], mesh.shape["cols"]) == (8, 4) else local_general
    return jax.shard_map(body, mesh=mesh, in_specs=in_specs, out_specs=out_specs, check_vma=False)
```

```python
import jax
import jax.numpy as jnp
from jax import lax
from jax.experimental import pallas as pl
from jax.experimental.pallas import tpu as pltpu
from jax.sharding import PartitionSpec as P

BLOCK = 16
COARSE = 512
ITERS = 4
HALO = 8
SIDE = 7
LANES = 128
PART = 64

MASS_TERM = 1.0
PRECISE = lax.Precision.HIGHEST
BOTH = ("rows", "cols")


def iota(shape, dim):
    return lax.broadcasted_iota(jnp.int32, shape, dim)


def roll(x, shift, axis):
    size = x.shape[axis]
    shift = shift % size
    return x if shift == 0 else pltpu.roll(x, shift, axis)


def lane_row():
    return iota((1, LANES), 1)


def pick_lanes(values, index):
    return jnp.take_along_axis(values, index, axis=1, mode="promise_in_bounds")


def fold_rows(plane):
    rows = plane.shape[0]
    return plane.reshape(rows // BLOCK, 2, 8, LANES).sum(axis=1)


def pack_blocks(folds):
    count = folds[0].shape[0]
    pad = (-count * len(folds)) % 8
    stacked = jnp.concatenate(folds + ([jnp.zeros((pad, LANES), jnp.float32)] if pad else []), axis=0)
    spread = iota((LANES, LANES), 0) // BLOCK == iota((LANES, LANES), 1) % (LANES // BLOCK)
    summed = jnp.dot(stacked, spread.astype(jnp.float32), precision=PRECISE)
    group = lane_row() // (LANES // BLOCK)
    row = jnp.zeros((1, LANES), jnp.float32)
    for index in range(len(folds) * count):
        row = row + jnp.where(group == index, summed[index : index + 1], 0.0)
    return row


def pack_scalars(partials, offset):
    lane = lane_row()
    row = jnp.zeros((1, LANES), jnp.float32)
    for index, partial in enumerate(partials):
        total = jnp.sum(jnp.sum(partial, axis=0, keepdims=True), axis=1, keepdims=True)
        row = row + jnp.where(lane == offset + index, total, 0.0)
    return row


def unfold(values, slot, width):
    devices = values.shape[0]
    lane = iota((devices, LANES), 1)
    part = jnp.where(lane < width, roll(values, -slot * width, 1), 0.0)
    step = width
    while step < LANES:
        part = part + roll(part, step, 1)
        step *= 2
    per_row = LANES // width
    own = jnp.where(iota((devices, LANES), 0) % per_row == lane // width, part, 0.0)
    rows = [
        jnp.sum(own[k * per_row : (k + 1) * per_row], axis=0, keepdims=True) for k in range(devices // per_row)
    ]
    return jnp.concatenate(rows, axis=0)


def coarse_solve(values, names, position, parts):
    line = jnp.zeros((8, COARSE), jnp.float32)
    for part, ref in enumerate(parts):
        aggregate = iota((PART, LANES), 0) + ((position ^ part) * PART + 1)
        total = jnp.zeros((PART, LANES), jnp.float32)
        for row in range(8):
            total = total + jnp.where(aggregate == names[row : row + 1], values[row : row + 1], 0.0)
        column = jnp.sum(total, axis=1, keepdims=True)
        line = line + (ref[...] * column).reshape(PART // 8, 8, COARSE).sum(axis=0)
    line = jnp.broadcast_to(jnp.sum(line, axis=0, keepdims=True), (8, COARSE))
    return [line[:, t * LANES : (t + 1) * LANES] for t in range(COARSE // LANES)]


def lookup(coarse, names):
    index = jnp.maximum(names - 1, 0)
    inner = index % LANES
    result = jnp.zeros(names.shape, jnp.float32)
    for tile, values in enumerate(coarse):
        result = jnp.where(index // LANES == tile, pick_lanes(values, inner), result)
    return jnp.where(names > 0, result, 0.0)


def apply_blocks(own, east, south, values, grid):
    count_x, count_y, blocks_x, blocks_y = grid
    width = blocks_x * blocks_y
    lane = iota(values.shape, 1)
    row, col = iota(values.shape, 0), lane // width
    at_x, at_y = (lane % width) // blocks_y, lane % blocks_y
    last_x, last_y = at_x == blocks_x - 1, at_y == blocks_y - 1
    step_e = width - (blocks_y - 1)
    step_s = (blocks_x - 1) * blocks_y

    def take(x, inner, outer, is_outer, missing):
        return jnp.where(missing, 0.0, jnp.where(is_outer, outer(x), inner(x)))

    from_e = take(
        values, lambda x: roll(x, -1, 1), lambda x: roll(x, -step_e, 1), last_y, last_y & (col == count_y - 1)
    )
    from_w = take(
        east * values, lambda x: roll(x, 1, 1), lambda x: roll(x, step_e, 1), at_y == 0, (at_y == 0) & (col == 0)
    )
    from_s = take(
        values,
        lambda x: roll(x, -blocks_y, 1),
        lambda x: roll(roll(x, -1, 0), step_s, 1),
        last_x,
        last_x & (row == count_x - 1),
    )
    from_n = take(
        south * values,
        lambda x: roll(x, blocks_y, 1),
        lambda x: roll(roll(x, 1, 0), -step_s, 1),
        at_x == 0,
        (at_x == 0) & (row == 0),
    )
    return own * values - east * from_e - south * from_s - from_w - from_n


def local_names(ids):
    rows = ids.shape[0]
    lane = iota((8, LANES), 1)
    at = lane % BLOCK
    starts = [0] + list(range(HALO, rows, BLOCK))
    result = jnp.zeros((8, LANES), jnp.float32)
    for index, start in enumerate(starts):
        main = ids[start : start + 8, :LANES]
        side = ids[start : start + 8, LANES:]
        inner = pick_lanes(main, (at * BLOCK) % LANES)
        outer = pick_lanes(side, jnp.where(at == 8, 0, LANES - 1))
        both = jnp.where(at < 8, inner, jnp.where(at < 10, outer, 0.0))
        result = jnp.where(lane // BLOCK == index, both, result)
    return result


def prolong_plane(values, rows):
    lane = iota((8, LANES), 1)
    bounds = [0] + list(range(HALO, rows, BLOCK)) + [rows]
    pieces = []
    for index in range(len(bounds) - 1):
        main = pick_lanes(values, lane // BLOCK + index * BLOCK)
        side = pick_lanes(values, jnp.where(lane < BLOCK, 8, 9) + index * BLOCK)
        line = jnp.concatenate([main, side], axis=1)
        pieces += [line] * ((bounds[index + 1] - bounds[index]) // 8)
    return jnp.concatenate(pieces, axis=0)


class Operator:
    def __init__(self, w_layer, w_row, w_col):
        self.w_layer, self.w_row, self.w_col = w_layer, w_row, w_col

    def wide(self, source):
        layers = self.w_row.shape[0]
        current = source(0)
        below = self.w_layer[0] * current
        for layer in range(layers):
            after = source(layer + 1) if layer + 1 < layers else None
            above = self.w_layer[layer + 1] * (current - after if after is not None else current)
            total = MASS_TERM * current + above
            total = total + below if layer == 0 else total - below
            flux = self.w_row[layer] * (current - roll(current, -1, 0))
            total = total + flux - roll(flux, 1, 0)
            flux = self.w_col[layer] * (current - roll(current, -1, 1))
            total = total + flux - roll(flux, 1, 1)
            yield layer, total
            current, below = after, above

    def near(self, source):
        layers, rows = self.w_row.shape[:2]
        inner = slice(HALO, rows - HALO)
        plane = source(0)
        current = near(plane)
        below = self.w_layer[0, inner, :LANES] * current
        for layer in range(layers):
            following = source(layer + 1) if layer + 1 < layers else None
            after = near(following) if following is not None else None
            above = self.w_layer[layer + 1, inner, :LANES] * (current - after if after is not None else current)
            total = MASS_TERM * current + above
            total = total + below if layer == 0 else total - below
            column = plane[:, :LANES]
            flux = self.w_row[layer, :, :LANES] * (column - roll(column, -1, 0))
            total = total + (flux - roll(flux, 1, 0))[HALO:-HALO]
            band = plane[HALO:-HALO]
            flux = self.w_col[layer, inner, :] * (band - roll(band, -1, 1))
            total = total + (flux - roll(flux, 1, 1))[:, :LANES]
            yield layer, total
            plane, current, below = following, after, above


def near(plane):
    return plane[HALO:-HALO, :LANES]


def tally(plane):
    return plane.reshape(plane.shape[0] // 8, 8, LANES).sum(axis=0)


def own_ids(ids):
    blocks_x = ids.shape[0] // 2
    lines = [jnp.broadcast_to(ids[bx : bx + 1], (BLOCK, LANES)) for bx in range(blocks_x)]
    return jnp.concatenate(lines, axis=0)


def rows_kernel(
    position, aggregate_hbm, loading_hbm, viscosity_hbm, shard_hbm,
    loading, viscosity, ids, near_rows, far_rows, shard, message,
    aggregate, sems,
):
    layers, rows, _ = loading.shape
    odd = position[0] % 2
    copies = [
        pltpu.make_async_copy(aggregate_hbm, aggregate, sems.at[0]),
        pltpu.make_async_copy(loading_hbm, loading, sems.at[1]),
        pltpu.make_async_copy(viscosity_hbm, viscosity, sems.at[2]),
        pltpu.make_async_copy(shard_hbm, shard, sems.at[3]),
    ]
    for copy in copies:
        copy.start()
    copies[0].wait()
    blocks_x, blocks_y = aggregate.shape
    lane = lane_row()
    flat = jnp.zeros((1, LANES), jnp.float32)
    for bx in range(blocks_x):
        names = jnp.zeros((1, LANES), jnp.float32)
        for by in range(blocks_y):
            name = (aggregate[bx, by] + 1).astype(jnp.float32)
            names = jnp.where(lane // BLOCK == by, name, names)
            flat = jnp.where(lane % (blocks_x * blocks_y) == bx * blocks_y + by, name, flat)
        ids[bx : bx + 1] = names
    ids[blocks_x:] = jnp.broadcast_to(flat, (ids.shape[0] - blocks_x, LANES))
    first, last = ids[0:1], ids[blocks_x - 1 : blocks_x]
    near_rows[2 * layers] = jnp.broadcast_to(jnp.where(odd == 1, first, last), (HALO, LANES))
    far_rows[2 * layers] = jnp.broadcast_to(jnp.where(odd == 1, last, first), (HALO, LANES))
    near_at = pl.multiple_of((1 - odd) * (rows - HALO), HALO)
    far_at = pl.multiple_of(odd * (rows - HALO), HALO)
    for k, (copy, source) in enumerate(zip(copies[1:3], (loading, viscosity))):
        copy.wait()
        near_rows[k * layers : (k + 1) * layers] = source[:, pl.ds(near_at, HALO), :]
        far_rows[k * layers : (k + 1) * layers] = source[:, pl.ds(far_at, HALO), :]
    fold = jnp.zeros((blocks_x, 8, LANES), jnp.float32)
    for layer in range(layers):
        fold = fold + fold_rows(loading[layer])
    width = blocks_x * blocks_y
    line = pack_blocks([fold.sum(axis=1)]) + jnp.where((lane >= width) & (lane < 2 * width), flat, 0.0)
    message[...] = jnp.broadcast_to(line, message.shape)
    copies[3].wait()


def tall_plane(slot, own, odd, near_rows, far_rows):
    low = jnp.where(odd == 1, near_rows[slot], far_rows[slot])
    high = jnp.where(odd == 1, far_rows[slot], near_rows[slot])
    return jnp.concatenate([low, own, high], axis=0)


def edge_kernel(position, loading, viscosity, own_names, near_rows, far_rows, near_cols, far_cols):
    layers = loading.shape[0]
    odd = position[0] % 2
    lane = lane_row()
    right = left = jnp.zeros(near_cols.shape, jnp.float32)
    for slot in range(2 * layers + 1):
        if slot < layers:
            own = loading[slot]
        elif slot < 2 * layers:
            own = viscosity[slot - layers]
        else:
            own = own_ids(own_names)
        plane = tall_plane(slot, own, odd, near_rows, far_rows)
        at = slot * SIDE
        here = (lane >= at) & (lane < at + SIDE)
        right = jnp.where(here, roll(plane, at + SIDE, 1), right)
        left = jnp.where(here, roll(plane, at, 1), left)
    odd_col = position[1] % 2
    near_cols[...] = jnp.where(odd_col == 1, left, right)
    far_cols[...] = jnp.where(odd_col == 1, right, left)


def start_kernel(
    position, loading, viscosity, own_names, near_rows, far_rows, near_cols, far_cols, arrived, *rest
):
    parts = rest[:8]
    resid, direction, image, inverse, w_layer, w_row, w_col, names_out, lifted_blocks, message = rest[8:18]
    wide, ids, scaled, scaled_image, rise = rest[18:]
    layers = loading.shape[0]
    blocks_x, blocks_y = loading.shape[1] // BLOCK, LANES // BLOCK
    width = blocks_x * blocks_y
    odd, odd_col = position[0] % 2, position[1] % 2
    lane = lane_row()
    from_west = jnp.where(odd_col == 1, near_cols[...], far_cols[...])
    from_east = jnp.where(odd_col == 1, far_cols[...], near_cols[...])

    def widen(slot, own):
        at = slot * SIDE
        beyond = jnp.where(lane < SIDE, roll(from_east, -at, 1), 0.0)
        beyond = jnp.where(lane >= LANES - SIDE, roll(from_west, LANES - SIDE - at, 1), beyond)
        return jnp.concatenate([tall_plane(slot, own, odd, near_rows, far_rows), beyond], axis=1)

    for layer in range(layers):
        resid[layer] = widen(layer, loading[layer])
        wide[layer] = widen(layers + layer, viscosity[layer])
    ids[...] = widen(2 * layers, own_ids(own_names))
    names_out[...] = local_names(ids)

    for layer in range(layers):
        visc = wide[layer]
        before = 0.5 * visc if layer == 0 else 0.5 * (visc + wide[layer - 1])
        after = 0.5 * visc if layer == layers - 1 else 0.5 * (visc + wide[layer + 1])
        by_row = 0.5 * (visc + roll(visc, -1, 0))
        by_col = 0.5 * (visc + roll(visc, -1, 1))
        if layer == 0:
            w_layer[0] = before
        w_layer[layer + 1] = after
        w_row[layer] = by_row
        w_col[layer] = by_col
        diagonal = MASS_TERM + before + after + by_row + roll(by_row, 1, 0) + by_col + roll(by_col, 1, 1)
        part = jnp.where(visc > 0.0, 1.0 / diagonal, 0.0)
        inverse[layer] = part
        scaled[layer] = part * resid[layer]
    folds_own, folds_east, folds_south = block_matrix(w_layer, w_row, w_col)

    sums = arrived[...]
    names = unfold(sums, 1, width).astype(jnp.int32)
    solved = coarse_solve(unfold(sums, 0, width), names, position[0], parts)
    lifted_blocks[...] = lookup(solved, names)
    rise[...] = prolong_plane(lookup(solved, names_out[...].astype(jnp.int32)), ids.shape[0])
    for layer in range(layers):
        direction[layer] = scaled[layer] + rise[...]

    operator = Operator(w_layer, w_row, w_col)
    zero = jnp.zeros((8, LANES), jnp.float32)
    folds = [jnp.zeros((blocks_x, 8, LANES), jnp.float32) for _ in range(2)]
    s_rp = s_rd = s_dq = s_eq = s_pq = s_ee = zero
    for layer, plane in operator.wide(lambda k: direction[k]):
        image[layer] = plane
        part = inverse[layer] * plane
        scaled_image[layer] = part
        q, e, d, r, p = near(plane), near(part), near(scaled[layer]), near(resid[layer]), near(direction[layer])
        s_rp += tally(r * p)
        s_rd += tally(r * d)
        s_dq += tally(d * q)
        s_eq += tally(e * q)
        s_pq += tally(p * q)
        folds[0] += fold_rows(q)
    for layer, image_e in operator.near(lambda k: scaled_image[k]):
        s_ee += tally(image_e * near(scaled_image[layer]))
        folds[1] += fold_rows(image_e)
    upper = pack_blocks([fold.sum(axis=1) for fold in folds])
    upper = upper + pack_scalars([s_rp, s_rd, s_dq, s_eq, s_pq, s_ee], 3 * width)
    lower = pack_blocks([folds_own, folds_east, folds_south])
    write_message(message, upper, lower)


def write_message(message, upper, lower):
    rows = iota(message.shape, 0)
    message[...] = jnp.where(rows % 2 == 0, upper, lower)


def block_matrix(w_layer, w_row, w_col):
    layers = w_row.shape[0]
    rows = w_row.shape[1]
    lane = lane_row()
    cols = jnp.zeros((rows, 2 * LANES), jnp.float32)
    line = jnp.zeros((rows, LANES), jnp.float32)
    for layer in range(layers):
        cols = cols + w_col[layer]
        line = line + w_row[layer, :, :LANES]
    ends = near(w_layer[0]) + near(w_layer[layers])
    own_cells = fold_rows(ends).sum(axis=1)
    east_face = fold_rows(jnp.where(lane % BLOCK == BLOCK - 1, near(cols), 0.0)).sum(axis=1)
    west_face = fold_rows(jnp.where(lane % BLOCK == 0, near(roll(cols, 1, 1)), 0.0)).sum(axis=1)
    count = own_cells.shape[0]
    south_face = jnp.concatenate(
        [line[HALO + BLOCK * (k + 1) - 1 : HALO + BLOCK * (k + 1)] for k in range(count)], axis=0
    )
    north_face = jnp.concatenate(
        [line[HALO + BLOCK * k - 1 : HALO + BLOCK * k] for k in range(count)], axis=0
    )
    mass = jnp.full((count, LANES), MASS_TERM * layers * BLOCK, jnp.float32)
    own = mass + own_cells + east_face + west_face + south_face + north_face
    return own, east_face, south_face


def lane_total(values, lane_at):
    return jnp.sum(values[:, lane_at : lane_at + 1], axis=0, keepdims=True)


def dot_blocks(left, right):
    return jnp.sum(jnp.sum(left * right, axis=0, keepdims=True), axis=1, keepdims=True)


def received(ref, parity):
    return ref[pl.ds(parity, ref.shape[0] // 2, stride=2), :]


def write_scalars(ref, values):
    lane = lane_row()
    line = jnp.zeros((1, LANES), jnp.float32)
    for index, value in enumerate(values):
        line = jnp.where(lane == index, value, line)
    ref[...] = jnp.broadcast_to(line, ref.shape)


def middle_kernel(grid, position, arrived0, arrived, names_ref, lifted0_ref, *rest):
    parts = rest[:8]
    resid0, direction0, image0, inverse, w_layer, w_row, w_col = rest[8:15]
    resid, lifted, direction, image, lifted_image, scalars, lifted_blocks, message = rest[15:23]
    scaled, scaled_image, scaled_lifted, rise_0, rise_1 = rest[23:]
    width = grid[2] * grid[3]
    layers, rows, _ = resid.shape
    sums = arrived0[...]
    names = unfold(sums, 1, width).astype(jnp.int32)
    here = names_ref[...].astype(jnp.int32)
    upper, lower = received(arrived, 0), received(arrived, 1)
    s_rp, s_rd, s_dq, s_eq, s_pq, s_ee = [lane_total(upper, 3 * width + k) for k in range(6)]
    r_q, r_e = [unfold(upper, k, width) for k in range(2)]
    own, east, south = [unfold(lower, k, width) for k in range(3)]
    lifted0 = lifted0_ref[...]
    r_d = r_q - apply_blocks(own, east, south, lifted0, grid)
    s_dd = s_dq - dot_blocks(lifted0, r_d)
    s_de = s_eq - dot_blocks(lifted0, r_e)
    alpha0 = s_rp / s_pq
    scaled_sum = s_rd - 2.0 * alpha0 * s_dq + alpha0 * alpha0 * s_eq
    coarse1 = unfold(sums, 0, width) - alpha0 * r_q
    solved = coarse_solve(coarse1, names, position[0], parts)
    lifted1 = lookup(solved, names)
    rise_0[...] = prolong_plane(lookup(solved, here), rows)
    inner1 = scaled_sum + dot_blocks(coarse1, lifted1)
    beta0 = inner1 / s_rp
    r_x = r_d - alpha0 * r_e + beta0 * r_q
    energy = (
        s_dd
        - 2.0 * alpha0 * s_de
        + alpha0 * alpha0 * s_ee
        + 2.0 * beta0 * (s_dq - alpha0 * s_eq)
        + beta0 * beta0 * s_pq
    )
    block_image = apply_blocks(own, east, south, lifted1, grid)
    alpha1 = inner1 / (energy + dot_blocks(lifted1, 2.0 * r_x + block_image))
    coarse2 = coarse1 - alpha1 * (r_x + block_image)
    solved = coarse_solve(coarse2, names, position[0], parts)
    lifted_blocks[...] = lookup(solved, names)
    rise_1[...] = prolong_plane(lookup(solved, here), rows)
    write_scalars(scalars, [alpha0, alpha1, inner1])

    operator = Operator(w_layer, w_row, w_col)
    for layer in range(layers):
        after = resid0[layer] - alpha0 * image0[layer]
        resid[layer] = after
        direction[layer] = inverse[layer] * after + rise_0[...] + beta0 * direction0[layer]
    zero = jnp.zeros((8, LANES), jnp.float32)
    folds = [jnp.zeros((grid[2], 8, LANES), jnp.float32) for _ in range(5)]
    s_rz = s_rd = s_zu = s_zq = s_pq = s_du = s_dq = s_us = s_uw = s_qw = zero
    s_ss = s_sw = s_ww = zero
    for layer, plane in operator.wide(lambda k: direction[k]):
        image[layer] = plane
        after = resid[layer] - alpha1 * plane
        resid[layer] = after
        part = inverse[layer] * after
        scaled[layer] = part
        up = part + rise_1[...]
        lifted[layer] = up
        weighted = inverse[layer] * plane
        scaled_image[layer] = weighted
        q, r, d, z, w, p = near(plane), near(after), near(part), near(up), near(weighted), near(direction[layer])
        s_rz += tally(r * z)
        s_rd += tally(r * d)
        s_zq += tally(z * q)
        s_pq += tally(p * q)
        s_dq += tally(d * q)
        s_qw += tally(q * w)
        folds[1] += fold_rows(q)
        folds[4] += fold_rows(r)
    for layer, plane in operator.wide(lambda k: lifted[k]):
        lifted_image[layer] = plane
        part = inverse[layer] * plane
        scaled_lifted[layer] = part
        u, s = near(plane), near(part)
        s_zu += tally(u * near(lifted[layer]))
        s_du += tally(u * near(scaled[layer]))
        s_us += tally(u * s)
        s_uw += tally(u * near(scaled_image[layer]))
        folds[0] += fold_rows(u)
    for layer, image_s in operator.near(lambda k: scaled_lifted[k]):
        s_ss += tally(image_s * near(scaled_lifted[layer]))
        s_sw += tally(image_s * near(scaled_image[layer]))
        folds[2] += fold_rows(image_s)
    for layer, image_w in operator.near(lambda k: scaled_image[k]):
        s_ww += tally(image_w * near(scaled_image[layer]))
        folds[3] += fold_rows(image_w)
    lines = [fold.sum(axis=1) for fold in folds]
    upper = pack_blocks(lines[:4])
    lower = pack_blocks(lines[4:]) + pack_scalars(
        [s_rz, s_rd, s_zu, s_zq, s_pq, s_du, s_dq, s_us, s_uw, s_qw, s_ss, s_sw, s_ww],
        width,
    )
    write_message(message, upper, lower)


def last_kernel(grid, position, arrived0, before, arrived, names_ref, scalars, lifted2_ref, *rest):
    parts = rest[:8]
    resid, lifted, direction1, image1, lifted_image, direction0, inverse, w_layer, w_row, w_col = rest[8:18]
    answer, out_resid = rest[18:20]
    direction, rise_3 = rest[20:]
    width = grid[2] * grid[3]
    layers, rows, _ = resid.shape
    names = unfold(arrived0[...], 1, width).astype(jnp.int32)
    here = names_ref[...].astype(jnp.int32)
    blocks = received(before, 1)
    own, east, south = [unfold(blocks, k, width) for k in range(3)]
    upper, lower = received(arrived, 0), received(arrived, 1)
    r_u, r_q, r_s, r_w = [unfold(upper, k, width) for k in range(4)]
    r_r = unfold(lower, 0, width)
    s_rz, s_rd, s_zu, s_zq, s_pq, s_du, s_dq, s_us, s_uw, s_qw, s_ss, s_sw, s_ww = [
        lane_total(lower, width + k) for k in range(13)
    ]
    lifted2 = lifted2_ref[...]
    r_d = r_u - apply_blocks(own, east, south, lifted2, grid)
    s_dd = s_du - dot_blocks(lifted2, r_d)
    s_ds = s_us - dot_blocks(lifted2, r_s)
    s_dw = s_uw - dot_blocks(lifted2, r_w)
    alpha0, alpha1, inner1 = [scalars[0:1, k : k + 1] for k in range(3)]
    inner2 = s_rz
    beta1 = inner2 / inner1
    alpha2 = inner2 / (s_zu + 2.0 * beta1 * s_zq + beta1 * beta1 * s_pq)
    coarse3 = r_r - alpha2 * (r_u + beta1 * r_q)
    solved = coarse_solve(coarse3, names, position[0], parts)
    lifted3 = lookup(solved, names)
    rise_3[...] = prolong_plane(lookup(solved, here), rows)
    scaled_sum = (
        s_rd
        - 2.0 * alpha2 * (s_du + beta1 * s_dq)
        + alpha2 * alpha2 * (s_us + 2.0 * beta1 * s_uw + beta1 * beta1 * s_qw)
    )
    inner3 = scaled_sum + dot_blocks(coarse3, lifted3)
    beta2 = inner3 / inner2
    rise = lifted3 + beta2 * lifted2
    k_d, k_s, k_w, k_p = 1.0 + beta2, -alpha2, -alpha2 * beta1, beta2 * beta1
    energy = (
        k_d * k_d * s_dd
        + k_s * k_s * s_ss
        + k_w * k_w * s_ww
        + k_p * k_p * s_pq
        + 2.0 * (k_d * (k_s * s_ds + k_w * s_dw + k_p * s_dq) + k_s * (k_w * s_sw + k_p * s_uw) + k_w * k_p * s_qw)
    )
    r_x = k_d * r_d + k_s * r_s + k_w * r_w + k_p * r_q
    block_image = apply_blocks(own, east, south, rise, grid)
    alpha3 = inner3 / (energy + dot_blocks(rise, 2.0 * r_x + block_image))

    for layer in range(layers):
        direction2 = lifted[layer] + beta1 * direction1[layer]
        after = resid[layer] - alpha2 * (lifted_image[layer] + beta1 * image1[layer])
        step = inverse[layer] * after + rise_3[...] + beta2 * direction2
        direction[layer] = step
        out_resid[layer] = near(after)
        answer[layer] = (
            alpha0 * near(direction0[layer])
            + alpha1 * near(direction1[layer])
            + alpha2 * near(direction2)
            + alpha3 * near(step)
        )
    for layer, plane in Operator(w_layer, w_row, w_col).near(lambda k: direction[k]):
        out_resid[layer] = out_resid[layer] - alpha3 * plane


def call(kernel, outs, scratch, name, smem, *operands, spaces=None):
    whole = pl.BlockSpec(memory_space=pltpu.VMEM)
    scalar = pl.BlockSpec(memory_space=pltpu.SMEM)
    specs = [scalar] * smem + [whole] * (len(operands) - smem)
    operands = list(operands)
    for index in spaces or ():
        specs[index] = pl.BlockSpec(memory_space=pltpu.HBM)
        operands[index] = pltpu.with_memory_space_constraint(operands[index], pltpu.HBM)
    return pl.pallas_call(
        kernel,
        out_shape=[jax.ShapeDtypeStruct(shape, jnp.float32) for shape in outs],
        in_specs=specs,
        out_specs=[whole] * len(outs),
        scratch_shapes=[pltpu.VMEM(s, jnp.float32) if isinstance(s, tuple) else s for s in scratch],
        compiler_params=pltpu.CompilerParams(vmem_limit_bytes=20 * 1024 * 1024),
        name=name,
    )(*operands)


def exchange(message):
    return lax.all_to_all(message, BOTH, 0, 0, tiled=True)


def pair(values, axis, mask):
    return lax.ppermute(values, axis, [(i, i ^ mask) for i in range(lax.axis_size(axis))])


def pair_far(values, axis):
    count = lax.axis_size(axis)
    return lax.ppermute(values, axis, [(i, i + 1 if i % 2 else i - 1) for i in range(1, count - 1)])


def local_steps(loading, viscosity, aggregate, coarse_inverse):
    layers, cells_x, cells_y = loading.shape
    blocks_x, blocks_y = aggregate.shape
    count_x, count_y = lax.axis_size("rows"), lax.axis_size("cols")
    devices = count_x * count_y
    grid = (count_x, count_y, blocks_x, blocks_y)
    position = jnp.stack([lax.axis_index(axis).astype(jnp.int32) for axis in BOTH])
    tall = cells_x + 2 * HALO
    edge = (2 * layers + 1, HALO, LANES)
    shard = coarse_inverse.T
    parts = [pair(shard, "rows", mask) for mask in (2, 4, 6)]
    loading, viscosity, ids, near_rows, far_rows, shard, message0 = call(
        rows_kernel,
        [loading.shape, viscosity.shape, (8, LANES), edge, edge, shard.shape, (devices, LANES)],
        [pltpu.SMEM(aggregate.shape, jnp.int32), pltpu.SemaphoreType.DMA((4,))],
        "rows",
        1,
        position,
        aggregate,
        loading,
        viscosity,
        shard,
        spaces=(1, 2, 3, 4),
    )
    own = (position, loading, viscosity, ids)
    near_rows, far_rows = pair(near_rows, "rows", 1), pair_far(far_rows, "rows")
    parts = [shard] + parts
    parts = [part for both in ((part, pair(part, "rows", 1)) for part in parts) for part in both]
    parts, far_rows = lax.optimization_barrier((parts, far_rows))
    near_cols, far_cols = call(edge_kernel, [(tall, LANES)] * 2, [], "edges", 1, *own, near_rows, far_rows)
    near_cols, far_cols = pair(near_cols, "cols", 1), pair_far(far_cols, "cols")
    arrived0 = exchange(message0)
    field = (layers, tall, 2 * LANES)
    taller = (layers + 1, tall, 2 * LANES)
    plane = (tall, 2 * LANES)
    message = (2 * devices, LANES)
    line = (8, LANES)
    resid, direction0, image0, inverse, w_layer, w_row, w_col, names, lifted_blocks, message1 = call(
        start_kernel,
        [field] * 4 + [taller, field, field, line, line, message],
        [field, plane, field, field, plane],
        "start",
        1,
        *own,
        near_rows,
        far_rows,
        near_cols,
        far_cols,
        arrived0,
        *parts,
    )
    weights = (inverse, w_layer, w_row, w_col)
    arrived1 = exchange(message1)
    resid, lifted, direction1, image1, lifted_image, scalars, lifted_blocks, message2 = call(
        lambda *refs: middle_kernel(grid, *refs),
        [field] * 5 + [line, line, message],
        [field] * 3 + [plane] * 2,
        "middle",
        1,
        position,
        arrived0,
        arrived1,
        names,
        lifted_blocks,
        *parts,
        resid,
        direction0,
        image0,
        *weights,
    )
    arrived2 = exchange(message2)
    return call(
        lambda *refs: last_kernel(grid, *refs),
        [loading.shape] * 2,
        [field, plane],
        "last",
        1,
        position,
        arrived0,
        arrived1,
        arrived2,
        names,
        scalars,
        lifted_blocks,
        *parts,
        resid,
        lifted,
        direction1,
        image1,
        lifted_image,
        direction0,
        *weights,
    )


def from_sides(block, axis, dim, width):
    count = lax.axis_size(axis)
    forward = [(i, i + 1) for i in range(count - 1)]
    backward = [(target, source) for source, target in forward]
    size = block.shape[dim]
    low = lax.ppermute(lax.slice_in_dim(block, size - width, size, axis=dim), axis, forward)
    high = lax.ppermute(lax.slice_in_dim(block, 0, width, axis=dim), axis, backward)
    return low, high


def widened(block, width_x, width_y):
    low, high = from_sides(block, "rows", block.ndim - 2, width_x)
    block = jnp.concatenate([low, block, high], axis=-2)
    turned = jnp.swapaxes(block, -1, -2)
    low, high = from_sides(turned, "cols", turned.ndim - 2, width_y)
    low, high = jnp.swapaxes(low, -1, -2), jnp.swapaxes(high, -1, -2)
    return jnp.concatenate([low, block, high], axis=-1)


def all_sum(values):
    count = lax.axis_size("rows") * lax.axis_size("cols")
    if count > 64:
        return lax.psum(lax.psum(values, "cols"), "rows")
    spread = jnp.broadcast_to(values[None], (count,) + values.shape)
    return lax.all_to_all(spread, BOTH, 0, 0).sum(axis=0)


def shifted(field, axis, step):
    return jnp.roll(field, step, axis=axis)


def local_general(loading, viscosity, aggregate, coarse_inverse):
    layers, cells_x, cells_y = loading.shape
    blocks_x, blocks_y = aggregate.shape
    ids = jnp.arange(COARSE, dtype=jnp.int32)
    whole_matrix = lax.all_gather(coarse_inverse, "rows", axis=1, tiled=True)
    fields = widened(jnp.stack([loading, viscosity]), HALO, HALO)
    wide_aggregate = widened(aggregate + 1, 1, 1) - 1
    table = (aggregate.reshape(-1)[:, None] == ids[None, :]).astype(jnp.float32)
    wide_table = (wide_aggregate.reshape(-1)[:, None] == ids[None, :]).astype(jnp.float32)

    residual, visc = fields[0], fields[1]
    inside = visc > 0.0
    pads = ((1, 1), (0, 0), (0, 0))
    padded = jnp.pad(visc, pads)
    weights = [
        0.5 * (visc + padded[:-2]),
        0.5 * (visc + padded[2:]),
        0.5 * (visc + shifted(visc, 1, 1)),
        0.5 * (visc + shifted(visc, 1, -1)),
        0.5 * (visc + shifted(visc, 2, 1)),
        0.5 * (visc + shifted(visc, 2, -1)),
    ]
    diagonal = MASS_TERM + sum(weights)
    inverse = jnp.where(inside, 1.0 / diagonal, 0.0)

    def operate(field):
        layered = jnp.pad(field, pads)
        sides = [
            layered[:-2],
            layered[2:],
            shifted(field, 1, 1),
            shifted(field, 1, -1),
            shifted(field, 2, 1),
            shifted(field, 2, -1),
        ]
        total = MASS_TERM * field
        for weight, side in zip(weights, sides):
            total = total + weight * (field - side)
        return total

    def inner_part(field):
        return field[:, HALO:-HALO, HALO:-HALO]

    def restrict(field):
        blocks = field.reshape(layers, blocks_x, BLOCK, blocks_y, BLOCK).sum(axis=(0, 2, 4))
        return jnp.dot(blocks.reshape(-1), table, precision=PRECISE).reshape(4, COARSE // 4)

    def prolong(values):
        per_block = jnp.dot(wide_table, values.reshape(-1), precision=PRECISE)
        per_block = per_block.reshape(blocks_x + 2, blocks_y + 2)
        spread = jnp.repeat(jnp.repeat(per_block, BLOCK, axis=0), BLOCK, axis=1)
        cut = BLOCK - HALO
        return spread[cut:-cut, cut:-cut][None]

    def coarse_apply(coarse):
        return jnp.dot(whole_matrix, coarse.reshape(-1), precision=PRECISE).reshape(coarse.shape)

    def scalars(*values):
        return jnp.stack([jnp.broadcast_to(v, (COARSE // 4,)) for v in values])

    coarse = all_sum(restrict(loading))
    lifted = coarse_apply(coarse)
    direction = inverse * residual + prolong(lifted)
    answer = jnp.zeros_like(loading)
    scaled_sum = inner_now = None
    for iteration in range(ITERS):
        image = operate(direction)
        near_image, near_scaled = inner_part(image), inner_part(inverse * image)
        near_direction, near_residual = inner_part(direction), inner_part(residual)
        packed = jnp.concatenate(
            [
                restrict(near_image),
                scalars(
                    jnp.sum(near_direction * near_image),
                    jnp.sum(near_residual * near_scaled),
                    jnp.sum(near_image * near_scaled),
                    jnp.sum(near_residual * inner_part(inverse) * near_residual),
                ),
            ]
        )
        packed = all_sum(packed)
        curvature, cross, square = packed[4, 0], packed[5, 0], packed[6, 0]
        if scaled_sum is None:
            scaled_sum = packed[7, 0]
            inner_now = scaled_sum + jnp.sum(coarse * lifted)
        alpha = inner_now / curvature
        answer = answer + alpha * near_direction
        residual = residual - alpha * image
        if iteration + 1 < ITERS:
            coarse = coarse - alpha * packed[:4]
            scaled_sum = scaled_sum - 2.0 * alpha * cross + alpha * alpha * square
            lifted = coarse_apply(coarse)
            inner_next = scaled_sum + jnp.sum(coarse * lifted)
            direction = inverse * residual + prolong(lifted) + inner_next / inner_now * direction
            inner_now = inner_next
    return answer, inner_part(residual)


def solution(mesh):
    in_specs = (
        P(None, "rows", "cols"),
        P(None, "rows", "cols"),
        P("rows", "cols"),
        P(None, "rows"),
    )
    out_specs = (P(None, "rows", "cols"), P(None, "rows", "cols"))
    body = local_steps if (mesh.shape["rows"], mesh.shape["cols"]) == (8, 4) else local_general
    return jax.shard_map(body, mesh=mesh, in_specs=in_specs, out_specs=out_specs, check_vma=False)
```

```python
import jax
import jax.numpy as jnp
from jax import lax
from jax.experimental import pallas as pl
from jax.experimental.pallas import tpu as pltpu
from jax.sharding import PartitionSpec as P

BLOCK = 16
COARSE = 512
ITERS = 4
HALO = 8
SIDE = 7
LANES = 128
PAD = 8
PART = 64

MASS_TERM = 1.0
PRECISE = lax.Precision.HIGHEST
BOTH = ("rows", "cols")


def iota(shape, dim):
    return lax.broadcasted_iota(jnp.int32, shape, dim)


def roll(x, shift, axis):
    size = x.shape[axis]
    shift = shift % size
    return x if shift == 0 else pltpu.roll(x, shift, axis)


def lane_row():
    return iota((1, LANES), 1)


def pick_lanes(values, index):
    return jnp.take_along_axis(values, index, axis=1, mode="promise_in_bounds")


def fold_rows(plane):
    rows = plane.shape[0]
    return plane.reshape(rows // BLOCK, 2, 8, LANES).sum(axis=1)


def pack_blocks(folds):
    count = folds[0].shape[0]
    pad = (-count * len(folds)) % 8
    stacked = jnp.concatenate(folds + ([jnp.zeros((pad, LANES), jnp.float32)] if pad else []), axis=0)
    spread = iota((LANES, LANES), 0) // BLOCK == iota((LANES, LANES), 1) % (LANES // BLOCK)
    summed = jnp.dot(stacked, spread.astype(jnp.float32), precision=PRECISE)
    group = lane_row() // (LANES // BLOCK)
    row = jnp.zeros((1, LANES), jnp.float32)
    for index in range(len(folds) * count):
        row = row + jnp.where(group == index, summed[index : index + 1], 0.0)
    return row


def pack_scalars(partials, offset):
    lane = lane_row()
    row = jnp.zeros((1, LANES), jnp.float32)
    for index, partial in enumerate(partials):
        total = jnp.sum(jnp.sum(partial, axis=0, keepdims=True), axis=1, keepdims=True)
        row = row + jnp.where(lane == offset + index, total, 0.0)
    return row


def unfold(values, slot, width):
    devices = values.shape[0]
    lane = iota((devices, LANES), 1)
    part = jnp.where(lane < width, roll(values, -slot * width, 1), 0.0)
    step = width
    while step < LANES:
        part = part + roll(part, step, 1)
        step *= 2
    per_row = LANES // width
    own = jnp.where(iota((devices, LANES), 0) % per_row == lane // width, part, 0.0)
    rows = [
        jnp.sum(own[k * per_row : (k + 1) * per_row], axis=0, keepdims=True) for k in range(devices // per_row)
    ]
    return jnp.concatenate(rows, axis=0)


def coarse_solve(values, names, position, parts):
    line = jnp.zeros((8, COARSE), jnp.float32)
    for part, ref in enumerate(parts):
        aggregate = iota((PART, LANES), 0) + ((position ^ part) * PART + 1)
        total = jnp.zeros((PART, LANES), jnp.float32)
        for row in range(8):
            total = total + jnp.where(aggregate == names[row : row + 1], values[row : row + 1], 0.0)
        column = jnp.sum(total, axis=1, keepdims=True)
        line = line + (ref[...] * column).reshape(PART // 8, 8, COARSE).sum(axis=0)
    line = jnp.broadcast_to(jnp.sum(line, axis=0, keepdims=True), (8, COARSE))
    return [line[:, t * LANES : (t + 1) * LANES] for t in range(COARSE // LANES)]


def lookup(coarse, names):
    index = jnp.maximum(names - 1, 0)
    inner = index % LANES
    result = jnp.zeros(names.shape, jnp.float32)
    for tile, values in enumerate(coarse):
        result = jnp.where(index // LANES == tile, pick_lanes(values, inner), result)
    return jnp.where(names > 0, result, 0.0)


def apply_blocks(diag, east, south, values, grid):
    count_x, count_y, blocks_x, blocks_y = grid
    width = blocks_x * blocks_y
    lane = iota(values.shape, 1)
    row, col = iota(values.shape, 0), lane // width
    at_x, at_y = (lane % width) // blocks_y, lane % blocks_y
    last_x, last_y = at_x == blocks_x - 1, at_y == blocks_y - 1
    step_e = width - (blocks_y - 1)
    step_s = (blocks_x - 1) * blocks_y

    def take(x, inner, outer, is_outer, missing):
        return jnp.where(missing, 0.0, jnp.where(is_outer, outer(x), inner(x)))

    from_e = take(
        values, lambda x: roll(x, -1, 1), lambda x: roll(x, -step_e, 1), last_y, last_y & (col == count_y - 1)
    )
    from_w = take(
        east * values, lambda x: roll(x, 1, 1), lambda x: roll(x, step_e, 1), at_y == 0, (at_y == 0) & (col == 0)
    )
    from_s = take(
        values,
        lambda x: roll(x, -blocks_y, 1),
        lambda x: roll(roll(x, -1, 0), step_s, 1),
        last_x,
        last_x & (row == count_x - 1),
    )
    from_n = take(
        south * values,
        lambda x: roll(x, blocks_y, 1),
        lambda x: roll(roll(x, 1, 0), -step_s, 1),
        at_x == 0,
        (at_x == 0) & (row == 0),
    )
    return diag * values - east * from_e - south * from_s - from_w - from_n


def local_names(ids):
    rows = ids.shape[1]
    lane = iota((8, LANES), 1)
    at = lane % BLOCK
    starts = [0] + list(range(HALO, rows, BLOCK))
    result = jnp.zeros((8, LANES), jnp.float32)
    for index, start in enumerate(starts):
        inner = pick_lanes(ids[0, start : start + 8], (at * BLOCK) % LANES)
        outer = pick_lanes(ids[1, start : start + 8], jnp.where(at == 8, 0, LANES - 1))
        both = jnp.where(at < 8, inner, jnp.where(at < 10, outer, 0.0))
        result = jnp.where(lane // BLOCK == index, both, result)
    return result


def prolong(target, values):
    lane = iota((8, LANES), 1)
    rows = target.shape[1]
    bounds = [0] + list(range(HALO, rows, BLOCK)) + [rows]
    for index in range(len(bounds) - 1):
        main = pick_lanes(values, lane // BLOCK + index * BLOCK)
        side = pick_lanes(values, jnp.where(lane < BLOCK, 8, 9) + index * BLOCK)
        for row in range(bounds[index], bounds[index + 1], 8):
            target[0, row : row + 8] = main
            target[1, row : row + 8] = side


def band(ref, index, step=0):
    rows = ref.shape[1]
    return ref[index, PAD + step : rows - PAD + step, :]


def put(ref, index, value):
    ref[index, PAD : ref.shape[1] - PAD, :] = value


def own(ref, index, step=0):
    rows = ref.shape[1]
    return ref[index, PAD + HALO + step : rows - PAD - HALO + step, :]


def beside(main, side):
    lane = iota(main.shape, 1)
    main_e, side_e = roll(main, -1, 1), roll(side, -1, 1)
    main_w, side_w = roll(main, 1, 1), roll(side, 1, 1)
    last, first = lane == LANES - 1, lane == 0
    east = jnp.where(last, side_e, main_e), jnp.where(last, main_e, side_e)
    west = jnp.where(first, side_w, main_w), jnp.where(first, main_w, side_w)
    return east, west


class Operator:
    def __init__(self, w_layer, w_row, w_east, w_west):
        self.w_layer, self.w_row, self.w_east, self.w_west = w_layer, w_row, w_east, w_west

    def wide(self, source):
        layers = self.w_row.shape[0] // 2
        current = [band(source, k * layers) for k in range(2)]
        below = [-band(self.w_layer, k * (layers + 1)) * current[k] for k in range(2)]
        for layer in range(layers):
            last = layer == layers - 1
            after = [None if last else band(source, k * layers + layer + 1) for k in range(2)]
            east, west = beside(*current)
            result = []
            for k in range(2):
                at = k * layers + layer
                here = current[k]
                above = band(self.w_layer, k * (layers + 1) + layer + 1) * (here if last else here - after[k])
                total = MASS_TERM * here + above - below[k]
                total += band(self.w_row, at) * (here - band(source, at, 1))
                total += band(self.w_row, at, -1) * (here - band(source, at, -1))
                total += band(self.w_east, at) * (here - east[k])
                total += band(self.w_west, at) * (here - west[k])
                result.append(total)
                below[k] = above
            yield layer, result
            current = after

    def near(self, source):
        layers = self.w_row.shape[0] // 2
        here = own(source, 0)
        below = -own(self.w_layer, 0) * here
        lane = iota(here.shape, 1)
        for layer in range(layers):
            last = layer == layers - 1
            after = None if last else own(source, layer + 1)
            side = own(source, layers + layer)
            above = own(self.w_layer, layer + 1) * (here if last else here - after)
            total = MASS_TERM * here + above - below
            total += own(self.w_row, layer) * (here - own(source, layer, 1))
            total += own(self.w_row, layer, -1) * (here - own(source, layer, -1))
            east = jnp.where(lane == LANES - 1, roll(side, -1, 1), roll(here, -1, 1))
            west = jnp.where(lane == 0, roll(side, 1, 1), roll(here, 1, 1))
            total += own(self.w_east, layer) * (here - east)
            total += own(self.w_west, layer) * (here - west)
            yield layer, total
            here, below = after, above


def near(plane):
    return plane[HALO:-HALO]


def tally(plane):
    return plane.reshape(plane.shape[0] // 8, 8, LANES).sum(axis=0)


def own_ids(ids):
    blocks_x = ids.shape[0] // 2
    lines = [jnp.broadcast_to(ids[bx : bx + 1], (BLOCK, LANES)) for bx in range(blocks_x)]
    return jnp.concatenate(lines, axis=0)


def rows_kernel(position, aggregate_hbm, loading, viscosity, ids, near_rows, far_rows, aggregate, sems):
    layers, rows, _ = loading.shape
    odd = position[0] % 2
    numbers = pltpu.make_async_copy(aggregate_hbm, aggregate, sems.at[4])
    numbers.start()
    copies = []
    for side, target in enumerate((near_rows, far_rows)):
        top = odd if side == 0 else 1 - odd
        at = pl.multiple_of((1 - top) * (rows - HALO), HALO)
        for k, source in enumerate((loading, viscosity)):
            copies.append(
                pltpu.make_async_copy(
                    source.at[:, pl.ds(at, HALO), :],
                    target.at[pl.ds(k * layers, layers)],
                    sems.at[2 * side + k],
                )
            )
    for copy in copies:
        copy.start()
    numbers.wait()
    blocks_x, blocks_y = aggregate.shape
    lane = lane_row()
    flat = jnp.zeros((1, LANES), jnp.float32)
    for bx in range(blocks_x):
        names = jnp.zeros((1, LANES), jnp.float32)
        for by in range(blocks_y):
            name = (aggregate[bx, by] + 1).astype(jnp.float32)
            names = jnp.where(lane // BLOCK == by, name, names)
            flat = jnp.where(lane % (blocks_x * blocks_y) == bx * blocks_y + by, name, flat)
        ids[bx : bx + 1] = names
    ids[blocks_x:] = jnp.broadcast_to(flat, (ids.shape[0] - blocks_x, LANES))
    first, last = ids[0:1], ids[blocks_x - 1 : blocks_x]
    near_rows[2 * layers] = jnp.broadcast_to(jnp.where(odd == 1, first, last), (HALO, LANES))
    far_rows[2 * layers] = jnp.broadcast_to(jnp.where(odd == 1, last, first), (HALO, LANES))
    for copy in copies:
        copy.wait()


def tall_plane(slot, own, odd, near_rows, far_rows):
    low = jnp.where(odd == 1, near_rows[slot], far_rows[slot])
    high = jnp.where(odd == 1, far_rows[slot], near_rows[slot])
    return jnp.concatenate([low, own, high], axis=0)


def edge_kernel(position, loading, viscosity, own_names, near_rows, far_rows, near_cols, far_cols, message):
    layers = loading.shape[0]
    odd = position[0] % 2
    lane = lane_row()
    right = left = jnp.zeros(near_cols.shape, jnp.float32)
    for slot in range(2 * layers + 1):
        if slot < layers:
            own = loading[slot]
        elif slot < 2 * layers:
            own = viscosity[slot - layers]
        else:
            own = own_ids(own_names)
        plane = tall_plane(slot, own, odd, near_rows, far_rows)
        at = slot * SIDE
        here = (lane >= at) & (lane < at + SIDE)
        right = jnp.where(here, roll(plane, at + SIDE, 1), right)
        left = jnp.where(here, roll(plane, at, 1), left)
    odd_col = position[1] % 2
    near_cols[...] = jnp.where(odd_col == 1, left, right)
    far_cols[...] = jnp.where(odd_col == 1, right, left)
    blocks_x, width = own_names.shape[0] // 2, own_names.shape[0] // 2 * (LANES // BLOCK)
    fold = jnp.zeros((blocks_x, 8, LANES), jnp.float32)
    for layer in range(layers):
        fold = fold + fold_rows(loading[layer])
    line = pack_blocks([fold.sum(axis=1)])
    line = line + jnp.where((lane >= width) & (lane < 2 * width), own_names[blocks_x : blocks_x + 1], 0.0)
    message[...] = jnp.broadcast_to(line, message.shape)


def start_kernel(
    position, loading, viscosity, own_names, near_rows, far_rows, near_cols, far_cols, arrived, *rest
):
    parts = rest[:8]
    resid, direction, image, inverse, w_layer, w_row, w_east, w_west, names_out, lifted_blocks, message = rest[8:19]
    wide, ids, scaled_image, rise = rest[19:]
    layers = loading.shape[0]
    blocks_x, blocks_y = loading.shape[1] // BLOCK, LANES // BLOCK
    width = blocks_x * blocks_y
    odd, odd_col = position[0] % 2, position[1] % 2
    lane = lane_row()
    from_west = jnp.where(odd_col == 1, near_cols[...], far_cols[...])
    from_east = jnp.where(odd_col == 1, far_cols[...], near_cols[...])

    def widen(slot, cells):
        at = slot * SIDE
        beyond = jnp.where(lane < SIDE, roll(from_east, -at, 1), 0.0)
        beyond = jnp.where(lane >= LANES - SIDE, roll(from_west, LANES - SIDE - at, 1), beyond)
        return tall_plane(slot, cells, odd, near_rows, far_rows), beyond

    for layer in range(layers):
        for k, tile in enumerate(widen(layer, loading[layer])):
            put(resid, k * layers + layer, tile)
        for k, tile in enumerate(widen(layers + layer, viscosity[layer])):
            put(wide, k * layers + layer, tile)
    ids[0], ids[1] = widen(2 * layers, own_ids(own_names))
    names_out[...] = local_names(ids)

    sums = arrived[...]
    names = unfold(sums, 1, width).astype(jnp.int32)
    solved = coarse_solve(unfold(sums, 0, width), names, position[0], parts)
    lifted_blocks[...] = lookup(solved, names)
    prolong(rise, lookup(solved, names_out[...].astype(jnp.int32)))

    for layer in range(layers):
        east, west = beside(band(wide, layer), band(wide, layers + layer))
        for k in range(2):
            at, face = k * layers + layer, k * (layers + 1) + layer
            visc = band(wide, at)
            before = 0.5 * (visc if layer == 0 else visc + band(wide, at - 1))
            after = 0.5 * (visc if layer == layers - 1 else visc + band(wide, at + 1))
            down, up = 0.5 * (visc + band(wide, at, 1)), 0.5 * (visc + band(wide, at, -1))
            right, left = 0.5 * (visc + east[k]), 0.5 * (visc + west[k])
            if layer == 0:
                put(w_layer, face, before)
            put(w_layer, face + 1, after)
            put(w_row, at, down)
            put(w_east, at, right)
            put(w_west, at, left)
            diagonal = MASS_TERM + before + after + up + down + left + right
            part = jnp.where(visc > 0.0, 1.0 / diagonal, 0.0)
            put(inverse, at, part)
            put(direction, at, part * band(resid, at) + rise[k])
    folds_own, folds_east, folds_south = block_matrix(w_layer, w_row, w_east, w_west)

    operator = Operator(w_layer, w_row, w_east, w_west)
    zero = jnp.zeros((8, LANES), jnp.float32)
    folds = [jnp.zeros((blocks_x, 8, LANES), jnp.float32) for _ in range(2)]
    s_rp = s_rd = s_dq = s_eq = s_pq = s_ee = zero
    for layer, planes in operator.wide(direction):
        for k, plane in enumerate(planes):
            at = k * layers + layer
            put(image, at, plane)
            put(scaled_image, at, band(inverse, at) * plane)
        q, r, p, v = near(planes[0]), own(resid, layer), own(direction, layer), own(inverse, layer)
        d, e = v * r, v * q
        s_rp += tally(r * p)
        s_rd += tally(r * d)
        s_dq += tally(d * q)
        s_eq += tally(e * q)
        s_pq += tally(p * q)
        folds[0] += fold_rows(q)
    for layer, image_e in operator.near(scaled_image):
        s_ee += tally(image_e * own(scaled_image, layer))
        folds[1] += fold_rows(image_e)
    upper = pack_blocks([fold.sum(axis=1) for fold in folds])
    upper = upper + pack_scalars([s_rp, s_rd, s_dq, s_eq, s_pq, s_ee], 3 * width)
    lower = pack_blocks([folds_own, folds_east, folds_south])
    write_message(message, upper, lower)


def write_message(message, upper, lower):
    rows = iota(message.shape, 0)
    message[...] = jnp.where(rows % 2 == 0, upper, lower)


def block_matrix(w_layer, w_row, w_east, w_west):
    layers = w_row.shape[0] // 2
    rows = w_row.shape[1]
    lane = lane_row()
    east = west = jnp.zeros((rows - 2 * (PAD + HALO), LANES), jnp.float32)
    line = jnp.zeros((rows, LANES), jnp.float32)
    for layer in range(layers):
        east = east + own(w_east, layer)
        west = west + own(w_west, layer)
        line = line + w_row[layer]
    own_cells = fold_rows(own(w_layer, 0) + own(w_layer, layers)).sum(axis=1)
    east_face = fold_rows(jnp.where(lane % BLOCK == BLOCK - 1, east, 0.0)).sum(axis=1)
    west_face = fold_rows(jnp.where(lane % BLOCK == 0, west, 0.0)).sum(axis=1)
    count = own_cells.shape[0]
    first = PAD + HALO - 1
    faces = [line[first + BLOCK * k : first + BLOCK * k + 1] for k in range(count + 1)]
    north_face, south_face = jnp.concatenate(faces[:-1], axis=0), jnp.concatenate(faces[1:], axis=0)
    mass = jnp.full((count, LANES), MASS_TERM * layers * BLOCK, jnp.float32)
    total = mass + own_cells + east_face + west_face + south_face + north_face
    return total, east_face, south_face


def lane_total(values, lane_at):
    return jnp.sum(values[:, lane_at : lane_at + 1], axis=0, keepdims=True)


def dot_blocks(left, right):
    return jnp.sum(jnp.sum(left * right, axis=0, keepdims=True), axis=1, keepdims=True)


def received(ref, parity):
    return ref[pl.ds(parity, ref.shape[0] // 2, stride=2), :]


def write_scalars(ref, values):
    lane = lane_row()
    line = jnp.zeros((1, LANES), jnp.float32)
    for index, value in enumerate(values):
        line = jnp.where(lane == index, value, line)
    ref[...] = jnp.broadcast_to(line, ref.shape)


def middle_kernel(grid, position, arrived0, arrived, names_ref, lifted0_ref, *rest):
    parts = rest[:8]
    resid0, direction0, image0, inverse, w_layer, w_row, w_east, w_west = rest[8:16]
    resid, lifted, direction, image, lifted_image, scalars, lifted_blocks, message = rest[16:24]
    scaled_image, scaled_lifted, rise_0, rise_1 = rest[24:]
    width = grid[2] * grid[3]
    layers = resid.shape[0] // 2
    sums = arrived0[...]
    names = unfold(sums, 1, width).astype(jnp.int32)
    here = names_ref[...].astype(jnp.int32)
    upper, lower = received(arrived, 0), received(arrived, 1)
    s_rp, s_rd, s_dq, s_eq, s_pq, s_ee = [lane_total(upper, 3 * width + k) for k in range(6)]
    r_q, r_e = [unfold(upper, k, width) for k in range(2)]
    diag, east, south = [unfold(lower, k, width) for k in range(3)]
    lifted0 = lifted0_ref[...]
    r_d = r_q - apply_blocks(diag, east, south, lifted0, grid)
    s_dd = s_dq - dot_blocks(lifted0, r_d)
    s_de = s_eq - dot_blocks(lifted0, r_e)
    alpha0 = s_rp / s_pq
    scaled_sum = s_rd - 2.0 * alpha0 * s_dq + alpha0 * alpha0 * s_eq
    coarse1 = unfold(sums, 0, width) - alpha0 * r_q
    solved = coarse_solve(coarse1, names, position[0], parts)
    lifted1 = lookup(solved, names)
    prolong(rise_0, lookup(solved, here))
    inner1 = scaled_sum + dot_blocks(coarse1, lifted1)
    beta0 = inner1 / s_rp
    r_x = r_d - alpha0 * r_e + beta0 * r_q
    energy = (
        s_dd
        - 2.0 * alpha0 * s_de
        + alpha0 * alpha0 * s_ee
        + 2.0 * beta0 * (s_dq - alpha0 * s_eq)
        + beta0 * beta0 * s_pq
    )
    block_image = apply_blocks(diag, east, south, lifted1, grid)
    alpha1 = inner1 / (energy + dot_blocks(lifted1, 2.0 * r_x + block_image))
    coarse2 = coarse1 - alpha1 * (r_x + block_image)
    solved = coarse_solve(coarse2, names, position[0], parts)
    lifted_blocks[...] = lookup(solved, names)
    prolong(rise_1, lookup(solved, here))
    write_scalars(scalars, [alpha0, alpha1, inner1])

    operator = Operator(w_layer, w_row, w_east, w_west)
    for at in range(2 * layers):
        after = band(resid0, at) - alpha0 * band(image0, at)
        put(resid, at, after)
        put(direction, at, band(inverse, at) * after + rise_0[at // layers] + beta0 * band(direction0, at))
    zero = jnp.zeros((8, LANES), jnp.float32)
    folds = [jnp.zeros((grid[2], 8, LANES), jnp.float32) for _ in range(5)]
    s_rz = s_rd = s_zu = s_zq = s_pq = s_du = s_dq = s_us = s_uw = s_qw = zero
    s_ss = s_sw = s_ww = zero
    for layer, planes in operator.wide(direction):
        for k, plane in enumerate(planes):
            at = k * layers + layer
            put(image, at, plane)
            after = band(resid, at) - alpha1 * plane
            put(resid, at, after)
            put(lifted, at, band(inverse, at) * after + rise_1[k])
            put(scaled_image, at, band(inverse, at) * plane)
        q, r, p, v = near(planes[0]), own(resid, layer), own(direction, layer), own(inverse, layer)
        d, z, w = v * r, own(lifted, layer), v * q
        s_rz += tally(r * z)
        s_rd += tally(r * d)
        s_zq += tally(z * q)
        s_pq += tally(p * q)
        s_dq += tally(d * q)
        s_qw += tally(q * w)
        folds[1] += fold_rows(q)
        folds[4] += fold_rows(r)
    for layer, planes in operator.wide(lifted):
        for k, plane in enumerate(planes):
            at = k * layers + layer
            put(lifted_image, at, plane)
            put(scaled_lifted, at, band(inverse, at) * plane)
        u = near(planes[0])
        v = own(inverse, layer) * u
        s_zu += tally(u * own(lifted, layer))
        s_du += tally(v * own(resid, layer))
        s_us += tally(u * v)
        s_uw += tally(u * own(scaled_image, layer))
        folds[0] += fold_rows(u)
    for layer, image_s in operator.near(scaled_lifted):
        s_ss += tally(image_s * own(scaled_lifted, layer))
        s_sw += tally(image_s * own(scaled_image, layer))
        folds[2] += fold_rows(image_s)
    for layer, image_w in operator.near(scaled_image):
        s_ww += tally(image_w * own(scaled_image, layer))
        folds[3] += fold_rows(image_w)
    lines = [fold.sum(axis=1) for fold in folds]
    upper = pack_blocks(lines[:4])
    lower = pack_blocks(lines[4:]) + pack_scalars(
        [s_rz, s_rd, s_zu, s_zq, s_pq, s_du, s_dq, s_us, s_uw, s_qw, s_ss, s_sw, s_ww],
        width,
    )
    write_message(message, upper, lower)


def last_kernel(grid, position, arrived0, before, arrived, names_ref, scalars, lifted2_ref, *rest):
    parts = rest[:8]
    resid, lifted, direction1, image1, lifted_image, direction0, inverse, w_layer, w_row, w_east, w_west = rest[8:19]
    outs = rest[19:21]
    direction, rise_3, answer, out_resid, sems = rest[21:]
    width = grid[2] * grid[3]
    layers = resid.shape[0] // 2
    names = unfold(arrived0[...], 1, width).astype(jnp.int32)
    here = names_ref[...].astype(jnp.int32)
    blocks = received(before, 1)
    diag, east, south = [unfold(blocks, k, width) for k in range(3)]
    upper, lower = received(arrived, 0), received(arrived, 1)
    r_u, r_q, r_s, r_w = [unfold(upper, k, width) for k in range(4)]
    r_r = unfold(lower, 0, width)
    s_rz, s_rd, s_zu, s_zq, s_pq, s_du, s_dq, s_us, s_uw, s_qw, s_ss, s_sw, s_ww = [
        lane_total(lower, width + k) for k in range(13)
    ]
    lifted2 = lifted2_ref[...]
    r_d = r_u - apply_blocks(diag, east, south, lifted2, grid)
    s_dd = s_du - dot_blocks(lifted2, r_d)
    s_ds = s_us - dot_blocks(lifted2, r_s)
    s_dw = s_uw - dot_blocks(lifted2, r_w)
    alpha0, alpha1, inner1 = [scalars[0:1, k : k + 1] for k in range(3)]
    inner2 = s_rz
    beta1 = inner2 / inner1
    alpha2 = inner2 / (s_zu + 2.0 * beta1 * s_zq + beta1 * beta1 * s_pq)
    coarse3 = r_r - alpha2 * (r_u + beta1 * r_q)
    solved = coarse_solve(coarse3, names, position[0], parts)
    lifted3 = lookup(solved, names)
    prolong(rise_3, lookup(solved, here))
    scaled_sum = (
        s_rd
        - 2.0 * alpha2 * (s_du + beta1 * s_dq)
        + alpha2 * alpha2 * (s_us + 2.0 * beta1 * s_uw + beta1 * beta1 * s_qw)
    )
    inner3 = scaled_sum + dot_blocks(coarse3, lifted3)
    beta2 = inner3 / inner2
    rise = lifted3 + beta2 * lifted2
    k_d, k_s, k_w, k_p = 1.0 + beta2, -alpha2, -alpha2 * beta1, beta2 * beta1
    energy = (
        k_d * k_d * s_dd
        + k_s * k_s * s_ss
        + k_w * k_w * s_ww
        + k_p * k_p * s_pq
        + 2.0 * (k_d * (k_s * s_ds + k_w * s_dw + k_p * s_dq) + k_s * (k_w * s_sw + k_p * s_uw) + k_w * k_p * s_qw)
    )
    r_x = k_d * r_d + k_s * r_s + k_w * r_w + k_p * r_q
    block_image = apply_blocks(diag, east, south, rise, grid)
    alpha3 = inner3 / (energy + dot_blocks(rise, 2.0 * r_x + block_image))

    for at in range(2 * layers):
        direction2 = band(lifted, at) + beta1 * band(direction1, at)
        after = band(resid, at) - alpha2 * (band(lifted_image, at) + beta1 * band(image1, at))
        step = band(inverse, at) * after + rise_3[at // layers] + beta2 * direction2
        put(direction, at, step)
        if at < layers:
            out_resid[at] = near(after)
            answer[at] = (
                alpha0 * own(direction0, at)
                + alpha1 * own(direction1, at)
                + alpha2 * near(direction2)
                + alpha3 * near(step)
            )
    copies = [pltpu.make_async_copy(answer, outs[0], sems.at[layers])]
    copies[0].start()
    for layer, plane in Operator(w_layer, w_row, w_east, w_west).near(direction):
        out_resid[layer] = out_resid[layer] - alpha3 * plane
        copies.append(pltpu.make_async_copy(out_resid.at[layer], outs[1].at[layer], sems.at[layer]))
        copies[-1].start()
    for copy in copies:
        copy.wait()


def call(kernel, outs, scratch, name, smem, *operands, spaces=None, out_space=pltpu.VMEM):
    whole = pl.BlockSpec(memory_space=pltpu.VMEM)
    scalar = pl.BlockSpec(memory_space=pltpu.SMEM)
    specs = [scalar] * smem + [whole] * (len(operands) - smem)
    operands = list(operands)
    for index in spaces or ():
        specs[index] = pl.BlockSpec(memory_space=pltpu.HBM)
        operands[index] = pltpu.with_memory_space_constraint(operands[index], pltpu.HBM)
    return pl.pallas_call(
        kernel,
        out_shape=[jax.ShapeDtypeStruct(shape, jnp.float32) for shape in outs],
        in_specs=specs,
        out_specs=[pl.BlockSpec(memory_space=out_space)] * len(outs),
        scratch_shapes=[pltpu.VMEM(s, jnp.float32) if isinstance(s, tuple) else s for s in scratch],
        compiler_params=pltpu.CompilerParams(vmem_limit_bytes=20 * 1024 * 1024),
        name=name,
    )(*operands)


def exchange(message):
    return lax.all_to_all(message, BOTH, 0, 0, tiled=True)


def pair(values, axis, mask):
    return lax.ppermute(values, axis, [(i, i ^ mask) for i in range(lax.axis_size(axis))])


def pair_far(values, axis):
    count = lax.axis_size(axis)
    return lax.ppermute(values, axis, [(i, i + 1 if i % 2 else i - 1) for i in range(1, count - 1)])


def local_steps(loading, viscosity, aggregate, coarse_inverse):
    layers, cells_x, cells_y = loading.shape
    blocks_x, blocks_y = aggregate.shape
    count_x, count_y = lax.axis_size("rows"), lax.axis_size("cols")
    devices = count_x * count_y
    grid = (count_x, count_y, blocks_x, blocks_y)
    position = jnp.stack([lax.axis_index(axis).astype(jnp.int32) for axis in BOTH])
    tall = cells_x + 2 * HALO
    edge = (2 * layers + 1, HALO, LANES)
    shard = coarse_inverse.T
    parts = [pair(shard, "rows", mask) for mask in (2, 4, 6)]
    ids, near_rows, far_rows = call(
        rows_kernel,
        [(8, LANES), edge, edge],
        [pltpu.SMEM(aggregate.shape, jnp.int32), pltpu.SemaphoreType.DMA((5,))],
        "rows",
        1,
        position,
        aggregate,
        loading,
        viscosity,
        spaces=(1, 2, 3),
    )
    own = (position, loading, viscosity, ids)
    near_rows, far_rows = pair(near_rows, "rows", 1), pair_far(far_rows, "rows")
    parts = [shard] + parts
    parts = [part for both in ((part, pair(part, "rows", 1)) for part in parts) for part in both]
    parts, far_rows = lax.optimization_barrier((parts, far_rows))
    near_cols, far_cols, message0 = call(
        edge_kernel, [(tall, LANES)] * 2 + [(devices, LANES)], [], "edges", 1, *own, near_rows, far_rows
    )
    near_cols, far_cols = pair(near_cols, "cols", 1), pair_far(far_cols, "cols")
    arrived0 = exchange(message0)
    field = (2 * layers, tall + 2 * PAD, LANES)
    taller = (2 * (layers + 1), tall + 2 * PAD, LANES)
    plane = (2, tall, LANES)
    message = (2 * devices, LANES)
    line = (8, LANES)
    resid, direction0, image0, inverse, w_layer, w_row, w_east, w_west, names, lifted_blocks, message1 = call(
        start_kernel,
        [field] * 4 + [taller, field, field, field, line, line, message],
        [field, plane, field, plane],
        "start",
        1,
        *own,
        near_rows,
        far_rows,
        near_cols,
        far_cols,
        arrived0,
        *parts,
    )
    weights = (inverse, w_layer, w_row, w_east, w_west)
    arrived1 = exchange(message1)
    resid, lifted, direction1, image1, lifted_image, scalars, lifted_blocks, message2 = call(
        lambda *refs: middle_kernel(grid, *refs),
        [field] * 5 + [line, line, message],
        [field] * 2 + [plane] * 2,
        "middle",
        1,
        position,
        arrived0,
        arrived1,
        names,
        lifted_blocks,
        *parts,
        resid,
        direction0,
        image0,
        *weights,
    )
    arrived2 = exchange(message2)
    return call(
        lambda *refs: last_kernel(grid, *refs),
        [loading.shape] * 2,
        [field, plane, loading.shape, loading.shape, pltpu.SemaphoreType.DMA((layers + 1,))],
        "last",
        1,
        position,
        arrived0,
        arrived1,
        arrived2,
        names,
        scalars,
        lifted_blocks,
        *parts,
        resid,
        lifted,
        direction1,
        image1,
        lifted_image,
        direction0,
        *weights,
        out_space=pltpu.HBM,
    )


def from_sides(block, axis, dim, width):
    count = lax.axis_size(axis)
    forward = [(i, i + 1) for i in range(count - 1)]
    backward = [(target, source) for source, target in forward]
    size = block.shape[dim]
    low = lax.ppermute(lax.slice_in_dim(block, size - width, size, axis=dim), axis, forward)
    high = lax.ppermute(lax.slice_in_dim(block, 0, width, axis=dim), axis, backward)
    return low, high


def widened(block, width_x, width_y):
    low, high = from_sides(block, "rows", block.ndim - 2, width_x)
    block = jnp.concatenate([low, block, high], axis=-2)
    turned = jnp.swapaxes(block, -1, -2)
    low, high = from_sides(turned, "cols", turned.ndim - 2, width_y)
    low, high = jnp.swapaxes(low, -1, -2), jnp.swapaxes(high, -1, -2)
    return jnp.concatenate([low, block, high], axis=-1)


def all_sum(values):
    count = lax.axis_size("rows") * lax.axis_size("cols")
    if count > 64:
        return lax.psum(lax.psum(values, "cols"), "rows")
    spread = jnp.broadcast_to(values[None], (count,) + values.shape)
    return lax.all_to_all(spread, BOTH, 0, 0).sum(axis=0)


def shifted(field, axis, step):
    return jnp.roll(field, step, axis=axis)


def local_general(loading, viscosity, aggregate, coarse_inverse):
    layers, cells_x, cells_y = loading.shape
    blocks_x, blocks_y = aggregate.shape
    ids = jnp.arange(COARSE, dtype=jnp.int32)
    whole_matrix = lax.all_gather(coarse_inverse, "rows", axis=1, tiled=True)
    fields = widened(jnp.stack([loading, viscosity]), HALO, HALO)
    wide_aggregate = widened(aggregate + 1, 1, 1) - 1
    table = (aggregate.reshape(-1)[:, None] == ids[None, :]).astype(jnp.float32)
    wide_table = (wide_aggregate.reshape(-1)[:, None] == ids[None, :]).astype(jnp.float32)

    residual, visc = fields[0], fields[1]
    inside = visc > 0.0
    pads = ((1, 1), (0, 0), (0, 0))
    padded = jnp.pad(visc, pads)
    weights = [
        0.5 * (visc + padded[:-2]),
        0.5 * (visc + padded[2:]),
        0.5 * (visc + shifted(visc, 1, 1)),
        0.5 * (visc + shifted(visc, 1, -1)),
        0.5 * (visc + shifted(visc, 2, 1)),
        0.5 * (visc + shifted(visc, 2, -1)),
    ]
    diagonal = MASS_TERM + sum(weights)
    inverse = jnp.where(inside, 1.0 / diagonal, 0.0)

    def operate(field):
        layered = jnp.pad(field, pads)
        sides = [
            layered[:-2],
            layered[2:],
            shifted(field, 1, 1),
            shifted(field, 1, -1),
            shifted(field, 2, 1),
            shifted(field, 2, -1),
        ]
        total = MASS_TERM * field
        for weight, side in zip(weights, sides):
            total = total + weight * (field - side)
        return total

    def inner_part(field):
        return field[:, HALO:-HALO, HALO:-HALO]

    def restrict(field):
        blocks = field.reshape(layers, blocks_x, BLOCK, blocks_y, BLOCK).sum(axis=(0, 2, 4))
        return jnp.dot(blocks.reshape(-1), table, precision=PRECISE).reshape(4, COARSE // 4)

    def prolong(values):
        per_block = jnp.dot(wide_table, values.reshape(-1), precision=PRECISE)
        per_block = per_block.reshape(blocks_x + 2, blocks_y + 2)
        spread = jnp.repeat(jnp.repeat(per_block, BLOCK, axis=0), BLOCK, axis=1)
        cut = BLOCK - HALO
        return spread[cut:-cut, cut:-cut][None]

    def coarse_apply(coarse):
        return jnp.dot(whole_matrix, coarse.reshape(-1), precision=PRECISE).reshape(coarse.shape)

    def scalars(*values):
        return jnp.stack([jnp.broadcast_to(v, (COARSE // 4,)) for v in values])

    coarse = all_sum(restrict(loading))
    lifted = coarse_apply(coarse)
    direction = inverse * residual + prolong(lifted)
    answer = jnp.zeros_like(loading)
    scaled_sum = inner_now = None
    for iteration in range(ITERS):
        image = operate(direction)
        near_image, near_scaled = inner_part(image), inner_part(inverse * image)
        near_direction, near_residual = inner_part(direction), inner_part(residual)
        packed = jnp.concatenate(
            [
                restrict(near_image),
                scalars(
                    jnp.sum(near_direction * near_image),
                    jnp.sum(near_residual * near_scaled),
                    jnp.sum(near_image * near_scaled),
                    jnp.sum(near_residual * inner_part(inverse) * near_residual),
                ),
            ]
        )
        packed = all_sum(packed)
        curvature, cross, square = packed[4, 0], packed[5, 0], packed[6, 0]
        if scaled_sum is None:
            scaled_sum = packed[7, 0]
            inner_now = scaled_sum + jnp.sum(coarse * lifted)
        alpha = inner_now / curvature
        answer = answer + alpha * near_direction
        residual = residual - alpha * image
        if iteration + 1 < ITERS:
            coarse = coarse - alpha * packed[:4]
            scaled_sum = scaled_sum - 2.0 * alpha * cross + alpha * alpha * square
            lifted = coarse_apply(coarse)
            inner_next = scaled_sum + jnp.sum(coarse * lifted)
            direction = inverse * residual + prolong(lifted) + inner_next / inner_now * direction
            inner_now = inner_next
    return answer, inner_part(residual)


def solution(mesh):
    in_specs = (
        P(None, "rows", "cols"),
        P(None, "rows", "cols"),
        P("rows", "cols"),
        P(None, "rows"),
    )
    out_specs = (P(None, "rows", "cols"), P(None, "rows", "cols"))
    body = local_steps if (mesh.shape["rows"], mesh.shape["cols"]) == (8, 4) else local_general
    return jax.shard_map(body, mesh=mesh, in_specs=in_specs, out_specs=out_specs, check_vma=False)
```

```python
import jax
import jax.numpy as jnp
from jax import lax
from jax.experimental import pallas as pl
from jax.experimental.pallas import tpu as pltpu
from jax.sharding import PartitionSpec as P

BLOCK = 16
COARSE = 512
ITERS = 4
HALO = 8
SIDE = 7
LANES = 128
PAD = 8
LONG = 33
PART = 64
TILES = PART * COARSE // (8 * LANES)

MASS_TERM = 1.0
PRECISE = lax.Precision.HIGHEST
BOTH = ("rows", "cols")


def iota(shape, dim):
    return lax.broadcasted_iota(jnp.int32, shape, dim)


def roll(x, shift, axis):
    size = x.shape[axis]
    shift = shift % size
    return x if shift == 0 else pltpu.roll(x, shift, axis)


def lane_row():
    return iota((1, LANES), 1)


def pick_lanes(values, index):
    return jnp.take_along_axis(values, index, axis=1, mode="promise_in_bounds")


def fold_rows(plane):
    rows = plane.shape[0]
    return plane.reshape(rows // BLOCK, 2, 8, LANES).sum(axis=1)


def pack_blocks(folds):
    count = folds[0].shape[0]
    pad = (-count * len(folds)) % 8
    stacked = jnp.concatenate(folds + ([jnp.zeros((pad, LANES), jnp.float32)] if pad else []), axis=0)
    spread = iota((LANES, LANES), 0) // BLOCK == iota((LANES, LANES), 1) % (LANES // BLOCK)
    summed = jnp.dot(stacked, spread.astype(jnp.float32), precision=PRECISE)
    group = lane_row() // (LANES // BLOCK)
    row = jnp.zeros((1, LANES), jnp.float32)
    for index in range(len(folds) * count):
        row = row + jnp.where(group == index, summed[index : index + 1], 0.0)
    return row


def pack_scalars(partials, offset):
    lane = lane_row()
    row = jnp.zeros((1, LANES), jnp.float32)
    for index, partial in enumerate(partials):
        total = jnp.sum(jnp.sum(partial, axis=0, keepdims=True), axis=1, keepdims=True)
        row = row + jnp.where(lane == offset + index, total, 0.0)
    return row


def unfold(values, slot, width):
    devices = values.shape[0]
    lane = iota((devices, LANES), 1)
    part = jnp.where(lane < width, roll(values, -slot * width, 1), 0.0)
    step = width
    while step < LANES:
        part = part + roll(part, step, 1)
        step *= 2
    per_row = LANES // width
    own = jnp.where(iota((devices, LANES), 0) % per_row == lane // width, part, 0.0)
    rows = [
        jnp.sum(own[k * per_row : (k + 1) * per_row], axis=0, keepdims=True) for k in range(devices // per_row)
    ]
    return jnp.concatenate(rows, axis=0)


def coarse_solve(values, names, position, parts):
    count = COARSE // LANES
    lines = [jnp.zeros((8, LANES), jnp.float32) for _ in range(count)]
    for part, ref in enumerate(parts):
        aggregate = iota((PART, LANES), 0) + ((position ^ part) * PART + 1)
        total = jnp.zeros((PART, LANES), jnp.float32)
        for row in range(8):
            total = total + jnp.where(aggregate == names[row : row + 1], values[row : row + 1], 0.0)
        column = jnp.sum(total, axis=1, keepdims=True)
        first = ref.shape[0] - TILES
        for index in range(TILES):
            at = 8 * (index // count)
            lines[index % count] += ref[first + index] * column[at : at + 8]
    return [jnp.broadcast_to(jnp.sum(line, axis=0, keepdims=True), (8, LANES)) for line in lines]


def lookup(coarse, names):
    index = jnp.maximum(names - 1, 0)
    inner = index % LANES
    result = jnp.zeros(names.shape, jnp.float32)
    for tile, values in enumerate(coarse):
        result = jnp.where(index // LANES == tile, pick_lanes(values, inner), result)
    return jnp.where(names > 0, result, 0.0)


def apply_blocks(diag, east, south, values, grid):
    count_x, count_y, blocks_x, blocks_y = grid
    width = blocks_x * blocks_y
    lane = iota(values.shape, 1)
    row, col = iota(values.shape, 0), lane // width
    at_x, at_y = (lane % width) // blocks_y, lane % blocks_y
    last_x, last_y = at_x == blocks_x - 1, at_y == blocks_y - 1
    step_e = width - (blocks_y - 1)
    step_s = (blocks_x - 1) * blocks_y

    def take(x, inner, outer, is_outer, missing):
        return jnp.where(missing, 0.0, jnp.where(is_outer, outer(x), inner(x)))

    from_e = take(
        values, lambda x: roll(x, -1, 1), lambda x: roll(x, -step_e, 1), last_y, last_y & (col == count_y - 1)
    )
    from_w = take(
        east * values, lambda x: roll(x, 1, 1), lambda x: roll(x, step_e, 1), at_y == 0, (at_y == 0) & (col == 0)
    )
    from_s = take(
        values,
        lambda x: roll(x, -blocks_y, 1),
        lambda x: roll(roll(x, -1, 0), step_s, 1),
        last_x,
        last_x & (row == count_x - 1),
    )
    from_n = take(
        south * values,
        lambda x: roll(x, blocks_y, 1),
        lambda x: roll(roll(x, 1, 0), -step_s, 1),
        at_x == 0,
        (at_x == 0) & (row == 0),
    )
    return diag * values - east * from_e - south * from_s - from_w - from_n


def local_names(ids):
    rows = ids.shape[1]
    lane = iota((8, LANES), 1)
    at = lane % BLOCK
    starts = [0] + list(range(HALO, rows, BLOCK))
    result = jnp.zeros((8, LANES), jnp.float32)
    for index, start in enumerate(starts):
        inner = pick_lanes(ids[0, start : start + 8], (at * BLOCK) % LANES)
        outer = pick_lanes(ids[1, start : start + 8], jnp.where(at == 8, 0, LANES - 1))
        both = jnp.where(at < 8, inner, jnp.where(at < 10, outer, 0.0))
        result = jnp.where(lane // BLOCK == index, both, result)
    return result


def prolong(target, values):
    lane = iota((8, LANES), 1)
    rows = target.shape[1]
    bounds = [0] + list(range(HALO, rows, BLOCK)) + [rows]
    for index in range(len(bounds) - 1):
        main = pick_lanes(values, lane // BLOCK + index * BLOCK)
        side = pick_lanes(values, jnp.where(lane < BLOCK, 8, 9) + index * BLOCK)
        for row in range(bounds[index], bounds[index + 1], 8):
            target[0, row : row + 8] = main
            target[1, row : row + 8] = side


def band(ref, index, step=0):
    rows = ref.shape[1]
    return ref[index, PAD + step : rows - PAD + step, :]


def put(ref, index, value):
    ref[index, PAD : ref.shape[1] - PAD, :] = value


def own(ref, index, step=0):
    rows = ref.shape[1]
    return ref[index, PAD + HALO + step : rows - PAD - HALO + step, :]


def beside(main, side):
    lane = iota(main.shape, 1)
    main_e, side_e = roll(main, -1, 1), roll(side, -1, 1)
    main_w, side_w = roll(main, 1, 1), roll(side, 1, 1)
    last, first = lane == LANES - 1, lane == 0
    east = jnp.where(last, side_e, main_e), jnp.where(last, main_e, side_e)
    west = jnp.where(first, side_w, main_w), jnp.where(first, main_w, side_w)
    return east, west


class Operator:
    def __init__(self, w_layer, w_row, w_east, w_west):
        self.w_layer, self.w_row, self.w_east, self.w_west = w_layer, w_row, w_east, w_west

    def wide(self, source):
        layers = self.w_row.shape[0] // 2
        current = [band(source, k * layers) for k in range(2)]
        below = [-band(self.w_layer, k * (layers + 1)) * current[k] for k in range(2)]
        for layer in range(layers):
            last = layer == layers - 1
            after = [None if last else band(source, k * layers + layer + 1) for k in range(2)]
            east, west = beside(*current)
            result = []
            for k in range(2):
                at = k * layers + layer
                here = current[k]
                above = band(self.w_layer, k * (layers + 1) + layer + 1) * (here if last else here - after[k])
                total = MASS_TERM * here + above - below[k]
                total += band(self.w_row, at) * (here - band(source, at, 1))
                total += band(self.w_row, at, -1) * (here - band(source, at, -1))
                total += band(self.w_east, at) * (here - east[k])
                total += band(self.w_west, at) * (here - west[k])
                result.append(total)
                below[k] = above
            yield layer, result
            current = after

    def near(self, source):
        layers = self.w_row.shape[0] // 2
        here = own(source, 0)
        below = -own(self.w_layer, 0) * here
        lane = iota(here.shape, 1)
        for layer in range(layers):
            last = layer == layers - 1
            after = None if last else own(source, layer + 1)
            side = own(source, layers + layer)
            above = own(self.w_layer, layer + 1) * (here if last else here - after)
            total = MASS_TERM * here + above - below
            total += own(self.w_row, layer) * (here - own(source, layer, 1))
            total += own(self.w_row, layer, -1) * (here - own(source, layer, -1))
            east = jnp.where(lane == LANES - 1, roll(side, -1, 1), roll(here, -1, 1))
            west = jnp.where(lane == 0, roll(side, 1, 1), roll(here, 1, 1))
            total += own(self.w_east, layer) * (here - east)
            total += own(self.w_west, layer) * (here - west)
            yield layer, total
            here, below = after, above


def near(plane):
    return plane[HALO:-HALO]


def tally(plane):
    return plane.reshape(plane.shape[0] // 8, 8, LANES).sum(axis=0)


def own_ids(ids):
    blocks_x = ids.shape[0] // 2
    lines = [jnp.broadcast_to(ids[bx : bx + 1], (BLOCK, LANES)) for bx in range(blocks_x)]
    return jnp.concatenate(lines, axis=0)


def rows_kernel(position, aggregate_hbm, loading, viscosity, shard, ids, near_rows, far_rows, aggregate, sems):
    layers, rows, _ = loading.shape
    odd = position[0] % 2
    numbers = pltpu.make_async_copy(aggregate_hbm, aggregate, sems.at[4])
    numbers.start()
    copies = []
    for side, target in enumerate((near_rows, far_rows)):
        top = odd if side == 0 else 1 - odd
        at = pl.multiple_of((1 - top) * (rows - HALO), HALO)
        for k, source in enumerate((loading, viscosity)):
            copies.append(
                pltpu.make_async_copy(
                    source.at[:, pl.ds(at, HALO), :],
                    target.at[pl.ds(k * layers, layers)],
                    sems.at[2 * side + k],
                )
            )
    copies.append(pltpu.make_async_copy(shard, near_rows.at[pl.ds(2 * layers + 1, TILES)], sems.at[5]))
    for copy in copies:
        copy.start()
    numbers.wait()
    blocks_x, blocks_y = aggregate.shape
    lane = lane_row()
    flat = jnp.zeros((1, LANES), jnp.float32)
    for bx in range(blocks_x):
        names = jnp.zeros((1, LANES), jnp.float32)
        for by in range(blocks_y):
            name = (aggregate[bx, by] + 1).astype(jnp.float32)
            names = jnp.where(lane // BLOCK == by, name, names)
            flat = jnp.where(lane % (blocks_x * blocks_y) == bx * blocks_y + by, name, flat)
        ids[bx : bx + 1] = names
    ids[blocks_x:] = jnp.broadcast_to(flat, (ids.shape[0] - blocks_x, LANES))
    first, last = ids[0:1], ids[blocks_x - 1 : blocks_x]
    near_rows[2 * layers] = jnp.broadcast_to(jnp.where(odd == 1, first, last), (HALO, LANES))
    far_rows[2 * layers] = jnp.broadcast_to(jnp.where(odd == 1, last, first), (HALO, LANES))
    for copy in copies:
        copy.wait()


def tall_plane(slot, own, odd, near_rows, far_rows):
    low = jnp.where(odd == 1, near_rows[slot], far_rows[slot])
    high = jnp.where(odd == 1, far_rows[slot], near_rows[slot])
    return jnp.concatenate([low, own, high], axis=0)


def edge_kernel(position, loading, viscosity, own_names, near_rows, far_rows, near_cols, far_cols, message):
    layers = loading.shape[0]
    odd = position[0] % 2
    lane = lane_row()
    tall = loading.shape[1] + 2 * HALO
    right = left = jnp.zeros((tall, LANES), jnp.float32)
    for slot in range(2 * layers + 1):
        if slot < layers:
            own = loading[slot]
        elif slot < 2 * layers:
            own = viscosity[slot - layers]
        else:
            own = own_ids(own_names)
        plane = tall_plane(slot, own, odd, near_rows, far_rows)
        at = slot * SIDE
        here = (lane >= at) & (lane < at + SIDE)
        right = jnp.where(here, roll(plane, at + SIDE, 1), right)
        left = jnp.where(here, roll(plane, at, 1), left)
    odd_col = position[1] % 2
    near_cols[:tall] = jnp.where(odd_col == 1, left, right)
    far_cols[:tall] = jnp.where(odd_col == 1, right, left)
    blocks_x, width = own_names.shape[0] // 2, own_names.shape[0] // 2 * (LANES // BLOCK)
    fold = jnp.zeros((blocks_x, 8, LANES), jnp.float32)
    for layer in range(layers):
        fold = fold + fold_rows(loading[layer])
    line = pack_blocks([fold.sum(axis=1)])
    line = line + jnp.where((lane >= width) & (lane < 2 * width), own_names[blocks_x : blocks_x + 1], 0.0)
    message[...] = jnp.broadcast_to(line, message.shape)


def start_kernel(
    position, loading, viscosity, own_names, near_rows, far_rows, near_cols, far_cols, arrived, *rest
):
    parts = rest[:8]
    resid, direction, image, inverse, w_layer, w_row, w_east, w_west, names_out, lifted_blocks, message = rest[8:19]
    wide, ids, scaled_image, rise = rest[19:]
    layers = loading.shape[0]
    blocks_x, blocks_y = loading.shape[1] // BLOCK, LANES // BLOCK
    width = blocks_x * blocks_y
    odd, odd_col = position[0] % 2, position[1] % 2
    lane = lane_row()
    tall = loading.shape[1] + 2 * HALO
    from_west = jnp.where(odd_col == 1, near_cols[:tall], far_cols[:tall])
    from_east = jnp.where(odd_col == 1, far_cols[:tall], near_cols[:tall])

    def widen(slot, cells):
        at = slot * SIDE
        beyond = jnp.where(lane < SIDE, roll(from_east, -at, 1), 0.0)
        beyond = jnp.where(lane >= LANES - SIDE, roll(from_west, LANES - SIDE - at, 1), beyond)
        return tall_plane(slot, cells, odd, near_rows, far_rows), beyond

    for layer in range(layers):
        for k, tile in enumerate(widen(layer, loading[layer])):
            put(resid, k * layers + layer, tile)
        for k, tile in enumerate(widen(layers + layer, viscosity[layer])):
            put(wide, k * layers + layer, tile)
    ids[0], ids[1] = widen(2 * layers, own_ids(own_names))
    names_out[...] = local_names(ids)

    sums = arrived[...]
    names = unfold(sums, 1, width).astype(jnp.int32)
    solved = coarse_solve(unfold(sums, 0, width), names, position[0], parts)
    lifted_blocks[...] = lookup(solved, names)
    prolong(rise, lookup(solved, names_out[...].astype(jnp.int32)))

    for layer in range(layers):
        east, west = beside(band(wide, layer), band(wide, layers + layer))
        for k in range(2):
            at, face = k * layers + layer, k * (layers + 1) + layer
            visc = band(wide, at)
            before = 0.5 * (visc if layer == 0 else visc + band(wide, at - 1))
            after = 0.5 * (visc if layer == layers - 1 else visc + band(wide, at + 1))
            down, up = 0.5 * (visc + band(wide, at, 1)), 0.5 * (visc + band(wide, at, -1))
            right, left = 0.5 * (visc + east[k]), 0.5 * (visc + west[k])
            if layer == 0:
                put(w_layer, face, before)
            put(w_layer, face + 1, after)
            put(w_row, at, down)
            put(w_east, at, right)
            put(w_west, at, left)
            diagonal = MASS_TERM + before + after + up + down + left + right
            part = jnp.where(visc > 0.0, 1.0 / diagonal, 0.0)
            put(inverse, at, part)
            put(direction, at, part * band(resid, at) + rise[k])
    folds_own, folds_east, folds_south = block_matrix(w_layer, w_row, w_east, w_west)

    operator = Operator(w_layer, w_row, w_east, w_west)
    zero = jnp.zeros((8, LANES), jnp.float32)
    folds = [jnp.zeros((blocks_x, 8, LANES), jnp.float32) for _ in range(2)]
    s_rp = s_rd = s_dq = s_eq = s_pq = s_ee = zero
    for layer, planes in operator.wide(direction):
        for k, plane in enumerate(planes):
            at = k * layers + layer
            put(image, at, plane)
            put(scaled_image, at, band(inverse, at) * plane)
        q, r, p, v = near(planes[0]), own(resid, layer), own(direction, layer), own(inverse, layer)
        d, e = v * r, v * q
        s_rp += tally(r * p)
        s_rd += tally(r * d)
        s_dq += tally(d * q)
        s_eq += tally(e * q)
        s_pq += tally(p * q)
        folds[0] += fold_rows(q)
    for layer, image_e in operator.near(scaled_image):
        s_ee += tally(image_e * own(scaled_image, layer))
        folds[1] += fold_rows(image_e)
    upper = pack_blocks([fold.sum(axis=1) for fold in folds])
    upper = upper + pack_scalars([s_rp, s_rd, s_dq, s_eq, s_pq, s_ee], 3 * width)
    lower = pack_blocks([folds_own, folds_east, folds_south])
    write_message(message, upper, lower)


def write_message(message, upper, lower):
    rows = iota(message.shape, 0)
    message[...] = jnp.where(rows % 2 == 0, upper, lower)


def block_matrix(w_layer, w_row, w_east, w_west):
    layers = w_row.shape[0] // 2
    rows = w_row.shape[1]
    lane = lane_row()
    east = west = jnp.zeros((rows - 2 * (PAD + HALO), LANES), jnp.float32)
    line = jnp.zeros((rows, LANES), jnp.float32)
    for layer in range(layers):
        east = east + own(w_east, layer)
        west = west + own(w_west, layer)
        line = line + w_row[layer]
    own_cells = fold_rows(own(w_layer, 0) + own(w_layer, layers)).sum(axis=1)
    east_face = fold_rows(jnp.where(lane % BLOCK == BLOCK - 1, east, 0.0)).sum(axis=1)
    west_face = fold_rows(jnp.where(lane % BLOCK == 0, west, 0.0)).sum(axis=1)
    count = own_cells.shape[0]
    first = PAD + HALO - 1
    faces = [line[first + BLOCK * k : first + BLOCK * k + 1] for k in range(count + 1)]
    north_face, south_face = jnp.concatenate(faces[:-1], axis=0), jnp.concatenate(faces[1:], axis=0)
    mass = jnp.full((count, LANES), MASS_TERM * layers * BLOCK, jnp.float32)
    total = mass + own_cells + east_face + west_face + south_face + north_face
    return total, east_face, south_face


def lane_total(values, lane_at):
    return jnp.sum(values[:, lane_at : lane_at + 1], axis=0, keepdims=True)


def dot_blocks(left, right):
    return jnp.sum(jnp.sum(left * right, axis=0, keepdims=True), axis=1, keepdims=True)


def received(ref, parity):
    return ref[pl.ds(parity, ref.shape[0] // 2, stride=2), :]


def write_scalars(ref, values):
    lane = lane_row()
    line = jnp.zeros((1, LANES), jnp.float32)
    for index, value in enumerate(values):
        line = jnp.where(lane == index, value, line)
    ref[...] = jnp.broadcast_to(line, ref.shape)


def middle_kernel(grid, position, arrived0, arrived, names_ref, lifted0_ref, *rest):
    parts = rest[:8]
    resid0, direction0, image0, inverse, w_layer, w_row, w_east, w_west = rest[8:16]
    resid, lifted, direction, image, lifted_image, scalars, lifted_blocks, message = rest[16:24]
    scaled_image, scaled_lifted, rise_0, rise_1 = rest[24:]
    width = grid[2] * grid[3]
    layers = resid.shape[0] // 2
    sums = arrived0[...]
    names = unfold(sums, 1, width).astype(jnp.int32)
    here = names_ref[...].astype(jnp.int32)
    upper, lower = received(arrived, 0), received(arrived, 1)
    s_rp, s_rd, s_dq, s_eq, s_pq, s_ee = [lane_total(upper, 3 * width + k) for k in range(6)]
    r_q, r_e = [unfold(upper, k, width) for k in range(2)]
    diag, east, south = [unfold(lower, k, width) for k in range(3)]
    lifted0 = lifted0_ref[...]
    r_d = r_q - apply_blocks(diag, east, south, lifted0, grid)
    s_dd = s_dq - dot_blocks(lifted0, r_d)
    s_de = s_eq - dot_blocks(lifted0, r_e)
    alpha0 = s_rp / s_pq
    scaled_sum = s_rd - 2.0 * alpha0 * s_dq + alpha0 * alpha0 * s_eq
    coarse1 = unfold(sums, 0, width) - alpha0 * r_q
    solved = coarse_solve(coarse1, names, position[0], parts)
    lifted1 = lookup(solved, names)
    prolong(rise_0, lookup(solved, here))
    inner1 = scaled_sum + dot_blocks(coarse1, lifted1)
    beta0 = inner1 / s_rp
    r_x = r_d - alpha0 * r_e + beta0 * r_q
    energy = (
        s_dd
        - 2.0 * alpha0 * s_de
        + alpha0 * alpha0 * s_ee
        + 2.0 * beta0 * (s_dq - alpha0 * s_eq)
        + beta0 * beta0 * s_pq
    )
    block_image = apply_blocks(diag, east, south, lifted1, grid)
    alpha1 = inner1 / (energy + dot_blocks(lifted1, 2.0 * r_x + block_image))
    coarse2 = coarse1 - alpha1 * (r_x + block_image)
    solved = coarse_solve(coarse2, names, position[0], parts)
    lifted_blocks[...] = lookup(solved, names)
    prolong(rise_1, lookup(solved, here))
    write_scalars(scalars, [alpha0, alpha1, inner1])

    operator = Operator(w_layer, w_row, w_east, w_west)
    for at in range(2 * layers):
        after = band(resid0, at) - alpha0 * band(image0, at)
        put(resid, at, after)
        put(direction, at, band(inverse, at) * after + rise_0[at // layers] + beta0 * band(direction0, at))
    zero = jnp.zeros((8, LANES), jnp.float32)
    folds = [jnp.zeros((grid[2], 8, LANES), jnp.float32) for _ in range(5)]
    s_rz = s_rd = s_zu = s_zq = s_pq = s_du = s_dq = s_us = s_uw = s_qw = zero
    s_ss = s_sw = s_ww = zero
    for layer, planes in operator.wide(direction):
        for k, plane in enumerate(planes):
            at = k * layers + layer
            put(image, at, plane)
            after = band(resid, at) - alpha1 * plane
            put(resid, at, after)
            put(lifted, at, band(inverse, at) * after + rise_1[k])
            put(scaled_image, at, band(inverse, at) * plane)
        q, r, p, v = near(planes[0]), own(resid, layer), own(direction, layer), own(inverse, layer)
        d, z, w = v * r, own(lifted, layer), v * q
        s_rz += tally(r * z)
        s_rd += tally(r * d)
        s_zq += tally(z * q)
        s_pq += tally(p * q)
        s_dq += tally(d * q)
        s_qw += tally(q * w)
        folds[1] += fold_rows(q)
        folds[4] += fold_rows(r)
    for layer, planes in operator.wide(lifted):
        for k, plane in enumerate(planes):
            at = k * layers + layer
            put(lifted_image, at, plane)
            put(scaled_lifted, at, band(inverse, at) * plane)
        u = near(planes[0])
        v = own(inverse, layer) * u
        s_zu += tally(u * own(lifted, layer))
        s_du += tally(v * own(resid, layer))
        s_us += tally(u * v)
        s_uw += tally(u * own(scaled_image, layer))
        folds[0] += fold_rows(u)
    for layer, image_s in operator.near(scaled_lifted):
        s_ss += tally(image_s * own(scaled_lifted, layer))
        s_sw += tally(image_s * own(scaled_image, layer))
        folds[2] += fold_rows(image_s)
    for layer, image_w in operator.near(scaled_image):
        s_ww += tally(image_w * own(scaled_image, layer))
        folds[3] += fold_rows(image_w)
    lines = [fold.sum(axis=1) for fold in folds]
    upper = pack_blocks(lines[:4])
    lower = pack_blocks(lines[4:]) + pack_scalars(
        [s_rz, s_rd, s_zu, s_zq, s_pq, s_du, s_dq, s_us, s_uw, s_qw, s_ss, s_sw, s_ww],
        width,
    )
    write_message(message, upper, lower)


def last_kernel(grid, position, arrived0, before, arrived, names_ref, scalars, lifted2_ref, *rest):
    parts = rest[:8]
    resid, lifted, direction1, image1, lifted_image, direction0, inverse, w_layer, w_row, w_east, w_west = rest[8:19]
    outs = rest[19:21]
    direction, rise_3, answer, out_resid, sems = rest[21:]
    width = grid[2] * grid[3]
    layers = resid.shape[0] // 2
    names = unfold(arrived0[...], 1, width).astype(jnp.int32)
    here = names_ref[...].astype(jnp.int32)
    blocks = received(before, 1)
    diag, east, south = [unfold(blocks, k, width) for k in range(3)]
    upper, lower = received(arrived, 0), received(arrived, 1)
    r_u, r_q, r_s, r_w = [unfold(upper, k, width) for k in range(4)]
    r_r = unfold(lower, 0, width)
    s_rz, s_rd, s_zu, s_zq, s_pq, s_du, s_dq, s_us, s_uw, s_qw, s_ss, s_sw, s_ww = [
        lane_total(lower, width + k) for k in range(13)
    ]
    lifted2 = lifted2_ref[...]
    r_d = r_u - apply_blocks(diag, east, south, lifted2, grid)
    s_dd = s_du - dot_blocks(lifted2, r_d)
    s_ds = s_us - dot_blocks(lifted2, r_s)
    s_dw = s_uw - dot_blocks(lifted2, r_w)
    alpha0, alpha1, inner1 = [scalars[0:1, k : k + 1] for k in range(3)]
    inner2 = s_rz
    beta1 = inner2 / inner1
    alpha2 = inner2 / (s_zu + 2.0 * beta1 * s_zq + beta1 * beta1 * s_pq)
    coarse3 = r_r - alpha2 * (r_u + beta1 * r_q)
    solved = coarse_solve(coarse3, names, position[0], parts)
    lifted3 = lookup(solved, names)
    prolong(rise_3, lookup(solved, here))
    scaled_sum = (
        s_rd
        - 2.0 * alpha2 * (s_du + beta1 * s_dq)
        + alpha2 * alpha2 * (s_us + 2.0 * beta1 * s_uw + beta1 * beta1 * s_qw)
    )
    inner3 = scaled_sum + dot_blocks(coarse3, lifted3)
    beta2 = inner3 / inner2
    rise = lifted3 + beta2 * lifted2
    k_d, k_s, k_w, k_p = 1.0 + beta2, -alpha2, -alpha2 * beta1, beta2 * beta1
    energy = (
        k_d * k_d * s_dd
        + k_s * k_s * s_ss
        + k_w * k_w * s_ww
        + k_p * k_p * s_pq
        + 2.0 * (k_d * (k_s * s_ds + k_w * s_dw + k_p * s_dq) + k_s * (k_w * s_sw + k_p * s_uw) + k_w * k_p * s_qw)
    )
    r_x = k_d * r_d + k_s * r_s + k_w * r_w + k_p * r_q
    block_image = apply_blocks(diag, east, south, rise, grid)
    alpha3 = inner3 / (energy + dot_blocks(rise, 2.0 * r_x + block_image))

    for at in range(2 * layers):
        direction2 = band(lifted, at) + beta1 * band(direction1, at)
        after = band(resid, at) - alpha2 * (band(lifted_image, at) + beta1 * band(image1, at))
        step = band(inverse, at) * after + rise_3[at // layers] + beta2 * direction2
        put(direction, at, step)
        if at < layers:
            out_resid[at] = near(after)
            answer[at] = (
                alpha0 * own(direction0, at)
                + alpha1 * own(direction1, at)
                + alpha2 * near(direction2)
                + alpha3 * near(step)
            )
    copies = [pltpu.make_async_copy(answer, outs[0], sems.at[layers])]
    copies[0].start()
    for layer, plane in Operator(w_layer, w_row, w_east, w_west).near(direction):
        out_resid[layer] = out_resid[layer] - alpha3 * plane
        copies.append(pltpu.make_async_copy(out_resid.at[layer], outs[1].at[layer], sems.at[layer]))
        copies[-1].start()
    for copy in copies:
        copy.wait()


def call(kernel, outs, scratch, name, smem, *operands, spaces=None, out_space=pltpu.VMEM):
    whole = pl.BlockSpec(memory_space=pltpu.VMEM)
    scalar = pl.BlockSpec(memory_space=pltpu.SMEM)
    specs = [scalar] * smem + [whole] * (len(operands) - smem)
    operands = list(operands)
    for index in spaces or ():
        specs[index] = pl.BlockSpec(memory_space=pltpu.HBM)
        operands[index] = pltpu.with_memory_space_constraint(operands[index], pltpu.HBM)
    return pl.pallas_call(
        kernel,
        out_shape=[jax.ShapeDtypeStruct(shape, jnp.float32) for shape in outs],
        in_specs=specs,
        out_specs=[pl.BlockSpec(memory_space=out_space)] * len(outs),
        scratch_shapes=[pltpu.VMEM(s, jnp.float32) if isinstance(s, tuple) else s for s in scratch],
        compiler_params=pltpu.CompilerParams(vmem_limit_bytes=20 * 1024 * 1024),
        name=name,
    )(*operands)


def exchange(message):
    return lax.all_to_all(message, BOTH, 0, 0, tiled=True)


def pair(values, axis, mask):
    return lax.ppermute(values, axis, [(i, i ^ mask) for i in range(lax.axis_size(axis))])


def pair_far(values, axis):
    count = lax.axis_size(axis)
    return lax.ppermute(values, axis, [(i, i + 1 if i % 2 else i - 1) for i in range(1, count - 1)])


def local_steps(loading, viscosity, aggregate, coarse_inverse):
    layers, cells_x, cells_y = loading.shape
    blocks_x, blocks_y = aggregate.shape
    count_x, count_y = lax.axis_size("rows"), lax.axis_size("cols")
    devices = count_x * count_y
    grid = (count_x, count_y, blocks_x, blocks_y)
    position = jnp.stack([lax.axis_index(axis).astype(jnp.int32) for axis in BOTH])
    tall = cells_x + 2 * HALO
    edge = (2 * layers + 1, HALO, LANES)
    shard = coarse_inverse.T.reshape(PART // 8, 8, COARSE // LANES, LANES)
    shard = shard.transpose(0, 2, 1, 3).reshape(TILES, 8, LANES)
    parts = [pair(shard, "rows", mask) for mask in (2, 4, 6)]

    ids, near_out, far_rows = call(
        rows_kernel,
        [(8, LANES), (edge[0] + TILES, 8, LANES), (LONG, 8, LANES)],
        [pltpu.SMEM(aggregate.shape, jnp.int32), pltpu.SemaphoreType.DMA((6,))],
        "rows",
        1,
        position,
        aggregate,
        loading,
        viscosity,
        shard,
        spaces=(1, 2, 3, 4),
    )
    own = (position, loading, viscosity, ids)
    near_rows, far_rows = pair(near_out, "rows", 1), pair_far(far_rows, "rows")
    near_cols, far_cols, message0 = call(
        edge_kernel, [(8 * LONG, LANES)] * 2 + [(devices, LANES)], [], "edges", 1, *own, near_rows, far_rows
    )
    near_cols, far_cols = pair(near_cols, "cols", 1), pair_far(far_cols, "cols")
    parts = [part for both in ((part, pair(part, "rows", 1)) for part in parts) for part in both]
    parts = [near_out, near_rows] + parts
    arrived0 = exchange(message0)
    parts, arrived0 = lax.optimization_barrier((parts, arrived0))
    field = (2 * layers, tall + 2 * PAD, LANES)
    taller = (2 * (layers + 1), tall + 2 * PAD, LANES)
    plane = (2, tall, LANES)
    message = (2 * devices, LANES)
    line = (8, LANES)
    resid, direction0, image0, inverse, w_layer, w_row, w_east, w_west, names, lifted_blocks, message1 = call(
        start_kernel,
        [field] * 4 + [taller, field, field, field, line, line, message],
        [field, plane, field, plane],
        "start",
        1,
        *own,
        near_rows,
        far_rows,
        near_cols,
        far_cols,
        arrived0,
        *parts,
    )
    weights = (inverse, w_layer, w_row, w_east, w_west)
    arrived1 = exchange(message1)
    resid, lifted, direction1, image1, lifted_image, scalars, lifted_blocks, message2 = call(
        lambda *refs: middle_kernel(grid, *refs),
        [field] * 5 + [line, line, message],
        [field] * 2 + [plane] * 2,
        "middle",
        1,
        position,
        arrived0,
        arrived1,
        names,
        lifted_blocks,
        *parts,
        resid,
        direction0,
        image0,
        *weights,
    )
    arrived2 = exchange(message2)
    return call(
        lambda *refs: last_kernel(grid, *refs),
        [loading.shape] * 2,
        [field, plane, loading.shape, loading.shape, pltpu.SemaphoreType.DMA((layers + 1,))],
        "last",
        1,
        position,
        arrived0,
        arrived1,
        arrived2,
        names,
        scalars,
        lifted_blocks,
        *parts,
        resid,
        lifted,
        direction1,
        image1,
        lifted_image,
        direction0,
        *weights,
        out_space=pltpu.HBM,
    )


def from_sides(block, axis, dim, width):
    count = lax.axis_size(axis)
    forward = [(i, i + 1) for i in range(count - 1)]
    backward = [(target, source) for source, target in forward]
    size = block.shape[dim]
    low = lax.ppermute(lax.slice_in_dim(block, size - width, size, axis=dim), axis, forward)
    high = lax.ppermute(lax.slice_in_dim(block, 0, width, axis=dim), axis, backward)
    return low, high


def widened(block, width_x, width_y):
    low, high = from_sides(block, "rows", block.ndim - 2, width_x)
    block = jnp.concatenate([low, block, high], axis=-2)
    turned = jnp.swapaxes(block, -1, -2)
    low, high = from_sides(turned, "cols", turned.ndim - 2, width_y)
    low, high = jnp.swapaxes(low, -1, -2), jnp.swapaxes(high, -1, -2)
    return jnp.concatenate([low, block, high], axis=-1)


def all_sum(values):
    count = lax.axis_size("rows") * lax.axis_size("cols")
    if count > 64:
        return lax.psum(lax.psum(values, "cols"), "rows")
    spread = jnp.broadcast_to(values[None], (count,) + values.shape)
    return lax.all_to_all(spread, BOTH, 0, 0).sum(axis=0)


def shifted(field, axis, step):
    return jnp.roll(field, step, axis=axis)


def local_general(loading, viscosity, aggregate, coarse_inverse):
    layers, cells_x, cells_y = loading.shape
    blocks_x, blocks_y = aggregate.shape
    ids = jnp.arange(COARSE, dtype=jnp.int32)
    whole_matrix = lax.all_gather(coarse_inverse, "rows", axis=1, tiled=True)
    fields = widened(jnp.stack([loading, viscosity]), HALO, HALO)
    wide_aggregate = widened(aggregate + 1, 1, 1) - 1
    table = (aggregate.reshape(-1)[:, None] == ids[None, :]).astype(jnp.float32)
    wide_table = (wide_aggregate.reshape(-1)[:, None] == ids[None, :]).astype(jnp.float32)

    residual, visc = fields[0], fields[1]
    inside = visc > 0.0
    pads = ((1, 1), (0, 0), (0, 0))
    padded = jnp.pad(visc, pads)
    weights = [
        0.5 * (visc + padded[:-2]),
        0.5 * (visc + padded[2:]),
        0.5 * (visc + shifted(visc, 1, 1)),
        0.5 * (visc + shifted(visc, 1, -1)),
        0.5 * (visc + shifted(visc, 2, 1)),
        0.5 * (visc + shifted(visc, 2, -1)),
    ]
    diagonal = MASS_TERM + sum(weights)
    inverse = jnp.where(inside, 1.0 / diagonal, 0.0)

    def operate(field):
        layered = jnp.pad(field, pads)
        sides = [
            layered[:-2],
            layered[2:],
            shifted(field, 1, 1),
            shifted(field, 1, -1),
            shifted(field, 2, 1),
            shifted(field, 2, -1),
        ]
        total = MASS_TERM * field
        for weight, side in zip(weights, sides):
            total = total + weight * (field - side)
        return total

    def inner_part(field):
        return field[:, HALO:-HALO, HALO:-HALO]

    def restrict(field):
        blocks = field.reshape(layers, blocks_x, BLOCK, blocks_y, BLOCK).sum(axis=(0, 2, 4))
        return jnp.dot(blocks.reshape(-1), table, precision=PRECISE).reshape(4, COARSE // 4)

    def prolong(values):
        per_block = jnp.dot(wide_table, values.reshape(-1), precision=PRECISE)
        per_block = per_block.reshape(blocks_x + 2, blocks_y + 2)
        spread = jnp.repeat(jnp.repeat(per_block, BLOCK, axis=0), BLOCK, axis=1)
        cut = BLOCK - HALO
        return spread[cut:-cut, cut:-cut][None]

    def coarse_apply(coarse):
        return jnp.dot(whole_matrix, coarse.reshape(-1), precision=PRECISE).reshape(coarse.shape)

    def scalars(*values):
        return jnp.stack([jnp.broadcast_to(v, (COARSE // 4,)) for v in values])

    coarse = all_sum(restrict(loading))
    lifted = coarse_apply(coarse)
    direction = inverse * residual + prolong(lifted)
    answer = jnp.zeros_like(loading)
    scaled_sum = inner_now = None
    for iteration in range(ITERS):
        image = operate(direction)
        near_image, near_scaled = inner_part(image), inner_part(inverse * image)
        near_direction, near_residual = inner_part(direction), inner_part(residual)
        packed = jnp.concatenate(
            [
                restrict(near_image),
                scalars(
                    jnp.sum(near_direction * near_image),
                    jnp.sum(near_residual * near_scaled),
                    jnp.sum(near_image * near_scaled),
                    jnp.sum(near_residual * inner_part(inverse) * near_residual),
                ),
            ]
        )
        packed = all_sum(packed)
        curvature, cross, square = packed[4, 0], packed[5, 0], packed[6, 0]
        if scaled_sum is None:
            scaled_sum = packed[7, 0]
            inner_now = scaled_sum + jnp.sum(coarse * lifted)
        alpha = inner_now / curvature
        answer = answer + alpha * near_direction
        residual = residual - alpha * image
        if iteration + 1 < ITERS:
            coarse = coarse - alpha * packed[:4]
            scaled_sum = scaled_sum - 2.0 * alpha * cross + alpha * alpha * square
            lifted = coarse_apply(coarse)
            inner_next = scaled_sum + jnp.sum(coarse * lifted)
            direction = inverse * residual + prolong(lifted) + inner_next / inner_now * direction
            inner_now = inner_next
    return answer, inner_part(residual)


def solution(mesh):
    in_specs = (
        P(None, "rows", "cols"),
        P(None, "rows", "cols"),
        P("rows", "cols"),
        P(None, "rows"),
    )
    out_specs = (P(None, "rows", "cols"), P(None, "rows", "cols"))
    body = local_steps if (mesh.shape["rows"], mesh.shape["cols"]) == (8, 4) else local_general
    return jax.shard_map(body, mesh=mesh, in_specs=in_specs, out_specs=out_specs, check_vma=False)
```

```python
import jax
import jax.numpy as jnp
from jax import lax
from jax.experimental import pallas as pl
from jax.experimental.pallas import tpu as pltpu
from jax.sharding import PartitionSpec as P

BLOCK = 16
COARSE = 512
ITERS = 4
HALO = 8
SIDE = 7
LANES = 128
PAD = 8
LONG = 33
PART = 64
TILES = PART * COARSE // (8 * LANES)

MASS_TERM = 1.0
PRECISE = lax.Precision.HIGHEST
BOTH = ("rows", "cols")


def iota(shape, dim):
    return lax.broadcasted_iota(jnp.int32, shape, dim)


def roll(x, shift, axis):
    size = x.shape[axis]
    shift = shift % size
    return x if shift == 0 else pltpu.roll(x, shift, axis)


def lane_row():
    return iota((1, LANES), 1)


def pick_lanes(values, index):
    return jnp.take_along_axis(values, index, axis=1, mode="promise_in_bounds")


def fold_rows(plane):
    rows = plane.shape[0]
    return plane.reshape(rows // BLOCK, 2, 8, LANES).sum(axis=1)


def pack_blocks(folds):
    count = folds[0].shape[0]
    pad = (-count * len(folds)) % 8
    stacked = jnp.concatenate(folds + ([jnp.zeros((pad, LANES), jnp.float32)] if pad else []), axis=0)
    spread = iota((LANES, LANES), 0) // BLOCK == iota((LANES, LANES), 1) % (LANES // BLOCK)
    summed = jnp.dot(stacked, spread.astype(jnp.float32), precision=PRECISE)
    group = lane_row() // (LANES // BLOCK)
    row = jnp.zeros((1, LANES), jnp.float32)
    for index in range(len(folds) * count):
        row = row + jnp.where(group == index, summed[index : index + 1], 0.0)
    return row


def pack_scalars(partials, offset):
    lane = lane_row()
    row = jnp.zeros((1, LANES), jnp.float32)
    for index, partial in enumerate(partials):
        total = jnp.sum(jnp.sum(partial, axis=0, keepdims=True), axis=1, keepdims=True)
        row = row + jnp.where(lane == offset + index, total, 0.0)
    return row


def unfold(values, slot, width):
    devices = values.shape[0]
    lane = iota((devices, LANES), 1)
    part = jnp.where(lane < width, roll(values, -slot * width, 1), 0.0)
    step = width
    while step < LANES:
        part = part + roll(part, step, 1)
        step *= 2
    per_row = LANES // width
    own = jnp.where(iota((devices, LANES), 0) % per_row == lane // width, part, 0.0)
    rows = [
        jnp.sum(own[k * per_row : (k + 1) * per_row], axis=0, keepdims=True) for k in range(devices // per_row)
    ]
    return jnp.concatenate(rows, axis=0)


def coarse_solve(values, names, position, parts):
    count = COARSE // LANES
    lines = [jnp.zeros((8, LANES), jnp.float32) for _ in range(count)]
    for part, ref in enumerate(parts):
        aggregate = iota((PART, LANES), 0) + ((position ^ part) * PART + 1)
        total = jnp.zeros((PART, LANES), jnp.float32)
        for row in range(8):
            total = total + jnp.where(aggregate == names[row : row + 1], values[row : row + 1], 0.0)
        column = jnp.sum(total, axis=1, keepdims=True)
        first = ref.shape[0] - TILES
        for index in range(TILES):
            at = 8 * (index // count)
            lines[index % count] += ref[first + index] * column[at : at + 8]
    return [jnp.broadcast_to(jnp.sum(line, axis=0, keepdims=True), (8, LANES)) for line in lines]


def lookup(coarse, names):
    index = jnp.maximum(names - 1, 0)
    inner = index % LANES
    result = jnp.zeros(names.shape, jnp.float32)
    for tile, values in enumerate(coarse):
        result = jnp.where(index // LANES == tile, pick_lanes(values, inner), result)
    return jnp.where(names > 0, result, 0.0)


def apply_blocks(diag, east, south, values, grid):
    count_x, count_y, blocks_x, blocks_y = grid
    width = blocks_x * blocks_y
    lane = iota(values.shape, 1)
    row, col = iota(values.shape, 0), lane // width
    at_x, at_y = (lane % width) // blocks_y, lane % blocks_y
    last_x, last_y = at_x == blocks_x - 1, at_y == blocks_y - 1
    step_e = width - (blocks_y - 1)
    step_s = (blocks_x - 1) * blocks_y

    def take(x, inner, outer, is_outer, missing):
        return jnp.where(missing, 0.0, jnp.where(is_outer, outer(x), inner(x)))

    from_e = take(
        values, lambda x: roll(x, -1, 1), lambda x: roll(x, -step_e, 1), last_y, last_y & (col == count_y - 1)
    )
    from_w = take(
        east * values, lambda x: roll(x, 1, 1), lambda x: roll(x, step_e, 1), at_y == 0, (at_y == 0) & (col == 0)
    )
    from_s = take(
        values,
        lambda x: roll(x, -blocks_y, 1),
        lambda x: roll(roll(x, -1, 0), step_s, 1),
        last_x,
        last_x & (row == count_x - 1),
    )
    from_n = take(
        south * values,
        lambda x: roll(x, blocks_y, 1),
        lambda x: roll(roll(x, 1, 0), -step_s, 1),
        at_x == 0,
        (at_x == 0) & (row == 0),
    )
    return diag * values - east * from_e - south * from_s - from_w - from_n


def local_names(ids):
    rows = ids.shape[1]
    lane = iota((8, LANES), 1)
    at = lane % BLOCK
    starts = [0] + list(range(HALO, rows, BLOCK))
    result = jnp.zeros((8, LANES), jnp.float32)
    for index, start in enumerate(starts):
        inner = pick_lanes(ids[0, start : start + 8], (at * BLOCK) % LANES)
        outer = pick_lanes(ids[1, start : start + 8], jnp.where(at == 8, 0, LANES - 1))
        both = jnp.where(at < 8, inner, jnp.where(at < 10, outer, 0.0))
        result = jnp.where(lane // BLOCK == index, both, result)
    return result


def prolong(target, values):
    lane = iota((8, LANES), 1)
    rows = target.shape[1]
    bounds = [0] + list(range(HALO, rows, BLOCK)) + [rows]
    for index in range(len(bounds) - 1):
        main = pick_lanes(values, lane // BLOCK + index * BLOCK)
        side = pick_lanes(values, jnp.where(lane < BLOCK, 8, 9) + index * BLOCK)
        for row in range(bounds[index], bounds[index + 1], 8):
            target[0, row : row + 8] = main
            target[1, row : row + 8] = side


def band(ref, index, step=0):
    rows = ref.shape[1]
    return ref[index, PAD + step : rows - PAD + step, :]


def put(ref, index, value):
    ref[index, PAD : ref.shape[1] - PAD, :] = value


def own(ref, index, step=0):
    rows = ref.shape[1]
    return ref[index, PAD + HALO + step : rows - PAD - HALO + step, :]


def beside(main, side):
    lane = iota(main.shape, 1)
    main_e, side_e = roll(main, -1, 1), roll(side, -1, 1)
    main_w, side_w = roll(main, 1, 1), roll(side, 1, 1)
    last, first = lane == LANES - 1, lane == 0
    east = jnp.where(last, side_e, main_e), jnp.where(last, main_e, side_e)
    west = jnp.where(first, side_w, main_w), jnp.where(first, main_w, side_w)
    return east, west


class Operator:
    def __init__(self, w_layer, w_row, w_east, w_west):
        self.w_layer, self.w_row, self.w_east, self.w_west = w_layer, w_row, w_east, w_west

    def wide(self, source):
        layers = self.w_row.shape[0] // 2
        current = [band(source, k * layers) for k in range(2)]
        below = [-band(self.w_layer, k * (layers + 1)) * current[k] for k in range(2)]
        for layer in range(layers):
            last = layer == layers - 1
            after = [None if last else band(source, k * layers + layer + 1) for k in range(2)]
            east, west = beside(*current)
            result = []
            for k in range(2):
                at = k * layers + layer
                here = current[k]
                above = band(self.w_layer, k * (layers + 1) + layer + 1) * (here if last else here - after[k])
                total = MASS_TERM * here + above - below[k]
                total += band(self.w_row, at) * (here - band(source, at, 1))
                total += band(self.w_row, at, -1) * (here - band(source, at, -1))
                total += band(self.w_east, at) * (here - east[k])
                total += band(self.w_west, at) * (here - west[k])
                result.append(total)
                below[k] = above
            yield layer, result
            current = after

    def near(self, source):
        layers = self.w_row.shape[0] // 2
        here = own(source, 0)
        below = -own(self.w_layer, 0) * here
        lane = iota(here.shape, 1)
        for layer in range(layers):
            last = layer == layers - 1
            after = None if last else own(source, layer + 1)
            side = own(source, layers + layer)
            above = own(self.w_layer, layer + 1) * (here if last else here - after)
            total = MASS_TERM * here + above - below
            total += own(self.w_row, layer) * (here - own(source, layer, 1))
            total += own(self.w_row, layer, -1) * (here - own(source, layer, -1))
            east = jnp.where(lane == LANES - 1, roll(side, -1, 1), roll(here, -1, 1))
            west = jnp.where(lane == 0, roll(side, 1, 1), roll(here, 1, 1))
            total += own(self.w_east, layer) * (here - east)
            total += own(self.w_west, layer) * (here - west)
            yield layer, total
            here, below = after, above


def near(plane):
    return plane[HALO:-HALO]


def tally(plane):
    return plane.reshape(plane.shape[0] // 8, 8, LANES).sum(axis=0)


def own_ids(ids):
    blocks_x = ids.shape[0] // 2
    lines = [jnp.broadcast_to(ids[bx : bx + 1], (BLOCK, LANES)) for bx in range(blocks_x)]
    return jnp.concatenate(lines, axis=0)


def rows_kernel(position, aggregate_hbm, loading, viscosity, shard, ids, near_rows, far_rows, aggregate, sems):
    layers, rows, _ = loading.shape
    odd = position[0] % 2
    numbers = pltpu.make_async_copy(aggregate_hbm, aggregate, sems.at[4])
    numbers.start()
    copies = []
    for side, target in enumerate((near_rows, far_rows)):
        top = odd if side == 0 else 1 - odd
        at = pl.multiple_of((1 - top) * (rows - HALO), HALO)
        for k, source in enumerate((loading, viscosity)):
            copies.append(
                pltpu.make_async_copy(
                    source.at[:, pl.ds(at, HALO), :],
                    target.at[pl.ds(k * layers, layers)],
                    sems.at[2 * side + k],
                )
            )
    copies.append(pltpu.make_async_copy(shard, near_rows.at[pl.ds(2 * layers + 1, TILES)], sems.at[5]))
    for copy in copies:
        copy.start()
    numbers.wait()
    blocks_x, blocks_y = aggregate.shape
    lane = lane_row()
    flat = jnp.zeros((1, LANES), jnp.float32)
    for bx in range(blocks_x):
        names = jnp.zeros((1, LANES), jnp.float32)
        for by in range(blocks_y):
            name = (aggregate[bx, by] + 1).astype(jnp.float32)
            names = jnp.where(lane // BLOCK == by, name, names)
            flat = jnp.where(lane % (blocks_x * blocks_y) == bx * blocks_y + by, name, flat)
        ids[bx : bx + 1] = names
    ids[blocks_x:] = jnp.broadcast_to(flat, (ids.shape[0] - blocks_x, LANES))
    first, last = ids[0:1], ids[blocks_x - 1 : blocks_x]
    near_rows[2 * layers] = jnp.broadcast_to(jnp.where(odd == 1, first, last), (HALO, LANES))
    far_rows[2 * layers] = jnp.broadcast_to(jnp.where(odd == 1, last, first), (HALO, LANES))
    for copy in copies:
        copy.wait()


def tall_plane(slot, own, odd, near_rows, far_rows):
    low = jnp.where(odd == 1, near_rows[slot], far_rows[slot])
    high = jnp.where(odd == 1, far_rows[slot], near_rows[slot])
    return jnp.concatenate([low, own, high], axis=0)


def edge_kernel(position, loading, viscosity, own_names, near_rows, far_rows, near_cols, far_cols, message):
    layers = loading.shape[0]
    odd = position[0] % 2
    lane = lane_row()
    tall = loading.shape[1] + 2 * HALO
    right = left = jnp.zeros((tall, LANES), jnp.float32)
    for slot in range(2 * layers + 1):
        if slot < layers:
            own = loading[slot]
        elif slot < 2 * layers:
            own = viscosity[slot - layers]
        else:
            own = own_ids(own_names)
        plane = tall_plane(slot, own, odd, near_rows, far_rows)
        at = slot * SIDE
        moved = roll(plane, at, 1)
        left = jnp.where((lane >= at) & (lane < at + SIDE), moved, left)
        right = jnp.where((lane - at + SIDE) % LANES < SIDE, moved, right)
    odd_col = position[1] % 2
    near_cols[:tall] = jnp.where(odd_col == 1, left, right)
    far_cols[:tall] = jnp.where(odd_col == 1, right, left)
    blocks_x, width = own_names.shape[0] // 2, own_names.shape[0] // 2 * (LANES // BLOCK)
    fold = jnp.zeros((blocks_x, 8, LANES), jnp.float32)
    for layer in range(layers):
        fold = fold + fold_rows(loading[layer])
    line = pack_blocks([fold.sum(axis=1)])
    line = line + jnp.where((lane >= width) & (lane < 2 * width), own_names[blocks_x : blocks_x + 1], 0.0)
    message[...] = jnp.broadcast_to(line, message.shape)


def start_kernel(
    position, loading, viscosity, own_names, near_rows, far_rows, near_cols, far_cols, arrived, *rest
):
    parts = rest[:8]
    resid, direction, image, inverse, w_layer, w_row, w_east, w_west, names_out, lifted_blocks, message = rest[8:19]
    wide, ids, scaled_image, rise = rest[19:]
    layers = loading.shape[0]
    blocks_x, blocks_y = loading.shape[1] // BLOCK, LANES // BLOCK
    width = blocks_x * blocks_y
    odd, odd_col = position[0] % 2, position[1] % 2
    lane = lane_row()
    tall = loading.shape[1] + 2 * HALO
    from_west = jnp.where(odd_col == 1, near_cols[:tall], far_cols[:tall])
    from_east = jnp.where(odd_col == 1, far_cols[:tall], near_cols[:tall])

    def widen(slot, cells):
        at = slot * SIDE
        both = jnp.where((lane >= at) & (lane < at + SIDE), from_east, from_west)
        beyond = jnp.where((lane < SIDE) | (lane >= LANES - SIDE), roll(both, -at, 1), 0.0)
        return tall_plane(slot, cells, odd, near_rows, far_rows), beyond

    for layer in range(layers):
        for k, tile in enumerate(widen(layer, loading[layer])):
            put(resid, k * layers + layer, tile)
        for k, tile in enumerate(widen(layers + layer, viscosity[layer])):
            put(wide, k * layers + layer, tile)
    ids[0], ids[1] = widen(2 * layers, own_ids(own_names))
    names_out[...] = local_names(ids)

    sums = arrived[...]
    names = unfold(sums, 1, width).astype(jnp.int32)
    solved = coarse_solve(unfold(sums, 0, width), names, position[0], parts)
    lifted_blocks[...] = lookup(solved, names)
    prolong(rise, lookup(solved, names_out[...].astype(jnp.int32)))

    for layer in range(layers):
        east, west = beside(band(wide, layer), band(wide, layers + layer))
        for k in range(2):
            at, face = k * layers + layer, k * (layers + 1) + layer
            visc = band(wide, at)
            before = 0.5 * (visc if layer == 0 else visc + band(wide, at - 1))
            after = 0.5 * (visc if layer == layers - 1 else visc + band(wide, at + 1))
            down, up = 0.5 * (visc + band(wide, at, 1)), 0.5 * (visc + band(wide, at, -1))
            right, left = 0.5 * (visc + east[k]), 0.5 * (visc + west[k])
            if layer == 0:
                put(w_layer, face, before)
            put(w_layer, face + 1, after)
            put(w_row, at, down)
            put(w_east, at, right)
            put(w_west, at, left)
            diagonal = MASS_TERM + before + after + up + down + left + right
            part = jnp.where(visc > 0.0, 1.0 / diagonal, 0.0)
            put(inverse, at, part)
            put(direction, at, part * band(resid, at) + rise[k])
    folds_own, folds_east, folds_south = block_matrix(w_layer, w_row, w_east, w_west)

    operator = Operator(w_layer, w_row, w_east, w_west)
    zero = jnp.zeros((8, LANES), jnp.float32)
    folds = [jnp.zeros((blocks_x, 8, LANES), jnp.float32) for _ in range(2)]
    s_rp = s_rd = s_dq = s_eq = s_pq = s_ee = zero
    for layer, planes in operator.wide(direction):
        for k, plane in enumerate(planes):
            at = k * layers + layer
            put(image, at, plane)
            put(scaled_image, at, band(inverse, at) * plane)
        q, r, p, v = near(planes[0]), own(resid, layer), own(direction, layer), own(inverse, layer)
        d, e = v * r, v * q
        s_rp += tally(r * p)
        s_rd += tally(r * d)
        s_dq += tally(d * q)
        s_eq += tally(e * q)
        s_pq += tally(p * q)
        folds[0] += fold_rows(q)
    for layer, image_e in operator.near(scaled_image):
        s_ee += tally(image_e * own(scaled_image, layer))
        folds[1] += fold_rows(image_e)
    upper = pack_blocks([fold.sum(axis=1) for fold in folds])
    upper = upper + pack_scalars([s_rp, s_rd, s_dq, s_eq, s_pq, s_ee], 3 * width)
    lower = pack_blocks([folds_own, folds_east, folds_south])
    write_message(message, upper, lower)


def write_message(message, upper, lower):
    rows = iota(message.shape, 0)
    message[...] = jnp.where(rows % 2 == 0, upper, lower)


def block_matrix(w_layer, w_row, w_east, w_west):
    layers = w_row.shape[0] // 2
    rows = w_row.shape[1]
    lane = lane_row()
    east = west = jnp.zeros((rows - 2 * (PAD + HALO), LANES), jnp.float32)
    line = jnp.zeros((rows, LANES), jnp.float32)
    for layer in range(layers):
        east = east + own(w_east, layer)
        west = west + own(w_west, layer)
        line = line + w_row[layer]
    own_cells = fold_rows(own(w_layer, 0) + own(w_layer, layers)).sum(axis=1)
    east_face = fold_rows(jnp.where(lane % BLOCK == BLOCK - 1, east, 0.0)).sum(axis=1)
    west_face = fold_rows(jnp.where(lane % BLOCK == 0, west, 0.0)).sum(axis=1)
    count = own_cells.shape[0]
    first = PAD + HALO - 1
    faces = [line[first + BLOCK * k : first + BLOCK * k + 1] for k in range(count + 1)]
    north_face, south_face = jnp.concatenate(faces[:-1], axis=0), jnp.concatenate(faces[1:], axis=0)
    mass = jnp.full((count, LANES), MASS_TERM * layers * BLOCK, jnp.float32)
    total = mass + own_cells + east_face + west_face + south_face + north_face
    return total, east_face, south_face


def lane_total(values, lane_at):
    return jnp.sum(values[:, lane_at : lane_at + 1], axis=0, keepdims=True)


def dot_blocks(left, right):
    return jnp.sum(jnp.sum(left * right, axis=0, keepdims=True), axis=1, keepdims=True)


def received(ref, parity):
    return ref[pl.ds(parity, ref.shape[0] // 2, stride=2), :]


def write_scalars(ref, values):
    lane = lane_row()
    line = jnp.zeros((1, LANES), jnp.float32)
    for index, value in enumerate(values):
        line = jnp.where(lane == index, value, line)
    ref[...] = jnp.broadcast_to(line, ref.shape)


def middle_kernel(grid, position, arrived0, arrived, names_ref, lifted0_ref, *rest):
    parts = rest[:8]
    resid0, direction0, image0, inverse, w_layer, w_row, w_east, w_west = rest[8:16]
    resid, lifted, direction, image, lifted_image, scalars, lifted_blocks, message = rest[16:24]
    scaled_image, scaled_lifted, rise_0, rise_1 = rest[24:]
    width = grid[2] * grid[3]
    layers = resid.shape[0] // 2
    sums = arrived0[...]
    names = unfold(sums, 1, width).astype(jnp.int32)
    here = names_ref[...].astype(jnp.int32)
    upper, lower = received(arrived, 0), received(arrived, 1)
    s_rp, s_rd, s_dq, s_eq, s_pq, s_ee = [lane_total(upper, 3 * width + k) for k in range(6)]
    r_q, r_e = [unfold(upper, k, width) for k in range(2)]
    diag, east, south = [unfold(lower, k, width) for k in range(3)]
    lifted0 = lifted0_ref[...]
    r_d = r_q - apply_blocks(diag, east, south, lifted0, grid)
    s_dd = s_dq - dot_blocks(lifted0, r_d)
    s_de = s_eq - dot_blocks(lifted0, r_e)
    alpha0 = s_rp / s_pq
    scaled_sum = s_rd - 2.0 * alpha0 * s_dq + alpha0 * alpha0 * s_eq
    coarse1 = unfold(sums, 0, width) - alpha0 * r_q
    solved = coarse_solve(coarse1, names, position[0], parts)
    lifted1 = lookup(solved, names)
    prolong(rise_0, lookup(solved, here))
    inner1 = scaled_sum + dot_blocks(coarse1, lifted1)
    beta0 = inner1 / s_rp
    r_x = r_d - alpha0 * r_e + beta0 * r_q
    energy = (
        s_dd
        - 2.0 * alpha0 * s_de
        + alpha0 * alpha0 * s_ee
        + 2.0 * beta0 * (s_dq - alpha0 * s_eq)
        + beta0 * beta0 * s_pq
    )
    block_image = apply_blocks(diag, east, south, lifted1, grid)
    alpha1 = inner1 / (energy + dot_blocks(lifted1, 2.0 * r_x + block_image))
    coarse2 = coarse1 - alpha1 * (r_x + block_image)
    solved = coarse_solve(coarse2, names, position[0], parts)
    lifted_blocks[...] = lookup(solved, names)
    prolong(rise_1, lookup(solved, here))
    write_scalars(scalars, [alpha0, alpha1, inner1])

    operator = Operator(w_layer, w_row, w_east, w_west)
    for at in range(2 * layers):
        after = band(resid0, at) - alpha0 * band(image0, at)
        put(resid, at, after)
        put(direction, at, band(inverse, at) * after + rise_0[at // layers] + beta0 * band(direction0, at))
    zero = jnp.zeros((8, LANES), jnp.float32)
    folds = [jnp.zeros((grid[2], 8, LANES), jnp.float32) for _ in range(5)]
    s_rz = s_rd = s_zu = s_zq = s_pq = s_du = s_dq = s_us = s_uw = s_qw = zero
    s_ss = s_sw = s_ww = zero
    for layer, planes in operator.wide(direction):
        for k, plane in enumerate(planes):
            at = k * layers + layer
            put(image, at, plane)
            after = band(resid, at) - alpha1 * plane
            put(resid, at, after)
            put(lifted, at, band(inverse, at) * after + rise_1[k])
            put(scaled_image, at, band(inverse, at) * plane)
        q, r, p, v = near(planes[0]), own(resid, layer), own(direction, layer), own(inverse, layer)
        d, z, w = v * r, own(lifted, layer), v * q
        s_rz += tally(r * z)
        s_rd += tally(r * d)
        s_zq += tally(z * q)
        s_pq += tally(p * q)
        s_dq += tally(d * q)
        s_qw += tally(q * w)
        folds[1] += fold_rows(q)
        folds[4] += fold_rows(r)
    for layer, planes in operator.wide(lifted):
        for k, plane in enumerate(planes):
            at = k * layers + layer
            put(lifted_image, at, plane)
            put(scaled_lifted, at, band(inverse, at) * plane)
        u = near(planes[0])
        v = own(inverse, layer) * u
        s_zu += tally(u * own(lifted, layer))
        s_du += tally(v * own(resid, layer))
        s_us += tally(u * v)
        s_uw += tally(u * own(scaled_image, layer))
        folds[0] += fold_rows(u)
    for layer, image_s in operator.near(scaled_lifted):
        s_ss += tally(image_s * own(scaled_lifted, layer))
        s_sw += tally(image_s * own(scaled_image, layer))
        folds[2] += fold_rows(image_s)
    for layer, image_w in operator.near(scaled_image):
        s_ww += tally(image_w * own(scaled_image, layer))
        folds[3] += fold_rows(image_w)
    lines = [fold.sum(axis=1) for fold in folds]
    upper = pack_blocks(lines[:4])
    lower = pack_blocks(lines[4:]) + pack_scalars(
        [s_rz, s_rd, s_zu, s_zq, s_pq, s_du, s_dq, s_us, s_uw, s_qw, s_ss, s_sw, s_ww],
        width,
    )
    write_message(message, upper, lower)


def last_kernel(grid, position, arrived0, before, arrived, names_ref, scalars, lifted2_ref, *rest):
    parts = rest[:8]
    resid, lifted, direction1, image1, lifted_image, direction0, inverse, w_layer, w_row, w_east, w_west = rest[8:19]
    outs = rest[19:21]
    direction, rise_3, answer, out_resid, sems = rest[21:]
    width = grid[2] * grid[3]
    layers = resid.shape[0] // 2
    names = unfold(arrived0[...], 1, width).astype(jnp.int32)
    here = names_ref[...].astype(jnp.int32)
    blocks = received(before, 1)
    diag, east, south = [unfold(blocks, k, width) for k in range(3)]
    upper, lower = received(arrived, 0), received(arrived, 1)
    r_u, r_q, r_s, r_w = [unfold(upper, k, width) for k in range(4)]
    r_r = unfold(lower, 0, width)
    s_rz, s_rd, s_zu, s_zq, s_pq, s_du, s_dq, s_us, s_uw, s_qw, s_ss, s_sw, s_ww = [
        lane_total(lower, width + k) for k in range(13)
    ]
    lifted2 = lifted2_ref[...]
    r_d = r_u - apply_blocks(diag, east, south, lifted2, grid)
    s_dd = s_du - dot_blocks(lifted2, r_d)
    s_ds = s_us - dot_blocks(lifted2, r_s)
    s_dw = s_uw - dot_blocks(lifted2, r_w)
    alpha0, alpha1, inner1 = [scalars[0:1, k : k + 1] for k in range(3)]
    inner2 = s_rz
    beta1 = inner2 / inner1
    alpha2 = inner2 / (s_zu + 2.0 * beta1 * s_zq + beta1 * beta1 * s_pq)
    coarse3 = r_r - alpha2 * (r_u + beta1 * r_q)
    solved = coarse_solve(coarse3, names, position[0], parts)
    lifted3 = lookup(solved, names)
    prolong(rise_3, lookup(solved, here))
    scaled_sum = (
        s_rd
        - 2.0 * alpha2 * (s_du + beta1 * s_dq)
        + alpha2 * alpha2 * (s_us + 2.0 * beta1 * s_uw + beta1 * beta1 * s_qw)
    )
    inner3 = scaled_sum + dot_blocks(coarse3, lifted3)
    beta2 = inner3 / inner2
    rise = lifted3 + beta2 * lifted2
    k_d, k_s, k_w, k_p = 1.0 + beta2, -alpha2, -alpha2 * beta1, beta2 * beta1
    energy = (
        k_d * k_d * s_dd
        + k_s * k_s * s_ss
        + k_w * k_w * s_ww
        + k_p * k_p * s_pq
        + 2.0 * (k_d * (k_s * s_ds + k_w * s_dw + k_p * s_dq) + k_s * (k_w * s_sw + k_p * s_uw) + k_w * k_p * s_qw)
    )
    r_x = k_d * r_d + k_s * r_s + k_w * r_w + k_p * r_q
    block_image = apply_blocks(diag, east, south, rise, grid)
    alpha3 = inner3 / (energy + dot_blocks(rise, 2.0 * r_x + block_image))

    for at in range(2 * layers):
        direction2 = band(lifted, at) + beta1 * band(direction1, at)
        after = band(resid, at) - alpha2 * (band(lifted_image, at) + beta1 * band(image1, at))
        step = band(inverse, at) * after + rise_3[at // layers] + beta2 * direction2
        put(direction, at, step)
        if at < layers:
            out_resid[at] = near(after)
            answer[at] = (
                alpha0 * own(direction0, at)
                + alpha1 * own(direction1, at)
                + alpha2 * near(direction2)
                + alpha3 * near(step)
            )
    copies = [pltpu.make_async_copy(answer, outs[0], sems.at[layers])]
    copies[0].start()
    for layer, plane in Operator(w_layer, w_row, w_east, w_west).near(direction):
        out_resid[layer] = out_resid[layer] - alpha3 * plane
        copies.append(pltpu.make_async_copy(out_resid.at[layer], outs[1].at[layer], sems.at[layer]))
        copies[-1].start()
    for copy in copies:
        copy.wait()


def call(kernel, outs, scratch, name, smem, *operands, spaces=None, out_space=pltpu.VMEM):
    whole = pl.BlockSpec(memory_space=pltpu.VMEM)
    scalar = pl.BlockSpec(memory_space=pltpu.SMEM)
    specs = [scalar] * smem + [whole] * (len(operands) - smem)
    operands = list(operands)
    for index in spaces or ():
        specs[index] = pl.BlockSpec(memory_space=pltpu.HBM)
        operands[index] = pltpu.with_memory_space_constraint(operands[index], pltpu.HBM)
    return pl.pallas_call(
        kernel,
        out_shape=[jax.ShapeDtypeStruct(shape, jnp.float32) for shape in outs],
        in_specs=specs,
        out_specs=[pl.BlockSpec(memory_space=out_space)] * len(outs),
        scratch_shapes=[pltpu.VMEM(s, jnp.float32) if isinstance(s, tuple) else s for s in scratch],
        compiler_params=pltpu.CompilerParams(vmem_limit_bytes=20 * 1024 * 1024),
        name=name,
    )(*operands)


def exchange(message):
    return lax.all_to_all(message, BOTH, 0, 0, tiled=True)


def pair(values, axis, mask):
    return lax.ppermute(values, axis, [(i, i ^ mask) for i in range(lax.axis_size(axis))])


def pair_far(values, axis):
    count = lax.axis_size(axis)
    return lax.ppermute(values, axis, [(i, i + 1 if i % 2 else i - 1) for i in range(1, count - 1)])


def local_steps(loading, viscosity, aggregate, coarse_inverse):
    layers, cells_x, cells_y = loading.shape
    blocks_x, blocks_y = aggregate.shape
    count_x, count_y = lax.axis_size("rows"), lax.axis_size("cols")
    devices = count_x * count_y
    grid = (count_x, count_y, blocks_x, blocks_y)
    position = jnp.stack([lax.axis_index(axis).astype(jnp.int32) for axis in BOTH])
    tall = cells_x + 2 * HALO
    edge = (2 * layers + 1, HALO, LANES)
    shard = coarse_inverse.T.reshape(PART // 8, 8, COARSE // LANES, LANES)
    shard = shard.transpose(0, 2, 1, 3).reshape(TILES, 8, LANES)
    parts = [pair(shard, "rows", mask) for mask in (2, 4, 6)]

    ids, near_out, far_rows = call(
        rows_kernel,
        [(8, LANES), (edge[0] + TILES, 8, LANES), (LONG, 8, LANES)],
        [pltpu.SMEM(aggregate.shape, jnp.int32), pltpu.SemaphoreType.DMA((6,))],
        "rows",
        1,
        position,
        aggregate,
        loading,
        viscosity,
        shard,
        spaces=(1, 2, 3, 4),
    )
    own = (position, loading, viscosity, ids)
    near_rows, far_rows = pair(near_out, "rows", 1), pair_far(far_rows, "rows")
    near_cols, far_cols, message0 = call(
        edge_kernel, [(8 * LONG, LANES)] * 2 + [(devices, LANES)], [], "edges", 1, *own, near_rows, far_rows
    )
    near_cols, far_cols = pair(near_cols, "cols", 1), pair_far(far_cols, "cols")
    parts = [part for both in ((part, pair(part, "rows", 1)) for part in parts) for part in both]
    parts = [near_out, near_rows] + parts
    arrived0 = exchange(message0)
    parts, arrived0 = lax.optimization_barrier((parts, arrived0))
    field = (2 * layers, tall + 2 * PAD, LANES)
    taller = (2 * (layers + 1), tall + 2 * PAD, LANES)
    plane = (2, tall, LANES)
    message = (2 * devices, LANES)
    line = (8, LANES)
    resid, direction0, image0, inverse, w_layer, w_row, w_east, w_west, names, lifted_blocks, message1 = call(
        start_kernel,
        [field] * 4 + [taller, field, field, field, line, line, message],
        [field, plane, field, plane],
        "start",
        1,
        *own,
        near_rows,
        far_rows,
        near_cols,
        far_cols,
        arrived0,
        *parts,
    )
    weights = (inverse, w_layer, w_row, w_east, w_west)
    arrived1 = exchange(message1)
    resid, lifted, direction1, image1, lifted_image, scalars, lifted_blocks, message2 = call(
        lambda *refs: middle_kernel(grid, *refs),
        [field] * 5 + [line, line, message],
        [field] * 2 + [plane] * 2,
        "middle",
        1,
        position,
        arrived0,
        arrived1,
        names,
        lifted_blocks,
        *parts,
        resid,
        direction0,
        image0,
        *weights,
    )
    arrived2 = exchange(message2)
    return call(
        lambda *refs: last_kernel(grid, *refs),
        [loading.shape] * 2,
        [field, plane, loading.shape, loading.shape, pltpu.SemaphoreType.DMA((layers + 1,))],
        "last",
        1,
        position,
        arrived0,
        arrived1,
        arrived2,
        names,
        scalars,
        lifted_blocks,
        *parts,
        resid,
        lifted,
        direction1,
        image1,
        lifted_image,
        direction0,
        *weights,
        out_space=pltpu.HBM,
    )


def from_sides(block, axis, dim, width):
    count = lax.axis_size(axis)
    forward = [(i, i + 1) for i in range(count - 1)]
    backward = [(target, source) for source, target in forward]
    size = block.shape[dim]
    low = lax.ppermute(lax.slice_in_dim(block, size - width, size, axis=dim), axis, forward)
    high = lax.ppermute(lax.slice_in_dim(block, 0, width, axis=dim), axis, backward)
    return low, high


def widened(block, width_x, width_y):
    low, high = from_sides(block, "rows", block.ndim - 2, width_x)
    block = jnp.concatenate([low, block, high], axis=-2)
    turned = jnp.swapaxes(block, -1, -2)
    low, high = from_sides(turned, "cols", turned.ndim - 2, width_y)
    low, high = jnp.swapaxes(low, -1, -2), jnp.swapaxes(high, -1, -2)
    return jnp.concatenate([low, block, high], axis=-1)


def all_sum(values):
    count = lax.axis_size("rows") * lax.axis_size("cols")
    if count > 64:
        return lax.psum(lax.psum(values, "cols"), "rows")
    spread = jnp.broadcast_to(values[None], (count,) + values.shape)
    return lax.all_to_all(spread, BOTH, 0, 0).sum(axis=0)


def shifted(field, axis, step):
    return jnp.roll(field, step, axis=axis)


def local_general(loading, viscosity, aggregate, coarse_inverse):
    layers, cells_x, cells_y = loading.shape
    blocks_x, blocks_y = aggregate.shape
    ids = jnp.arange(COARSE, dtype=jnp.int32)
    whole_matrix = lax.all_gather(coarse_inverse, "rows", axis=1, tiled=True)
    fields = widened(jnp.stack([loading, viscosity]), HALO, HALO)
    wide_aggregate = widened(aggregate + 1, 1, 1) - 1
    table = (aggregate.reshape(-1)[:, None] == ids[None, :]).astype(jnp.float32)
    wide_table = (wide_aggregate.reshape(-1)[:, None] == ids[None, :]).astype(jnp.float32)

    residual, visc = fields[0], fields[1]
    inside = visc > 0.0
    pads = ((1, 1), (0, 0), (0, 0))
    padded = jnp.pad(visc, pads)
    weights = [
        0.5 * (visc + padded[:-2]),
        0.5 * (visc + padded[2:]),
        0.5 * (visc + shifted(visc, 1, 1)),
        0.5 * (visc + shifted(visc, 1, -1)),
        0.5 * (visc + shifted(visc, 2, 1)),
        0.5 * (visc + shifted(visc, 2, -1)),
    ]
    diagonal = MASS_TERM + sum(weights)
    inverse = jnp.where(inside, 1.0 / diagonal, 0.0)

    def operate(field):
        layered = jnp.pad(field, pads)
        sides = [
            layered[:-2],
            layered[2:],
            shifted(field, 1, 1),
            shifted(field, 1, -1),
            shifted(field, 2, 1),
            shifted(field, 2, -1),
        ]
        total = MASS_TERM * field
        for weight, side in zip(weights, sides):
            total = total + weight * (field - side)
        return total

    def inner_part(field):
        return field[:, HALO:-HALO, HALO:-HALO]

    def restrict(field):
        blocks = field.reshape(layers, blocks_x, BLOCK, blocks_y, BLOCK).sum(axis=(0, 2, 4))
        return jnp.dot(blocks.reshape(-1), table, precision=PRECISE).reshape(4, COARSE // 4)

    def prolong(values):
        per_block = jnp.dot(wide_table, values.reshape(-1), precision=PRECISE)
        per_block = per_block.reshape(blocks_x + 2, blocks_y + 2)
        spread = jnp.repeat(jnp.repeat(per_block, BLOCK, axis=0), BLOCK, axis=1)
        cut = BLOCK - HALO
        return spread[cut:-cut, cut:-cut][None]

    def coarse_apply(coarse):
        return jnp.dot(whole_matrix, coarse.reshape(-1), precision=PRECISE).reshape(coarse.shape)

    def scalars(*values):
        return jnp.stack([jnp.broadcast_to(v, (COARSE // 4,)) for v in values])

    coarse = all_sum(restrict(loading))
    lifted = coarse_apply(coarse)
    direction = inverse * residual + prolong(lifted)
    answer = jnp.zeros_like(loading)
    scaled_sum = inner_now = None
    for iteration in range(ITERS):
        image = operate(direction)
        near_image, near_scaled = inner_part(image), inner_part(inverse * image)
        near_direction, near_residual = inner_part(direction), inner_part(residual)
        packed = jnp.concatenate(
            [
                restrict(near_image),
                scalars(
                    jnp.sum(near_direction * near_image),
                    jnp.sum(near_residual * near_scaled),
                    jnp.sum(near_image * near_scaled),
                    jnp.sum(near_residual * inner_part(inverse) * near_residual),
                ),
            ]
        )
        packed = all_sum(packed)
        curvature, cross, square = packed[4, 0], packed[5, 0], packed[6, 0]
        if scaled_sum is None:
            scaled_sum = packed[7, 0]
            inner_now = scaled_sum + jnp.sum(coarse * lifted)
        alpha = inner_now / curvature
        answer = answer + alpha * near_direction
        residual = residual - alpha * image
        if iteration + 1 < ITERS:
            coarse = coarse - alpha * packed[:4]
            scaled_sum = scaled_sum - 2.0 * alpha * cross + alpha * alpha * square
            lifted = coarse_apply(coarse)
            inner_next = scaled_sum + jnp.sum(coarse * lifted)
            direction = inverse * residual + prolong(lifted) + inner_next / inner_now * direction
            inner_now = inner_next
    return answer, inner_part(residual)


def solution(mesh):
    in_specs = (
        P(None, "rows", "cols"),
        P(None, "rows", "cols"),
        P("rows", "cols"),
        P(None, "rows"),
    )
    out_specs = (P(None, "rows", "cols"), P(None, "rows", "cols"))
    body = local_steps if (mesh.shape["rows"], mesh.shape["cols"]) == (8, 4) else local_general
    return jax.shard_map(body, mesh=mesh, in_specs=in_specs, out_specs=out_specs, check_vma=False)
```

```python
import jax
import jax.numpy as jnp
from jax import lax
from jax.experimental import pallas as pl
from jax.experimental.pallas import tpu as pltpu
from jax.sharding import PartitionSpec as P

BLOCK = 16
COARSE = 512
ITERS = 4
HALO = 8
SIDE = 7
LANES = 128
PAD = 8
LONG = 33
PART = 64
TILES = PART * COARSE // (8 * LANES)

MASS_TERM = 1.0
PRECISE = lax.Precision.HIGHEST
BOTH = ("rows", "cols")


def iota(shape, dim):
    return lax.broadcasted_iota(jnp.int32, shape, dim)


def roll(x, shift, axis):
    size = x.shape[axis]
    shift = shift % size
    return x if shift == 0 else pltpu.roll(x, shift, axis)


def lane_row():
    return iota((1, LANES), 1)


def pick_lanes(values, index):
    return jnp.take_along_axis(values, index, axis=1, mode="promise_in_bounds")


def fold_rows(plane):
    rows = plane.shape[0]
    return plane.reshape(rows // BLOCK, 2, 8, LANES).sum(axis=1)


def pack_blocks(folds):
    count = folds[0].shape[0]
    pad = (-count * len(folds)) % 8
    stacked = jnp.concatenate(folds + ([jnp.zeros((pad, LANES), jnp.float32)] if pad else []), axis=0)
    spread = iota((LANES, LANES), 0) // BLOCK == iota((LANES, LANES), 1) % (LANES // BLOCK)
    summed = jnp.dot(stacked, spread.astype(jnp.float32), precision=PRECISE)
    group = lane_row() // (LANES // BLOCK)
    row = jnp.zeros((1, LANES), jnp.float32)
    for index in range(len(folds) * count):
        row = row + jnp.where(group == index, summed[index : index + 1], 0.0)
    return row


def pack_scalars(partials, offset):
    lane = lane_row()
    row = jnp.zeros((1, LANES), jnp.float32)
    for index, partial in enumerate(partials):
        total = jnp.sum(jnp.sum(partial, axis=0, keepdims=True), axis=1, keepdims=True)
        row = row + jnp.where(lane == offset + index, total, 0.0)
    return row


def unfold(values, slot, width):
    devices = values.shape[0]
    lane = iota((devices, LANES), 1)
    part = jnp.where(lane < width, roll(values, -slot * width, 1), 0.0)
    step = width
    while step < LANES:
        part = part + roll(part, step, 1)
        step *= 2
    per_row = LANES // width
    own = jnp.where(iota((devices, LANES), 0) % per_row == lane // width, part, 0.0)
    rows = [
        jnp.sum(own[k * per_row : (k + 1) * per_row], axis=0, keepdims=True) for k in range(devices // per_row)
    ]
    return jnp.concatenate(rows, axis=0)


def coarse_solve(values, names, position, parts):
    count = COARSE // LANES
    lines = [jnp.zeros((8, LANES), jnp.float32) for _ in range(count)]
    for part, ref in enumerate(parts):
        aggregate = iota((PART, LANES), 0) + ((position ^ part) * PART + 1)
        total = jnp.zeros((PART, LANES), jnp.float32)
        for row in range(8):
            total = total + jnp.where(aggregate == names[row : row + 1], values[row : row + 1], 0.0)
        column = jnp.sum(total, axis=1, keepdims=True)
        first = ref.shape[0] - TILES
        for index in range(TILES):
            at = 8 * (index // count)
            lines[index % count] += ref[first + index] * column[at : at + 8]
    return [jnp.broadcast_to(jnp.sum(line, axis=0, keepdims=True), (8, LANES)) for line in lines]


def lookup(coarse, names):
    index = jnp.maximum(names - 1, 0)
    inner = index % LANES
    result = jnp.zeros(names.shape, jnp.float32)
    for tile, values in enumerate(coarse):
        result = jnp.where(index // LANES == tile, pick_lanes(values, inner), result)
    return jnp.where(names > 0, result, 0.0)


def apply_blocks(diag, east, south, values, grid):
    count_x, count_y, blocks_x, blocks_y = grid
    width = blocks_x * blocks_y
    lane = iota(values.shape, 1)
    row, col = iota(values.shape, 0), lane // width
    at_x, at_y = (lane % width) // blocks_y, lane % blocks_y
    last_x, last_y = at_x == blocks_x - 1, at_y == blocks_y - 1
    step_e = width - (blocks_y - 1)
    step_s = (blocks_x - 1) * blocks_y

    def take(x, inner, outer, is_outer, missing):
        return jnp.where(missing, 0.0, jnp.where(is_outer, outer(x), inner(x)))

    from_e = take(
        values, lambda x: roll(x, -1, 1), lambda x: roll(x, -step_e, 1), last_y, last_y & (col == count_y - 1)
    )
    from_w = take(
        east * values, lambda x: roll(x, 1, 1), lambda x: roll(x, step_e, 1), at_y == 0, (at_y == 0) & (col == 0)
    )
    from_s = take(
        values,
        lambda x: roll(x, -blocks_y, 1),
        lambda x: roll(roll(x, -1, 0), step_s, 1),
        last_x,
        last_x & (row == count_x - 1),
    )
    from_n = take(
        south * values,
        lambda x: roll(x, blocks_y, 1),
        lambda x: roll(roll(x, 1, 0), -step_s, 1),
        at_x == 0,
        (at_x == 0) & (row == 0),
    )
    return diag * values - east * from_e - south * from_s - from_w - from_n


def local_names(ids):
    rows = ids.shape[1]
    lane = iota((8, LANES), 1)
    at = lane % BLOCK
    starts = [0] + list(range(HALO, rows, BLOCK))
    result = jnp.zeros((8, LANES), jnp.float32)
    for index, start in enumerate(starts):
        inner = pick_lanes(ids[0, start : start + 8], (at * BLOCK) % LANES)
        outer = pick_lanes(ids[1, start : start + 8], jnp.where(at == 8, 0, LANES - 1))
        both = jnp.where(at < 8, inner, jnp.where(at < 10, outer, 0.0))
        result = jnp.where(lane // BLOCK == index, both, result)
    return result


def prolong(target, values):
    lane = iota((8, LANES), 1)
    rows = target.shape[1]
    bounds = [0] + list(range(HALO, rows, BLOCK)) + [rows]
    for index in range(len(bounds) - 1):
        main = pick_lanes(values, lane // BLOCK + index * BLOCK)
        side = pick_lanes(values, jnp.where(lane < BLOCK, 8, 9) + index * BLOCK)
        for row in range(bounds[index], bounds[index + 1], 8):
            target[0, row : row + 8] = main
            target[1, row : row + 8] = side


def band(ref, index, step=0):
    rows = ref.shape[1]
    return ref[index, PAD + step : rows - PAD + step, :]


def put(ref, index, value):
    ref[index, PAD : ref.shape[1] - PAD, :] = value


def own(ref, index, step=0):
    rows = ref.shape[1]
    return ref[index, PAD + HALO + step : rows - PAD - HALO + step, :]


def beside(main, side):
    lane = iota(main.shape, 1)
    main_e, side_e = roll(main, -1, 1), roll(side, -1, 1)
    main_w, side_w = roll(main, 1, 1), roll(side, 1, 1)
    last, first = lane == LANES - 1, lane == 0
    east = jnp.where(last, side_e, main_e), jnp.where(last, main_e, side_e)
    west = jnp.where(first, side_w, main_w), jnp.where(first, main_w, side_w)
    return east, west


class Operator:
    def __init__(self, w_layer, w_row, w_east, w_west):
        self.w_layer, self.w_row, self.w_east, self.w_west = w_layer, w_row, w_east, w_west

    def wide(self, source):
        layers = self.w_row.shape[0] // 2
        current = [band(source, k * layers) for k in range(2)]
        below = [-band(self.w_layer, k * (layers + 1)) * current[k] for k in range(2)]
        for layer in range(layers):
            last = layer == layers - 1
            after = [None if last else band(source, k * layers + layer + 1) for k in range(2)]
            east, west = beside(*current)
            result = []
            for k in range(2):
                at = k * layers + layer
                here = current[k]
                above = band(self.w_layer, k * (layers + 1) + layer + 1) * (here if last else here - after[k])
                total = MASS_TERM * here + above - below[k]
                total += band(self.w_row, at) * (here - band(source, at, 1))
                total += band(self.w_row, at, -1) * (here - band(source, at, -1))
                total += band(self.w_east, at) * (here - east[k])
                total += band(self.w_west, at) * (here - west[k])
                result.append(total)
                below[k] = above
            yield layer, result
            current = after

    def near(self, source):
        layers = self.w_row.shape[0] // 2
        here = own(source, 0)
        below = -own(self.w_layer, 0) * here
        lane = iota(here.shape, 1)
        for layer in range(layers):
            last = layer == layers - 1
            after = None if last else own(source, layer + 1)
            side = own(source, layers + layer)
            above = own(self.w_layer, layer + 1) * (here if last else here - after)
            total = MASS_TERM * here + above - below
            total += own(self.w_row, layer) * (here - own(source, layer, 1))
            total += own(self.w_row, layer, -1) * (here - own(source, layer, -1))
            east = jnp.where(lane == LANES - 1, roll(side, -1, 1), roll(here, -1, 1))
            west = jnp.where(lane == 0, roll(side, 1, 1), roll(here, 1, 1))
            total += own(self.w_east, layer) * (here - east)
            total += own(self.w_west, layer) * (here - west)
            yield layer, total
            here, below = after, above


def near(plane):
    return plane[HALO:-HALO]


def tally(plane):
    return plane.reshape(plane.shape[0] // 8, 8, LANES).sum(axis=0)


def own_ids(ids):
    blocks_x = ids.shape[0] // 2
    lines = [jnp.broadcast_to(ids[bx : bx + 1], (BLOCK, LANES)) for bx in range(blocks_x)]
    return jnp.concatenate(lines, axis=0)


def rows_kernel(position, aggregate_hbm, loading, viscosity, shard, ids, near_rows, far_rows, aggregate, sems):
    layers, rows, _ = loading.shape
    odd = position[0] % 2
    numbers = pltpu.make_async_copy(aggregate_hbm, aggregate, sems.at[4])
    numbers.start()
    copies = []
    for side, target in enumerate((near_rows, far_rows)):
        top = odd if side == 0 else 1 - odd
        at = pl.multiple_of((1 - top) * (rows - HALO), HALO)
        for k, source in enumerate((loading, viscosity)):
            copies.append(
                pltpu.make_async_copy(
                    source.at[:, pl.ds(at, HALO), :],
                    target.at[pl.ds(k * layers, layers)],
                    sems.at[2 * side + k],
                )
            )
    piece = TILES // 4
    for k in range(4):
        target = near_rows.at[pl.ds(2 * layers + 1 + k * piece, piece)]
        copies.append(pltpu.make_async_copy(shard.at[pl.ds(k * piece, piece)], target, sems.at[5 + k]))
    for copy in copies:
        copy.start()
    numbers.wait()
    blocks_x, blocks_y = aggregate.shape
    lane = lane_row()
    flat = jnp.zeros((1, LANES), jnp.float32)
    for bx in range(blocks_x):
        names = jnp.zeros((1, LANES), jnp.float32)
        for by in range(blocks_y):
            name = (aggregate[bx, by] + 1).astype(jnp.float32)
            names = jnp.where(lane // BLOCK == by, name, names)
            flat = jnp.where(lane % (blocks_x * blocks_y) == bx * blocks_y + by, name, flat)
        ids[bx : bx + 1] = names
    ids[blocks_x:] = jnp.broadcast_to(flat, (ids.shape[0] - blocks_x, LANES))
    first, last = ids[0:1], ids[blocks_x - 1 : blocks_x]
    near_rows[2 * layers] = jnp.broadcast_to(jnp.where(odd == 1, first, last), (HALO, LANES))
    far_rows[2 * layers] = jnp.broadcast_to(jnp.where(odd == 1, last, first), (HALO, LANES))
    for copy in copies:
        copy.wait()


def tall_plane(slot, own, odd, near_rows, far_rows):
    low = jnp.where(odd == 1, near_rows[slot], far_rows[slot])
    high = jnp.where(odd == 1, far_rows[slot], near_rows[slot])
    return jnp.concatenate([low, own, high], axis=0)


def edge_kernel(position, loading, viscosity, own_names, near_rows, far_rows, near_cols, far_cols, message):
    layers = loading.shape[0]
    odd = position[0] % 2
    lane = lane_row()
    tall = loading.shape[1] + 2 * HALO
    right = left = jnp.zeros((tall, LANES), jnp.float32)
    for slot in range(2 * layers + 1):
        if slot < layers:
            own = loading[slot]
        elif slot < 2 * layers:
            own = viscosity[slot - layers]
        else:
            own = own_ids(own_names)
        plane = tall_plane(slot, own, odd, near_rows, far_rows)
        at = slot * SIDE
        moved = roll(plane, at, 1)
        left = jnp.where((lane >= at) & (lane < at + SIDE), moved, left)
        right = jnp.where((lane - at + SIDE) % LANES < SIDE, moved, right)
    odd_col = position[1] % 2
    near_cols[:tall] = jnp.where(odd_col == 1, left, right)
    far_cols[:tall] = jnp.where(odd_col == 1, right, left)
    blocks_x, width = own_names.shape[0] // 2, own_names.shape[0] // 2 * (LANES // BLOCK)
    fold = jnp.zeros((blocks_x, 8, LANES), jnp.float32)
    for layer in range(layers):
        fold = fold + fold_rows(loading[layer])
    line = pack_blocks([fold.sum(axis=1)])
    line = line + jnp.where((lane >= width) & (lane < 2 * width), own_names[blocks_x : blocks_x + 1], 0.0)
    message[...] = jnp.broadcast_to(line, message.shape)


def start_kernel(
    position, loading, viscosity, own_names, near_rows, far_rows, near_cols, far_cols, arrived, *rest
):
    parts = rest[:8]
    resid, direction, image, inverse, w_layer, w_row, w_east, w_west, names_out, lifted_blocks, message = rest[8:19]
    wide, ids, scaled_image, rise = rest[19:]
    layers = loading.shape[0]
    blocks_x, blocks_y = loading.shape[1] // BLOCK, LANES // BLOCK
    width = blocks_x * blocks_y
    odd, odd_col = position[0] % 2, position[1] % 2
    lane = lane_row()
    tall = loading.shape[1] + 2 * HALO
    from_west = jnp.where(odd_col == 1, near_cols[:tall], far_cols[:tall])
    from_east = jnp.where(odd_col == 1, far_cols[:tall], near_cols[:tall])

    def widen(slot, cells):
        at = slot * SIDE
        both = jnp.where((lane >= at) & (lane < at + SIDE), from_east, from_west)
        beyond = jnp.where((lane < SIDE) | (lane >= LANES - SIDE), roll(both, -at, 1), 0.0)
        return tall_plane(slot, cells, odd, near_rows, far_rows), beyond

    for layer in range(layers):
        for k, tile in enumerate(widen(layer, loading[layer])):
            put(resid, k * layers + layer, tile)
        for k, tile in enumerate(widen(layers + layer, viscosity[layer])):
            put(wide, k * layers + layer, tile)
    ids[0], ids[1] = widen(2 * layers, own_ids(own_names))
    names_out[...] = local_names(ids)

    sums = arrived[...]
    names = unfold(sums, 1, width).astype(jnp.int32)
    solved = coarse_solve(unfold(sums, 0, width), names, position[0], parts)
    lifted_blocks[...] = lookup(solved, names)
    prolong(rise, lookup(solved, names_out[...].astype(jnp.int32)))

    for layer in range(layers):
        east, west = beside(band(wide, layer), band(wide, layers + layer))
        for k in range(2):
            at, face = k * layers + layer, k * (layers + 1) + layer
            visc = band(wide, at)
            before = 0.5 * (visc if layer == 0 else visc + band(wide, at - 1))
            after = 0.5 * (visc if layer == layers - 1 else visc + band(wide, at + 1))
            down, up = 0.5 * (visc + band(wide, at, 1)), 0.5 * (visc + band(wide, at, -1))
            right, left = 0.5 * (visc + east[k]), 0.5 * (visc + west[k])
            if layer == 0:
                put(w_layer, face, before)
            put(w_layer, face + 1, after)
            put(w_row, at, down)
            put(w_east, at, right)
            put(w_west, at, left)
            diagonal = MASS_TERM + before + after + up + down + left + right
            part = jnp.where(visc > 0.0, 1.0 / diagonal, 0.0)
            put(inverse, at, part)
            put(direction, at, part * band(resid, at) + rise[k])
    folds_own, folds_east, folds_south = block_matrix(w_layer, w_row, w_east, w_west)

    operator = Operator(w_layer, w_row, w_east, w_west)
    zero = jnp.zeros((8, LANES), jnp.float32)
    folds = [jnp.zeros((blocks_x, 8, LANES), jnp.float32) for _ in range(2)]
    s_rp = s_rd = s_dq = s_eq = s_pq = s_ee = zero
    for layer, planes in operator.wide(direction):
        for k, plane in enumerate(planes):
            at = k * layers + layer
            put(image, at, plane)
            put(scaled_image, at, band(inverse, at) * plane)
        q, r, p, v = near(planes[0]), own(resid, layer), own(direction, layer), own(inverse, layer)
        d, e = v * r, v * q
        s_rp += tally(r * p)
        s_rd += tally(r * d)
        s_dq += tally(d * q)
        s_eq += tally(e * q)
        s_pq += tally(p * q)
        folds[0] += fold_rows(q)
    for layer, image_e in operator.near(scaled_image):
        s_ee += tally(image_e * own(scaled_image, layer))
        folds[1] += fold_rows(image_e)
    upper = pack_blocks([fold.sum(axis=1) for fold in folds])
    upper = upper + pack_scalars([s_rp, s_rd, s_dq, s_eq, s_pq, s_ee], 3 * width)
    lower = pack_blocks([folds_own, folds_east, folds_south])
    write_message(message, upper, lower)


def write_message(message, upper, lower):
    rows = iota(message.shape, 0)
    message[...] = jnp.where(rows % 2 == 0, upper, lower)


def block_matrix(w_layer, w_row, w_east, w_west):
    layers = w_row.shape[0] // 2
    rows = w_row.shape[1]
    lane = lane_row()
    east = west = jnp.zeros((rows - 2 * (PAD + HALO), LANES), jnp.float32)
    line = jnp.zeros((rows, LANES), jnp.float32)
    for layer in range(layers):
        east = east + own(w_east, layer)
        west = west + own(w_west, layer)
        line = line + w_row[layer]
    own_cells = fold_rows(own(w_layer, 0) + own(w_layer, layers)).sum(axis=1)
    east_face = fold_rows(jnp.where(lane % BLOCK == BLOCK - 1, east, 0.0)).sum(axis=1)
    west_face = fold_rows(jnp.where(lane % BLOCK == 0, west, 0.0)).sum(axis=1)
    count = own_cells.shape[0]
    first = PAD + HALO - 1
    faces = [line[first + BLOCK * k : first + BLOCK * k + 1] for k in range(count + 1)]
    north_face, south_face = jnp.concatenate(faces[:-1], axis=0), jnp.concatenate(faces[1:], axis=0)
    mass = jnp.full((count, LANES), MASS_TERM * layers * BLOCK, jnp.float32)
    total = mass + own_cells + east_face + west_face + south_face + north_face
    return total, east_face, south_face


def lane_total(values, lane_at):
    return jnp.sum(values[:, lane_at : lane_at + 1], axis=0, keepdims=True)


def dot_blocks(left, right):
    return jnp.sum(jnp.sum(left * right, axis=0, keepdims=True), axis=1, keepdims=True)


def received(ref, parity):
    return ref[pl.ds(parity, ref.shape[0] // 2, stride=2), :]


def write_scalars(ref, values):
    lane = lane_row()
    line = jnp.zeros((1, LANES), jnp.float32)
    for index, value in enumerate(values):
        line = jnp.where(lane == index, value, line)
    ref[...] = jnp.broadcast_to(line, ref.shape)


def middle_kernel(grid, position, arrived0, arrived, names_ref, lifted0_ref, *rest):
    parts = rest[:8]
    resid0, direction0, image0, inverse, w_layer, w_row, w_east, w_west = rest[8:16]
    resid, lifted, direction, image, lifted_image, scalars, lifted_blocks, message = rest[16:24]
    scaled_image, scaled_lifted, rise_0, rise_1 = rest[24:]
    width = grid[2] * grid[3]
    layers = resid.shape[0] // 2
    sums = arrived0[...]
    names = unfold(sums, 1, width).astype(jnp.int32)
    here = names_ref[...].astype(jnp.int32)
    upper, lower = received(arrived, 0), received(arrived, 1)
    s_rp, s_rd, s_dq, s_eq, s_pq, s_ee = [lane_total(upper, 3 * width + k) for k in range(6)]
    r_q, r_e = [unfold(upper, k, width) for k in range(2)]
    diag, east, south = [unfold(lower, k, width) for k in range(3)]
    lifted0 = lifted0_ref[...]
    r_d = r_q - apply_blocks(diag, east, south, lifted0, grid)
    s_dd = s_dq - dot_blocks(lifted0, r_d)
    s_de = s_eq - dot_blocks(lifted0, r_e)
    alpha0 = s_rp / s_pq
    scaled_sum = s_rd - 2.0 * alpha0 * s_dq + alpha0 * alpha0 * s_eq
    coarse1 = unfold(sums, 0, width) - alpha0 * r_q
    solved = coarse_solve(coarse1, names, position[0], parts)
    lifted1 = lookup(solved, names)
    prolong(rise_0, lookup(solved, here))
    inner1 = scaled_sum + dot_blocks(coarse1, lifted1)
    beta0 = inner1 / s_rp
    r_x = r_d - alpha0 * r_e + beta0 * r_q
    energy = (
        s_dd
        - 2.0 * alpha0 * s_de
        + alpha0 * alpha0 * s_ee
        + 2.0 * beta0 * (s_dq - alpha0 * s_eq)
        + beta0 * beta0 * s_pq
    )
    block_image = apply_blocks(diag, east, south, lifted1, grid)
    alpha1 = inner1 / (energy + dot_blocks(lifted1, 2.0 * r_x + block_image))
    coarse2 = coarse1 - alpha1 * (r_x + block_image)
    solved = coarse_solve(coarse2, names, position[0], parts)
    lifted_blocks[...] = lookup(solved, names)
    prolong(rise_1, lookup(solved, here))
    write_scalars(scalars, [alpha0, alpha1, inner1])

    operator = Operator(w_layer, w_row, w_east, w_west)
    for at in range(2 * layers):
        after = band(resid0, at) - alpha0 * band(image0, at)
        put(resid, at, after)
        put(direction, at, band(inverse, at) * after + rise_0[at // layers] + beta0 * band(direction0, at))
    zero = jnp.zeros((8, LANES), jnp.float32)
    folds = [jnp.zeros((grid[2], 8, LANES), jnp.float32) for _ in range(5)]
    s_rz = s_rd = s_zu = s_zq = s_pq = s_du = s_dq = s_us = s_uw = s_qw = zero
    s_ss = s_sw = s_ww = zero
    for layer, planes in operator.wide(direction):
        for k, plane in enumerate(planes):
            at = k * layers + layer
            put(image, at, plane)
            after = band(resid, at) - alpha1 * plane
            put(resid, at, after)
            put(lifted, at, band(inverse, at) * after + rise_1[k])
            put(scaled_image, at, band(inverse, at) * plane)
        q, r, p, v = near(planes[0]), own(resid, layer), own(direction, layer), own(inverse, layer)
        d, z, w = v * r, own(lifted, layer), v * q
        s_rz += tally(r * z)
        s_rd += tally(r * d)
        s_zq += tally(z * q)
        s_pq += tally(p * q)
        s_dq += tally(d * q)
        s_qw += tally(q * w)
        folds[1] += fold_rows(q)
        folds[4] += fold_rows(r)
    for layer, planes in operator.wide(lifted):
        for k, plane in enumerate(planes):
            at = k * layers + layer
            put(lifted_image, at, plane)
            put(scaled_lifted, at, band(inverse, at) * plane)
        u = near(planes[0])
        v = own(inverse, layer) * u
        s_zu += tally(u * own(lifted, layer))
        s_du += tally(v * own(resid, layer))
        s_us += tally(u * v)
        s_uw += tally(u * own(scaled_image, layer))
        folds[0] += fold_rows(u)
    for layer, image_s in operator.near(scaled_lifted):
        s_ss += tally(image_s * own(scaled_lifted, layer))
        s_sw += tally(image_s * own(scaled_image, layer))
        folds[2] += fold_rows(image_s)
    for layer, image_w in operator.near(scaled_image):
        s_ww += tally(image_w * own(scaled_image, layer))
        folds[3] += fold_rows(image_w)
    lines = [fold.sum(axis=1) for fold in folds]
    upper = pack_blocks(lines[:4])
    lower = pack_blocks(lines[4:]) + pack_scalars(
        [s_rz, s_rd, s_zu, s_zq, s_pq, s_du, s_dq, s_us, s_uw, s_qw, s_ss, s_sw, s_ww],
        width,
    )
    write_message(message, upper, lower)


def last_kernel(grid, position, arrived0, before, arrived, names_ref, scalars, lifted2_ref, *rest):
    parts = rest[:8]
    resid, lifted, direction1, image1, lifted_image, direction0, inverse, w_layer, w_row, w_east, w_west = rest[8:19]
    outs = rest[19:21]
    direction, rise_3, answer, out_resid, sems = rest[21:]
    width = grid[2] * grid[3]
    layers = resid.shape[0] // 2
    names = unfold(arrived0[...], 1, width).astype(jnp.int32)
    here = names_ref[...].astype(jnp.int32)
    blocks = received(before, 1)
    diag, east, south = [unfold(blocks, k, width) for k in range(3)]
    upper, lower = received(arrived, 0), received(arrived, 1)
    r_u, r_q, r_s, r_w = [unfold(upper, k, width) for k in range(4)]
    r_r = unfold(lower, 0, width)
    s_rz, s_rd, s_zu, s_zq, s_pq, s_du, s_dq, s_us, s_uw, s_qw, s_ss, s_sw, s_ww = [
        lane_total(lower, width + k) for k in range(13)
    ]
    lifted2 = lifted2_ref[...]
    r_d = r_u - apply_blocks(diag, east, south, lifted2, grid)
    s_dd = s_du - dot_blocks(lifted2, r_d)
    s_ds = s_us - dot_blocks(lifted2, r_s)
    s_dw = s_uw - dot_blocks(lifted2, r_w)
    alpha0, alpha1, inner1 = [scalars[0:1, k : k + 1] for k in range(3)]
    inner2 = s_rz
    beta1 = inner2 / inner1
    alpha2 = inner2 / (s_zu + 2.0 * beta1 * s_zq + beta1 * beta1 * s_pq)
    coarse3 = r_r - alpha2 * (r_u + beta1 * r_q)
    solved = coarse_solve(coarse3, names, position[0], parts)
    lifted3 = lookup(solved, names)
    prolong(rise_3, lookup(solved, here))
    scaled_sum = (
        s_rd
        - 2.0 * alpha2 * (s_du + beta1 * s_dq)
        + alpha2 * alpha2 * (s_us + 2.0 * beta1 * s_uw + beta1 * beta1 * s_qw)
    )
    inner3 = scaled_sum + dot_blocks(coarse3, lifted3)
    beta2 = inner3 / inner2
    rise = lifted3 + beta2 * lifted2
    k_d, k_s, k_w, k_p = 1.0 + beta2, -alpha2, -alpha2 * beta1, beta2 * beta1
    energy = (
        k_d * k_d * s_dd
        + k_s * k_s * s_ss
        + k_w * k_w * s_ww
        + k_p * k_p * s_pq
        + 2.0 * (k_d * (k_s * s_ds + k_w * s_dw + k_p * s_dq) + k_s * (k_w * s_sw + k_p * s_uw) + k_w * k_p * s_qw)
    )
    r_x = k_d * r_d + k_s * r_s + k_w * r_w + k_p * r_q
    block_image = apply_blocks(diag, east, south, rise, grid)
    alpha3 = inner3 / (energy + dot_blocks(rise, 2.0 * r_x + block_image))

    for at in range(2 * layers):
        direction2 = band(lifted, at) + beta1 * band(direction1, at)
        after = band(resid, at) - alpha2 * (band(lifted_image, at) + beta1 * band(image1, at))
        step = band(inverse, at) * after + rise_3[at // layers] + beta2 * direction2
        put(direction, at, step)
        if at < layers:
            out_resid[at] = near(after)
            answer[at] = (
                alpha0 * own(direction0, at)
                + alpha1 * own(direction1, at)
                + alpha2 * near(direction2)
                + alpha3 * near(step)
            )
    copies = [pltpu.make_async_copy(answer, outs[0], sems.at[layers])]
    copies[0].start()
    for layer, plane in Operator(w_layer, w_row, w_east, w_west).near(direction):
        out_resid[layer] = out_resid[layer] - alpha3 * plane
        copies.append(pltpu.make_async_copy(out_resid.at[layer], outs[1].at[layer], sems.at[layer]))
        copies[-1].start()
    for copy in copies:
        copy.wait()


def call(kernel, outs, scratch, name, smem, *operands, spaces=None, out_space=pltpu.VMEM):
    whole = pl.BlockSpec(memory_space=pltpu.VMEM)
    scalar = pl.BlockSpec(memory_space=pltpu.SMEM)
    specs = [scalar] * smem + [whole] * (len(operands) - smem)
    operands = list(operands)
    for index in spaces or ():
        specs[index] = pl.BlockSpec(memory_space=pltpu.HBM)
        operands[index] = pltpu.with_memory_space_constraint(operands[index], pltpu.HBM)
    return pl.pallas_call(
        kernel,
        out_shape=[jax.ShapeDtypeStruct(shape, jnp.float32) for shape in outs],
        in_specs=specs,
        out_specs=[pl.BlockSpec(memory_space=out_space)] * len(outs),
        scratch_shapes=[pltpu.VMEM(s, jnp.float32) if isinstance(s, tuple) else s for s in scratch],
        compiler_params=pltpu.CompilerParams(vmem_limit_bytes=20 * 1024 * 1024),
        name=name,
    )(*operands)


def exchange(message):
    return lax.all_to_all(message, BOTH, 0, 0, tiled=True)


def pair(values, axis, mask):
    return lax.ppermute(values, axis, [(i, i ^ mask) for i in range(lax.axis_size(axis))])


def pair_far(values, axis):
    count = lax.axis_size(axis)
    return lax.ppermute(values, axis, [(i, i + 1 if i % 2 else i - 1) for i in range(1, count - 1)])


def local_steps(loading, viscosity, aggregate, coarse_inverse):
    layers, cells_x, cells_y = loading.shape
    blocks_x, blocks_y = aggregate.shape
    count_x, count_y = lax.axis_size("rows"), lax.axis_size("cols")
    devices = count_x * count_y
    grid = (count_x, count_y, blocks_x, blocks_y)
    position = jnp.stack([lax.axis_index(axis).astype(jnp.int32) for axis in BOTH])
    tall = cells_x + 2 * HALO
    edge = (2 * layers + 1, HALO, LANES)
    shard = coarse_inverse.T.reshape(PART // 8, 8, COARSE // LANES, LANES)
    shard = shard.transpose(0, 2, 1, 3).reshape(TILES, 8, LANES)
    parts = [pair(shard, "rows", mask) for mask in (2, 4, 6)]

    ids, near_out, far_rows = call(
        rows_kernel,
        [(8, LANES), (edge[0] + TILES, 8, LANES), (LONG, 8, LANES)],
        [pltpu.SMEM(aggregate.shape, jnp.int32), pltpu.SemaphoreType.DMA((9,))],
        "rows",
        1,
        position,
        aggregate,
        loading,
        viscosity,
        shard,
        spaces=(1, 2, 3, 4),
    )
    own = (position, loading, viscosity, ids)
    near_rows, far_rows = pair(near_out, "rows", 1), pair_far(far_rows, "rows")
    near_cols, far_cols, message0 = call(
        edge_kernel, [(8 * LONG, LANES)] * 2 + [(devices, LANES)], [], "edges", 1, *own, near_rows, far_rows
    )
    near_cols, far_cols = pair(near_cols, "cols", 1), pair_far(far_cols, "cols")
    parts = [part for both in ((part, pair(part, "rows", 1)) for part in parts) for part in both]
    parts = [near_out, near_rows] + parts
    arrived0 = exchange(message0)
    parts, arrived0 = lax.optimization_barrier((parts, arrived0))
    field = (2 * layers, tall + 2 * PAD, LANES)
    taller = (2 * (layers + 1), tall + 2 * PAD, LANES)
    plane = (2, tall, LANES)
    message = (2 * devices, LANES)
    line = (8, LANES)
    resid, direction0, image0, inverse, w_layer, w_row, w_east, w_west, names, lifted_blocks, message1 = call(
        start_kernel,
        [field] * 4 + [taller, field, field, field, line, line, message],
        [field, plane, field, plane],
        "start",
        1,
        *own,
        near_rows,
        far_rows,
        near_cols,
        far_cols,
        arrived0,
        *parts,
    )
    weights = (inverse, w_layer, w_row, w_east, w_west)
    arrived1 = exchange(message1)
    resid, lifted, direction1, image1, lifted_image, scalars, lifted_blocks, message2 = call(
        lambda *refs: middle_kernel(grid, *refs),
        [field] * 5 + [line, line, message],
        [field] * 2 + [plane] * 2,
        "middle",
        1,
        position,
        arrived0,
        arrived1,
        names,
        lifted_blocks,
        *parts,
        resid,
        direction0,
        image0,
        *weights,
    )
    arrived2 = exchange(message2)
    return call(
        lambda *refs: last_kernel(grid, *refs),
        [loading.shape] * 2,
        [field, plane, loading.shape, loading.shape, pltpu.SemaphoreType.DMA((layers + 1,))],
        "last",
        1,
        position,
        arrived0,
        arrived1,
        arrived2,
        names,
        scalars,
        lifted_blocks,
        *parts,
        resid,
        lifted,
        direction1,
        image1,
        lifted_image,
        direction0,
        *weights,
        out_space=pltpu.HBM,
    )


def from_sides(block, axis, dim, width):
    count = lax.axis_size(axis)
    forward = [(i, i + 1) for i in range(count - 1)]
    backward = [(target, source) for source, target in forward]
    size = block.shape[dim]
    low = lax.ppermute(lax.slice_in_dim(block, size - width, size, axis=dim), axis, forward)
    high = lax.ppermute(lax.slice_in_dim(block, 0, width, axis=dim), axis, backward)
    return low, high


def widened(block, width_x, width_y):
    low, high = from_sides(block, "rows", block.ndim - 2, width_x)
    block = jnp.concatenate([low, block, high], axis=-2)
    turned = jnp.swapaxes(block, -1, -2)
    low, high = from_sides(turned, "cols", turned.ndim - 2, width_y)
    low, high = jnp.swapaxes(low, -1, -2), jnp.swapaxes(high, -1, -2)
    return jnp.concatenate([low, block, high], axis=-1)


def all_sum(values):
    count = lax.axis_size("rows") * lax.axis_size("cols")
    if count > 64:
        return lax.psum(lax.psum(values, "cols"), "rows")
    spread = jnp.broadcast_to(values[None], (count,) + values.shape)
    return lax.all_to_all(spread, BOTH, 0, 0).sum(axis=0)


def shifted(field, axis, step):
    return jnp.roll(field, step, axis=axis)


def local_general(loading, viscosity, aggregate, coarse_inverse):
    layers, cells_x, cells_y = loading.shape
    blocks_x, blocks_y = aggregate.shape
    ids = jnp.arange(COARSE, dtype=jnp.int32)
    whole_matrix = lax.all_gather(coarse_inverse, "rows", axis=1, tiled=True)
    fields = widened(jnp.stack([loading, viscosity]), HALO, HALO)
    wide_aggregate = widened(aggregate + 1, 1, 1) - 1
    table = (aggregate.reshape(-1)[:, None] == ids[None, :]).astype(jnp.float32)
    wide_table = (wide_aggregate.reshape(-1)[:, None] == ids[None, :]).astype(jnp.float32)

    residual, visc = fields[0], fields[1]
    inside = visc > 0.0
    pads = ((1, 1), (0, 0), (0, 0))
    padded = jnp.pad(visc, pads)
    weights = [
        0.5 * (visc + padded[:-2]),
        0.5 * (visc + padded[2:]),
        0.5 * (visc + shifted(visc, 1, 1)),
        0.5 * (visc + shifted(visc, 1, -1)),
        0.5 * (visc + shifted(visc, 2, 1)),
        0.5 * (visc + shifted(visc, 2, -1)),
    ]
    diagonal = MASS_TERM + sum(weights)
    inverse = jnp.where(inside, 1.0 / diagonal, 0.0)

    def operate(field):
        layered = jnp.pad(field, pads)
        sides = [
            layered[:-2],
            layered[2:],
            shifted(field, 1, 1),
            shifted(field, 1, -1),
            shifted(field, 2, 1),
            shifted(field, 2, -1),
        ]
        total = MASS_TERM * field
        for weight, side in zip(weights, sides):
            total = total + weight * (field - side)
        return total

    def inner_part(field):
        return field[:, HALO:-HALO, HALO:-HALO]

    def restrict(field):
        blocks = field.reshape(layers, blocks_x, BLOCK, blocks_y, BLOCK).sum(axis=(0, 2, 4))
        return jnp.dot(blocks.reshape(-1), table, precision=PRECISE).reshape(4, COARSE // 4)

    def prolong(values):
        per_block = jnp.dot(wide_table, values.reshape(-1), precision=PRECISE)
        per_block = per_block.reshape(blocks_x + 2, blocks_y + 2)
        spread = jnp.repeat(jnp.repeat(per_block, BLOCK, axis=0), BLOCK, axis=1)
        cut = BLOCK - HALO
        return spread[cut:-cut, cut:-cut][None]

    def coarse_apply(coarse):
        return jnp.dot(whole_matrix, coarse.reshape(-1), precision=PRECISE).reshape(coarse.shape)

    def scalars(*values):
        return jnp.stack([jnp.broadcast_to(v, (COARSE // 4,)) for v in values])

    coarse = all_sum(restrict(loading))
    lifted = coarse_apply(coarse)
    direction = inverse * residual + prolong(lifted)
    answer = jnp.zeros_like(loading)
    scaled_sum = inner_now = None
    for iteration in range(ITERS):
        image = operate(direction)
        near_image, near_scaled = inner_part(image), inner_part(inverse * image)
        near_direction, near_residual = inner_part(direction), inner_part(residual)
        packed = jnp.concatenate(
            [
                restrict(near_image),
                scalars(
                    jnp.sum(near_direction * near_image),
                    jnp.sum(near_residual * near_scaled),
                    jnp.sum(near_image * near_scaled),
                    jnp.sum(near_residual * inner_part(inverse) * near_residual),
                ),
            ]
        )
        packed = all_sum(packed)
        curvature, cross, square = packed[4, 0], packed[5, 0], packed[6, 0]
        if scaled_sum is None:
            scaled_sum = packed[7, 0]
            inner_now = scaled_sum + jnp.sum(coarse * lifted)
        alpha = inner_now / curvature
        answer = answer + alpha * near_direction
        residual = residual - alpha * image
        if iteration + 1 < ITERS:
            coarse = coarse - alpha * packed[:4]
            scaled_sum = scaled_sum - 2.0 * alpha * cross + alpha * alpha * square
            lifted = coarse_apply(coarse)
            inner_next = scaled_sum + jnp.sum(coarse * lifted)
            direction = inverse * residual + prolong(lifted) + inner_next / inner_now * direction
            inner_now = inner_next
    return answer, inner_part(residual)


def solution(mesh):
    in_specs = (
        P(None, "rows", "cols"),
        P(None, "rows", "cols"),
        P("rows", "cols"),
        P(None, "rows"),
    )
    out_specs = (P(None, "rows", "cols"), P(None, "rows", "cols"))
    body = local_steps if (mesh.shape["rows"], mesh.shape["cols"]) == (8, 4) else local_general
    return jax.shard_map(body, mesh=mesh, in_specs=in_specs, out_specs=out_specs, check_vma=False)
```
